32 devices in a mesh: section: 4 (over x, core), gx: 2 (over y), gy: 4 (over z).
Axes of the slice: x: 2, y: 2, z: 4, core: 2. Of those that a mesh axis runs over, the one named last changes fastest.
Arguments:
- voltage: float32 [8, 64, 1024], P(None, ('section', 'gx'), 'gy'), may hold values from -1.8 to 1.8
- capacity: float32 [8, 64, 1024], P(None, ('section', 'gx'), 'gy'), may hold values from 0.05 to 0.5
- node_class: int32 [8, 64, 1024], P(None, ('section', 'gx'), 'gy'), may hold values from 0 to 7
- via_sites: int32 [7, 64, 1024], P(None, ('section', 'gx'), 'gy'), may hold values 0 or 1
- ball_sites: int32 [64, 1024], P(('section', 'gx'), 'gy'), may hold values 0 or 1
- load_type: int32 [64, 1024], P(('section', 'gx'), 'gy'), may hold values from 0 to 15
- load_table: float32 [16, 5], replicated, may hold values from -4 to 4
Outputs:
- sections: float32 [5, 8, 64, 1024], P(None, None, ('section', 'gx'), 'gy')
- next_voltage: float32 [8, 64, 1024], P(None, ('section', 'gx'), 'gy')
The draws below stay inside these ranges and needn't reach their ends.
Inputs may be any that keep to these rules, and one draw needn't show every extreme that they name: `node_class`: index into the table of 8 conductances. `load_type`: row of load_table.
All inputs are finite; a program needn't handle non-finite values. No bound on the sum of `via_sites` or of `ball_sites` on one device may be relied on, other than what follows from the above.
Results may differ from the reference program's by a relative error of at most 0.0003.
Values sent between devices are 32-bit elements; how exact they have to be, the bound alone decides.
A program may use at most 128 MiB of HBM per device.

```python
import math
import jax
import jax.numpy as jnp
import numpy as np
from jax import lax

LAYERS = 8
SECTIONS = 5
LEVELS = 3
SWEEPS = 2
COARSE_SWEEPS = 4
CYCLES = 2
CLASSES = 8
LOADS = 16
NX = 64
NY = 1024


def place_ends(drawn, key, low, high):
    longest = drawn.shape.index(max(drawn.shape))
    spots = []
    for shift in (0, 1):
        where = [jax.random.randint(jax.random.fold_in(key, axis), (), 0, length) for axis, length in enumerate(drawn.shape)]
        where[longest] = (where[longest] + shift) % drawn.shape[longest]
        spots.append(tuple(where))
    return drawn.at[spots[0]].set(low).at[spots[1]].set(high)


def block_scale(own_key, dims, cuts, low, top_value):
    def one(position, parts):
        heights = jax.random.uniform(jax.random.fold_in(jax.random.fold_in(own_key, 6), position), (parts,), jnp.float32, low / len(cuts), top_value / len(cuts))
        return jnp.repeat(jnp.exp(heights), dims[position] // parts).reshape((-1,) + (1,) * (len(dims) - position - 1))

    gain = one(*cuts[0])
    for cut in cuts[1:]:
        gain = gain * one(*cut)
    return gain


def cumulative_ranks(count, slope):
    weights = [(1 << 20) // math.isqrt(grade ** slope) + 1 for grade in range(1, count + 1)]
    deviation = 1 + sum(weights) // (1 << 30)
    return np.cumsum(np.array([max(1, weight // deviation) for weight in weights]))


def ranked(stream_key, shape, amount, skew):
    grid = cumulative_ranks(amount, skew)
    ticket = jax.random.randint(jax.random.fold_in(stream_key, 1), shape, 0, int(grid[amount - 1]))
    grade = jnp.searchsorted(jnp.asarray(grid, jnp.int32), ticket, side="right")
    return jax.random.permutation(jax.random.fold_in(stream_key, 2), amount)[grade].astype(jnp.int32)


def normal_values(stream_key, shape, width, limit, split=(), dtype=jnp.bfloat16):
    values = jax.random.normal(stream_key, shape, jnp.float32) * width
    if len(split) > 0:
        values = block_scale(stream_key, shape, split, -0.22, 0.18) * values
    return jnp.clip(values, min=-limit, max=limit).astype(dtype)


def setup_inputs(seed: int = 0) -> dict:
    key_of = jax.random.split(jax.random.key(seed), 8)
    return {
        "voltage": normal_values(key_of[0], (LAYERS, NX, NY), 0.3, 1.8, ((1, 8), (2, 4)), jnp.float32),
        "capacity": jnp.clip(jnp.exp(math.log(0.5) - 2.3025851 * jax.random.uniform(key_of[1], (LAYERS, NX, NY), jnp.float32) ** block_scale(key_of[1], (LAYERS, NX, NY), ((1, 8), (2, 4)), -0.2, 0.2)), 0.05, 0.5),
        "node_class": place_ends(jax.random.randint(key_of[2], (LAYERS, NX, NY), 0, CLASSES), jax.random.fold_in(key_of[2], 1), 0, CLASSES - 1).astype(jnp.int32),
        "via_sites": place_ends((jax.random.randint(key_of[3], (LAYERS - 1, NX, NY), 0, 3) < 1).astype(jnp.int32), jax.random.fold_in(key_of[3], 1), 0, 1),
        "ball_sites": place_ends((jax.random.randint(key_of[4], (NX, NY), 0, 16) < 1).astype(jnp.int32), jax.random.fold_in(key_of[4], 1), 0, 1),
        "load_type": place_ends(ranked(key_of[5], (NX, NY), LOADS, 2), jax.random.fold_in(key_of[5], 3), 0, LOADS - 1).astype(jnp.int32),
        "load_table": normal_values(key_of[6], (LOADS, SECTIONS), 1.0, 4.0, (), jnp.float32),
    }


node_table = (0.35, 0.55, 0.8, 1.1, 1.5, 2.0, 2.7, 3.6)
via_conductance = 2.5
ball_conductance = 4.0
damping = 0.8
slab_partner = (0, 2, 1, 4, 3)


def pair_times(first, second):
    return (first[0] * second[0] - first[1] * second[1], first[0] * second[1] + first[1] * second[0])


def pair_over(first, second):
    divisor = second[0] * second[0] + second[1] * second[1]
    return ((first[0] * second[0] + first[1] * second[1]) / divisor,
            (first[1] * second[0] - first[0] * second[1]) / divisor)


def pair_minus(first, second):
    return (first[0] - second[0], first[1] - second[1])


def poly_value(coeffs, point):
    total = (0.0, 0.0)
    for c in reversed(coeffs):
        total = pair_times(total, point)
        total = (total[0] + c, total[1])
    return total


def poly_product(first, second):
    result = [0.0] * (len(first) + len(second) - 1)
    for i in range(len(first)):
        for j in range(len(second)):
            result[i + j] = result[i + j] + first[i] * second[j]
    return result


def poly_roots(coeffs):
    leading = coeffs[-1]
    scaled = [c / leading for c in coeffs]
    degree = len(coeffs) - 1
    guesses = []
    current = (1.0, 0.0)
    for k in range(degree):
        guesses.append(current)
        current = pair_times(current, (0.4, 0.9))
    for repeat_index in range(800):
        for k in range(degree):
            divisor = (1.0, 0.0)
            for j in range(degree):
                if j != k:
                    divisor = pair_times(divisor, pair_minus(guesses[k], guesses[j]))
            guesses[k] = pair_minus(guesses[k], pair_over(poly_value(scaled, guesses[k]), divisor))
    return guesses


def matrix_product(first, second):
    return [[sum(first[i][k] * second[k][j] for k in range(len(second))) for j in range(len(second[0]))]
            for i in range(len(first))]


def matrix_inverse(matrix):
    order = len(matrix)
    work = [list(matrix[i]) + [1.0 if i == j else 0.0 for j in range(order)] for i in range(order)]
    for column in range(order):
        pivot = column
        for i in range(column + 1, order):
            if abs(work[i][column]) > abs(work[pivot][column]):
                pivot = i
        work[column], work[pivot] = work[pivot], work[column]
        factor = work[column][column]
        work[column] = [entry / factor for entry in work[column]]
        for i in range(order):
            if i != column:
                scale_row = work[i][column]
                work[i] = [work[i][j] - scale_row * work[column][j] for j in range(2 * order)]
    return [row[order:] for row in work]


def eigen_vector(matrix, value):
    order = len(matrix)
    size_inner = order - 1
    system = []
    for i in range(size_inner):
        row = []
        for j in range(order):
            entry = (matrix[i][j], 0.0)
            if i == j:
                entry = pair_minus(entry, value)
            row.append(entry)
        row[order - 1] = (-row[order - 1][0], -row[order - 1][1])
        system.append(row)
    for column in range(size_inner):
        pivot = column
        for i in range(column + 1, size_inner):
            left_size = system[i][column][0] ** 2 + system[i][column][1] ** 2
            right_size = system[pivot][column][0] ** 2 + system[pivot][column][1] ** 2
            if left_size > right_size:
                pivot = i
        system[column], system[pivot] = system[pivot], system[column]
        for i in range(size_inner):
            if i != column:
                factor = pair_over(system[i][column], system[column][column])
                system[i] = [pair_minus(system[i][j], pair_times(factor, system[column][j])) for j in range(order)]
    vector = [pair_over(system[i][order - 1], system[i][i]) for i in range(size_inner)]
    vector.append((1.0, 0.0))
    return vector


def radau_tables():
    section_count = 5
    generator = [1.0]
    for k in range(section_count - 1):
        generator = poly_product(generator, [0.0, 1.0])
    for k in range(section_count):
        generator = poly_product(generator, [-1.0, 1.0])
    for k in range(section_count - 1):
        generator = [j * generator[j] for j in range(1, len(generator))]
    abscissae = sorted(root[0] for root in poly_roots(generator))
    vander = [[abscissae[i] ** j for j in range(section_count)] for i in range(section_count)]
    integrals = [[abscissae[i] ** (j + 1) / (j + 1) for j in range(section_count)] for i in range(section_count)]
    butcher = matrix_product(integrals, matrix_inverse(vander))
    inverse = matrix_inverse(butcher)
    coeffs = [0.0] * (section_count + 1)
    coeffs[section_count] = 1.0
    current = [[0.0] * section_count for _ in range(section_count)]
    for k in range(1, section_count + 1):
        current = matrix_product(inverse, current)
        for i in range(section_count):
            current[i][i] = current[i][i] + coeffs[section_count - k + 1]
        applied = matrix_product(inverse, current)
        coeffs[section_count - k] = -sum(applied[i][i] for i in range(section_count)) / k
    eigen_values = poly_roots(coeffs)
    real_pick = 0
    for k in range(section_count):
        if abs(eigen_values[k][1]) < abs(eigen_values[real_pick][1]):
            real_pick = k
    upper_half = [k for k in range(section_count) if eigen_values[k][1] > 1e-9]
    upper_half = sorted(upper_half, key=lambda k: -eigen_values[k][0])
    columns = [[entry[0] for entry in eigen_vector(inverse, (eigen_values[real_pick][0], 0.0))]]
    for k in upper_half:
        vector = eigen_vector(inverse, eigen_values[k])
        columns.append([entry[0] for entry in vector])
        columns.append([entry[1] for entry in vector])
    transform = [[columns[j][i] for j in range(section_count)] for i in range(section_count)]
    inverse_transform = matrix_inverse(transform)
    blocks = matrix_product(matrix_product(inverse_transform, inverse), transform)
    diagonal = [blocks[k][k] for k in range(section_count)]
    coupling = [blocks[k][slab_partner[k]] if slab_partner[k] != k else 0.0 for k in range(section_count)]
    return transform, inverse_transform, diagonal, coupling


def lookup(classes, values_table):
    result = jnp.zeros(classes.shape, jnp.float32)
    for k in range(len(values_table)):
        result = result + jnp.where(classes == k, jnp.float32(values_table[k]), jnp.float32(0.0))
    return result


def series(near_side, far_side):
    return 2.0 * near_side * far_side / (near_side + far_side)


def branch_set(conduct, padded, via_sites, ball_sites, capacity):
    lower_x = series(padded[:, :-2, 1:-1], conduct)
    upper_x = series(conduct, padded[:, 2:, 1:-1])
    lower_y = series(padded[:, 1:-1, :-2], conduct)
    upper_y = series(conduct, padded[:, 1:-1, 2:])
    vertical = jnp.where(via_sites == 1, jnp.float32(via_conductance), jnp.float32(0.0))
    ground = jnp.where(ball_sites == 1, jnp.float32(ball_conductance), jnp.float32(0.0))
    return (capacity, lower_x, upper_x, lower_y, upper_y, vertical, ground)


def layer_terms(vertical, ground, layers):
    zero_plane = jnp.zeros((1,) + vertical.shape[1:], jnp.float32)
    via_above = jnp.concatenate([vertical, zero_plane], axis=0)
    via_below = jnp.concatenate([zero_plane, vertical], axis=0)
    grounded = jnp.concatenate([ground[None], jnp.zeros((layers - 1,) + ground.shape, jnp.float32)], axis=0)
    return via_above, via_below, grounded


def network(voltage, padded_voltage, branches):
    capacity, lower_x, upper_x, lower_y, upper_y, vertical, ground = branches
    via_above, via_below, grounded = layer_terms(vertical, ground, voltage.shape[0])
    branch_total = lower_x + upper_x + lower_y + upper_y + via_above + via_below + grounded
    zero_plane = jnp.zeros((1,) + voltage.shape[1:], jnp.float32)
    volt_above = jnp.concatenate([voltage[1:], zero_plane], axis=0)
    volt_below = jnp.concatenate([zero_plane, voltage[:-1]], axis=0)
    inflow = (upper_x * padded_voltage[:, 2:, 1:-1] + lower_x * padded_voltage[:, :-2, 1:-1]
              + upper_y * padded_voltage[:, 1:-1, 2:] + lower_y * padded_voltage[:, 1:-1, :-2]
              + via_above * volt_above + via_below * volt_below)
    return branch_total * voltage - inflow


def section_sources(load_type, load_table):
    surface = jnp.zeros((SECTIONS,) + load_type.shape, jnp.float32)
    for t in range(LOADS):
        surface = surface + jnp.where((load_type == t)[None], load_table[t][:, None, None], jnp.float32(0.0))
    return surface


def pair_rows(array):
    extent = array.shape
    return array.reshape(extent[:-2] + (extent[-2] // 2, 2, extent[-1])).sum(axis=-2)


def pair_cols(array):
    extent = array.shape
    return array.reshape(extent[:-1] + (extent[-1] // 2, 2)).sum(axis=-1)


def take_rows(array, offset):
    extent = array.shape
    return array.reshape(extent[:-2] + (extent[-2] // 2, 2, extent[-1]))[..., offset, :]


def take_cols(array, offset):
    extent = array.shape
    return array.reshape(extent[:-1] + (extent[-1] // 2, 2))[..., offset]


def block_sum(array):
    return pair_cols(pair_rows(array))


def coarsen(branches):
    capacity, lower_x, upper_x, lower_y, upper_y, vertical, ground = branches
    return (block_sum(capacity), pair_cols(take_rows(lower_x, 0)), pair_cols(take_rows(upper_x, 1)),
            pair_rows(take_cols(lower_y, 0)), pair_rows(take_cols(upper_y, 1)),
            block_sum(vertical), block_sum(ground))


def level_operator(branches, shifts, couple, partner):
    capacity, lower_x, upper_x, lower_y, upper_y, vertical, ground = branches
    via_above, via_below, grounded = layer_terms(vertical, ground, capacity.shape[0])
    branch_total = lower_x + upper_x + lower_y + upper_y + via_above + via_below + grounded
    diagonal = shifts[:, None, None, None] * capacity + branch_total
    coupled = couple[:, None, None, None] * capacity
    diagonal_mate = jnp.stack([diagonal[p] for p in partner])
    coupled_mate = jnp.stack([coupled[p] for p in partner])
    determinant = diagonal * diagonal_mate - coupled * coupled_mate
    self_weight = diagonal_mate / determinant
    mate_weight = -coupled / determinant
    return (lower_x, upper_x, lower_y, upper_y, via_above, via_below, diagonal, coupled, self_weight, mate_weight, partner)


def operate(iterate, operator, neighbours):
    lower_x, upper_x, lower_y, upper_y, via_above, via_below, diagonal, coupled, self_weight, mate_weight, partner = operator
    upper_rows, lower_rows, right_cols, left_cols = neighbours
    zero_plane = jnp.zeros_like(iterate[:, :1])
    from_above = jnp.concatenate([iterate[:, 1:], zero_plane], axis=1)
    from_below = jnp.concatenate([zero_plane, iterate[:, :-1]], axis=1)
    inflow = (upper_x * upper_rows + lower_x * lower_rows + upper_y * right_cols + lower_y * left_cols
              + via_above * from_above + via_below * from_below)
    partner_field = jnp.stack([iterate[p] for p in partner])
    return diagonal * iterate - inflow + coupled * partner_field


def relax(iterate, source, operator, neighbour_fn):
    partner = operator[-1]
    if iterate is None:
        residual = source
    else:
        residual = source - operate(iterate, operator, neighbour_fn(iterate))
    mate_values = jnp.stack([residual[p] for p in partner])
    update = operator[8] * residual + operator[9] * mate_values
    if iterate is None:
        return damping * update
    return iterate + damping * update


def vcycle(operators, level_index, iterate, source, neighbour_fn):
    operator = operators[level_index]
    if level_index == len(operators) - 1:
        for _ in range(COARSE_SWEEPS):
            iterate = relax(iterate, source, operator, neighbour_fn)
        return iterate
    for _ in range(SWEEPS):
        iterate = relax(iterate, source, operator, neighbour_fn)
    residual = source - operate(iterate, operator, neighbour_fn(iterate))
    coarse = vcycle(operators, level_index + 1, None, block_sum(residual), neighbour_fn)
    iterate = iterate + jnp.repeat(jnp.repeat(coarse, 2, axis=2), 2, axis=3)
    for _ in range(SWEEPS):
        iterate = relax(iterate, source, operator, neighbour_fn)
    return iterate


def solve(source, branches, shifts, couple, partner, neighbour_fn):
    operators = []
    for level_index in range(LEVELS):
        if level_index > 0:
            branches = coarsen(branches)
        operators.append(level_operator(branches, shifts, couple, partner))
    iterate = vcycle(operators, 0, None, source, neighbour_fn)
    for _ in range(CYCLES - 1):
        iterate = vcycle(operators, 0, iterate, source, neighbour_fn)
    return iterate


def padded_faces(iterate):
    padded = jnp.pad(iterate, ((0, 0), (0, 0), (1, 1), (1, 1)))
    return padded[:, :, 2:, 1:-1], padded[:, :, :-2, 1:-1], padded[:, :, 1:-1, 2:], padded[:, :, 1:-1, :-2]


def reference(voltage, capacity, node_class, via_sites, ball_sites, load_type, load_table):
    transform, inverse_transform, diagonal_np, coupling_np = radau_tables()
    conduct = lookup(node_class, node_table)
    padded = jnp.pad(conduct, ((0, 0), (1, 1), (1, 1)))
    padded_voltage = jnp.pad(voltage, ((0, 0), (1, 1), (1, 1)))
    branches = branch_set(conduct, padded, via_sites, ball_sites, capacity)
    leakage = network(voltage, padded_voltage, branches)
    surface = section_sources(load_type, load_table)
    forcing = jnp.concatenate([jnp.broadcast_to(-leakage[:-1], (SECTIONS,) + leakage[:-1].shape),
                               (surface - leakage[-1])[:, None]], axis=1)
    transformed = jnp.einsum("jk,klrc->jlrc", jnp.asarray(inverse_transform, jnp.float32), forcing,
                             precision=lax.Precision.HIGHEST)
    shifts = jnp.asarray(diagonal_np, jnp.float32)
    couple = jnp.asarray(coupling_np, jnp.float32)
    solution = solve(transformed, branches, shifts, couple, slab_partner, padded_faces)
    sections = jnp.einsum("jk,klrc->jlrc", jnp.asarray(transform, jnp.float32), solution,
                        precision=lax.Precision.HIGHEST)
    return sections, voltage + sections[SECTIONS - 1]
```

```python
import functools

import jax
import jax.numpy as jnp
from jax import lax
from jax.experimental import pallas as pl
from jax.experimental.pallas import tpu as pltpu
from jax.sharding import PartitionSpec as P

SECTIONS = 5
LEVELS = 3
LOADS = 16
LANES = 128
BOTH_CYCLES = 56
STEP = 16
REAL = (0,)
PAIR = (1, 2)
GX, GY, GV, GY_LOW, GV_LOW, W_REAL, W_SAME, W_MATE, D_REAL, D_SAME, D_MATE, GROUND, CAP = range(13)
COEFFS = 13

node_table = (0.35, 0.55, 0.8, 1.1, 1.5, 2.0, 2.7, 3.6)
via_conductance = 2.5
ball_conductance = 4.0
damping = 0.8
slab_partner = (0, 2, 1, 4, 3)
row_axes = ("section", "gx")


def pair_times(first, second):
    return (
        first[0] * second[0] - first[1] * second[1],
        first[0] * second[1] + first[1] * second[0],
    )


def pair_over(first, second):
    divisor = second[0] * second[0] + second[1] * second[1]
    return (
        (first[0] * second[0] + first[1] * second[1]) / divisor,
        (first[1] * second[0] - first[0] * second[1]) / divisor,
    )


def pair_minus(first, second):
    return (first[0] - second[0], first[1] - second[1])


def poly_value(coeffs, point):
    total = (0.0, 0.0)
    for c in reversed(coeffs):
        total = pair_times(total, point)
        total = (total[0] + c, total[1])
    return total


def poly_product(first, second):
    result = [0.0] * (len(first) + len(second) - 1)
    for i in range(len(first)):
        for j in range(len(second)):
            result[i + j] = result[i + j] + first[i] * second[j]
    return result


def poly_roots(coeffs):
    leading = coeffs[-1]
    scaled = [c / leading for c in coeffs]
    degree = len(coeffs) - 1
    guesses = []
    current = (1.0, 0.0)
    for k in range(degree):
        guesses.append(current)
        current = pair_times(current, (0.4, 0.9))
    for repeat_index in range(800):
        for k in range(degree):
            divisor = (1.0, 0.0)
            for j in range(degree):
                if j != k:
                    divisor = pair_times(divisor, pair_minus(guesses[k], guesses[j]))
            guesses[k] = pair_minus(guesses[k], pair_over(poly_value(scaled, guesses[k]), divisor))
    return guesses


def matrix_product(first, second):
    return [
        [
            sum((first[i][k] * second[k][j] for k in range(len(second))))
            for j in range(len(second[0]))
        ]
        for i in range(len(first))
    ]


def matrix_inverse(matrix):
    order = len(matrix)
    work = [list(matrix[i]) + [1.0 if i == j else 0.0 for j in range(order)] for i in range(order)]
    for column in range(order):
        pivot = column
        for i in range(column + 1, order):
            if abs(work[i][column]) > abs(work[pivot][column]):
                pivot = i
        work[column], work[pivot] = (work[pivot], work[column])
        factor = work[column][column]
        work[column] = [entry / factor for entry in work[column]]
        for i in range(order):
            if i != column:
                scale_row = work[i][column]
                work[i] = [work[i][j] - scale_row * work[column][j] for j in range(2 * order)]
    return [row[order:] for row in work]


def eigen_vector(matrix, value):
    order = len(matrix)
    size_inner = order - 1
    system = []
    for i in range(size_inner):
        row = []
        for j in range(order):
            entry = (matrix[i][j], 0.0)
            if i == j:
                entry = pair_minus(entry, value)
            row.append(entry)
        row[order - 1] = (-row[order - 1][0], -row[order - 1][1])
        system.append(row)
    for column in range(size_inner):
        pivot = column
        for i in range(column + 1, size_inner):
            left_size = system[i][column][0] ** 2 + system[i][column][1] ** 2
            right_size = system[pivot][column][0] ** 2 + system[pivot][column][1] ** 2
            if left_size > right_size:
                pivot = i
        system[column], system[pivot] = (system[pivot], system[column])
        for i in range(size_inner):
            if i != column:
                factor = pair_over(system[i][column], system[column][column])
                system[i] = [
                    pair_minus(system[i][j], pair_times(factor, system[column][j]))
                    for j in range(order)
                ]
    vector = [pair_over(system[i][order - 1], system[i][i]) for i in range(size_inner)]
    vector.append((1.0, 0.0))
    return vector


def radau_tables():
    section_count = 5
    generator = [1.0]
    for k in range(section_count - 1):
        generator = poly_product(generator, [0.0, 1.0])
    for k in range(section_count):
        generator = poly_product(generator, [-1.0, 1.0])
    for k in range(section_count - 1):
        generator = [j * generator[j] for j in range(1, len(generator))]
    abscissae = sorted((root[0] for root in poly_roots(generator)))
    vander = [[abscissae[i] ** j for j in range(section_count)] for i in range(section_count)]
    integrals = [
        [abscissae[i] ** (j + 1) / (j + 1) for j in range(section_count)]
        for i in range(section_count)
    ]
    butcher = matrix_product(integrals, matrix_inverse(vander))
    inverse = matrix_inverse(butcher)
    coeffs = [0.0] * (section_count + 1)
    coeffs[section_count] = 1.0
    current = [[0.0] * section_count for _ in range(section_count)]
    for k in range(1, section_count + 1):
        current = matrix_product(inverse, current)
        for i in range(section_count):
            current[i][i] = current[i][i] + coeffs[section_count - k + 1]
        applied = matrix_product(inverse, current)
        coeffs[section_count - k] = -sum((applied[i][i] for i in range(section_count))) / k
    eigen_values = poly_roots(coeffs)
    real_pick = 0
    for k in range(section_count):
        if abs(eigen_values[k][1]) < abs(eigen_values[real_pick][1]):
            real_pick = k
    upper_half = [k for k in range(section_count) if eigen_values[k][1] > 1e-09]
    upper_half = sorted(upper_half, key=lambda k: -eigen_values[k][0])
    columns = [[entry[0] for entry in eigen_vector(inverse, (eigen_values[real_pick][0], 0.0))]]
    for k in upper_half:
        vector = eigen_vector(inverse, eigen_values[k])
        columns.append([entry[0] for entry in vector])
        columns.append([entry[1] for entry in vector])
    transform = [[columns[j][i] for j in range(section_count)] for i in range(section_count)]
    inverse_transform = matrix_inverse(transform)
    blocks = matrix_product(matrix_product(inverse_transform, inverse), transform)
    diagonal = [blocks[k][k] for k in range(section_count)]
    coupling = [
        blocks[k][slab_partner[k]] if slab_partner[k] != k else 0.0 for k in range(section_count)
    ]
    return (transform, inverse_transform, diagonal, coupling)


def left_by(value, count):
    return pltpu.roll(value, LANES - count, axis=1)


def right_by(value, count):
    return pltpu.roll(value, count, axis=1)


def from_above(value):
    return pltpu.roll(value, value.shape[0] - 1, axis=0)


def from_below(value):
    return pltpu.roll(value, 1, axis=0)


def lane_ids(layers):
    return lax.broadcasted_iota(jnp.int32, (layers, LANES), 1)


def layer_ids(layers):
    return lax.broadcasted_iota(jnp.int32, (layers, LANES), 0)


def is_low(layers, stride):
    return (lane_ids(layers) // stride) % 2 == 0


def blocks(count, step, body):
    if count <= step:
        body(0)
        return

    def one(b, carry):
        body(b * step)
        return carry

    lax.fori_loop(0, count // step, one, 0)


def seam_low(level, value):
    if level == 1:
        return right_by(value, 1)
    return jnp.where(is_low(value.shape[0], 2), left_by(value, 1), right_by(value, 2))


def seam_high(level, value):
    if level == 1:
        return left_by(value, 1)
    return jnp.where(is_low(value.shape[0], 2), left_by(value, 2), right_by(value, 1))


def merge(low, stride, first, second):
    return jnp.where(low, first + left_by(first, stride), second + right_by(second, stride))


def weights(cap, total, lam0, alpha, beta):
    real = lam0 * cap + total
    mate = beta * cap
    both = alpha * cap + total
    scale = damping / (both * both + mate * mate)
    return damping / real, both * scale, mate * scale, real, both, mate


def solve_node(fields, weight, values):
    if fields == REAL:
        return (weight[0] * values[0],)
    return (
        weight[1] * values[0] - weight[2] * values[1],
        weight[1] * values[1] + weight[2] * values[0],
    )


def sweep(level, refs, fields, source, restrict=False):
    edge, g, x, f = refs[level]
    tiles, layers = f.shape[1], f.shape[2]
    stride = 2**level
    half = tiles // 2
    step = min(STEP, half)
    target = 1 - source
    if level:
        for k in fields:
            x[source, k, 0] = seam_low(level, x[source, k, tiles])
            x[source, k, tiles + 1] = seam_high(level, x[source, k, 1])

    def part(begin):
        found = []
        xs = [[x[source, k, begin + r] for r in range(step + 2)] for k in fields]
        for r in range(step):
            i = begin + r
            ahead, behind = edge[i + 1], edge[i]
            gy, gy_low, gv, gv_low = g[GY, i], g[GY_LOW, i], g[GV, i], g[GV_LOW, i]
            here = [xs[n][r + 1] for n in range(len(fields))]
            values = []
            for n, k in enumerate(fields):
                along = ahead * xs[n][r + 2] + behind * xs[n][r]
                across = gy * left_by(here[n], stride) + gy_low * right_by(here[n], stride)
                through = gv * from_above(here[n]) + gv_low * from_below(here[n])
                values.append((f[k, i] + along) + (across + through))
            if not restrict:
                if fields == REAL:
                    weight = (g[W_REAL, i],)
                else:
                    weight = (None, g[W_SAME, i], g[W_MATE, i])
                change = solve_node(fields, weight, values)
                found.append([(1.0 - damping) * here[n] + change[n] for n in range(len(fields))])
            elif fields == REAL:
                found.append([values[0] - g[D_REAL, i] * here[0]])
            else:
                same, mate = g[D_SAME, i], g[D_MATE, i]
                found.append(
                    [
                        values[0] - same * here[0] - mate * here[1],
                        values[1] - same * here[1] + mate * here[0],
                    ]
                )
        return found

    def body(start):
        parts = [part(start), part(half + start)]
        if not restrict:
            for p in range(2):
                for r in range(step):
                    for n, k in enumerate(fields):
                        x[target, k, p * half + start + r + 1] = parts[p][r][n]
            return
        edge_next, g_next, x_next, f_next = refs[level + 1]
        low = is_low(layers, stride)
        for r in range(0, step, 2):
            i = start // 2 + r // 2
            summed = [
                merge(
                    low,
                    stride,
                    parts[0][r][n] + parts[0][r + 1][n],
                    parts[1][r][n] + parts[1][r + 1][n],
                )
                for n in range(len(fields))
            ]
            weight = [g_next[w, i] for w in (W_REAL, W_SAME, W_MATE)]
            first = solve_node(fields, weight, summed)
            for n, k in enumerate(fields):
                f_next[k, i] = summed[n]
                x_next[0, k, i + 1] = first[n]

    blocks(half, step, body)


def prolong(level, refs, fields, target):
    x, f = refs[level][2:]
    x_next, f_next = refs[level + 1][2:]
    layers = f.shape[2]
    stride = 2**level
    half = f.shape[1] // 2
    count = f_next.shape[1]
    step = min(STEP, count)

    def body(start):
        low = is_low(layers, stride)
        for r in range(step):
            for k in fields:
                coarse = x_next[1, k, start + r + 1]
                both = (
                    jnp.where(low, coarse, right_by(coarse, stride)),
                    jnp.where(low, left_by(coarse, stride), coarse),
                )
                for p in range(2):
                    for t in range(2):
                        row = p * half + 2 * (start + r) + t + 1
                        x[target, k, row] = x[target, k, row] + both[p]

    blocks(count, step, body)


def coarsen(level, refs, scal):
    edge, g = refs[level][:2]
    edge_next, g_next = refs[level + 1][:2]
    layers = g.shape[2]
    stride = 2**level
    half = g.shape[1] // 2
    count = g_next.shape[1]
    step = min(STEP, count)

    def cross(start):
        low = is_low(layers, stride)
        for r in range(step):
            j = 2 * (start + r) + 2
            edge_next[start + r + 1] = merge(low, stride, edge[j], edge[half + j])

    blocks(count, step, cross)
    first = seam_low(level + 1, edge_next[count])
    edge_next[0] = jnp.where(lane_ids(layers) % (2 * stride) == 0, 0.0, first)

    def body(start):
        low = is_low(layers, stride)
        for r in range(step):
            i = start + r
            j = 2 * i

            def summed(plane, p):
                return g[plane, p * half + j] + g[plane, p * half + j + 1]

            def joined(plane):
                return merge(low, stride, summed(plane, 0), summed(plane, 1))

            gy = jnp.where(low, left_by(summed(GY, 0), stride), summed(GY, 1))
            gv, ground, cap = joined(GV), joined(GROUND), joined(CAP)
            gy_low, gv_low = right_by(gy, 2 * stride), from_below(gv)
            total = (edge_next[i + 1] + edge_next[i]) + (gy + gy_low) + (gv + gv_low) + ground
            found = weights(cap, total, *scal)
            for k, entry in enumerate((gy, gv, gy_low, gv_low) + found + (ground, cap)):
                g_next[k + 1, i] = entry

    blocks(count, step, body)


def cycle(refs, fields):
    sweep(0, refs, fields, 0)
    sweep(0, refs, fields, 1, restrict=True)
    sweep(1, refs, fields, 0)
    sweep(1, refs, fields, 1, restrict=True)
    for n in range(3):
        sweep(2, refs, fields, n % 2)
    prolong(1, refs, fields, 1)
    sweep(1, refs, fields, 1)
    sweep(1, refs, fields, 0)
    prolong(0, refs, fields, 1)
    sweep(0, refs, fields, 1)
    sweep(0, refs, fields, 0)


def kernel(
    sizes, tables, load_table, voltage_in, capacity_in, node_class_in, via_sites_in,
    ball_sites_in, load_type_in, sections, next_voltage,
    voltage, capacity, node_class, via_sites, ball_sites, load_type,
    planes, edge, edge_in, send, recv, surf, e0, e1, e2, g0, g1, g2, x0, x1, x2, f0, f1, f2,
    packed, landed, pair_buf, pair_in, real_buf, real_in,
    load_sem, edge_send, edge_recv, send_sem, recv_sem, pass_send, pass_recv,
    ring_send, ring_recv, pair_send, pair_recv, real_send, real_recv, own_sem,
):
    parts, gx_count, gy_count, width, margin, columns = sizes
    transform, inverse_transform, diagonal, coupling = tables
    layers = voltage.shape[0]
    block = voltage.shape[1]
    wide = voltage.shape[2]
    tiles = wide // LANES
    regions = parts // 2
    count = 4 * block + 1
    section_here = lax.axis_index("section")
    gx_here = lax.axis_index("gx")
    gy_here = lax.axis_index("gy")
    mine = section_here * gx_count + gx_here
    system = section_here % 2
    all_regions = regions * gy_count

    def snake(place, row):
        return place + (row % 2) * (gx_count - 1 - 2 * place)

    def turned(place, column):
        return place + (column % 2) * (regions - 1 - 2 * place)

    pair = section_here // 2
    spot = turned(pair * gx_count + snake(gx_here, pair), gy_here)
    region = gy_here * regions + spot

    def owner(place, column):
        found = turned(place, column)
        row = found // gx_count
        return row * 2 + system, snake(found % gx_count, row)

    def group_device(index):
        return {"section": index // gx_count, "gx": index % gx_count}

    def region_device(index):
        column = index // regions
        owner_section, owner_gx = owner(index % regions, column)
        return {"section": owner_section, "gx": owner_gx, "gy": column}

    after = region_device((region + 1) % all_regions)
    before = region_device((region + all_regions - 1) % all_regions)
    right = {"gy": (gy_here + 1) % gy_count}
    left = {"gy": (gy_here + gy_count - 1) % gy_count}
    has_after = region < all_regions - 1
    has_before = region > 0
    has_right = gy_here < gy_count - 1
    has_left = gy_here > 0
    partner = {"section": section_here + 1 - 2 * system}

    barrier = pltpu.get_barrier_semaphore()

    def greet(place):
        pl.semaphore_signal(
            barrier, inc=1, device_id=place, device_id_type=pl.DeviceIdType.MESH
        )

    for d in range(1, parts):
        greet(group_device((mine + d) % parts))
    greeted = parts - 1
    ends = ((has_right, right), (has_left, left))
    ring_ends = ((has_after, after), (has_before, before)) if margin < BOTH_CYCLES else ()
    for exists, place in ends + ring_ends:
        greeted = greeted + exists.astype(jnp.int32)

        @pl.when(exists)
        def _():
            greet(place)

    fetches = []
    for n, (whole, here) in enumerate(
        (
            (node_class_in, node_class),
            (via_sites_in, via_sites),
            (ball_sites_in, ball_sites),
            (load_type_in, load_type),
            (voltage_in, voltage),
            (capacity_in, capacity),
        )
    ):
        copy = pltpu.make_async_copy(whole, here, load_sem.at[n])
        copy.start()
        fetches.append(copy)
    for copy in fetches:
        copy.wait()

    def remote(source, target, source_sem, target_sem, place):
        return pltpu.make_async_remote_copy(
            src_ref=source,
            dst_ref=target,
            send_sem=source_sem,
            recv_sem=target_sem,
            device_id=place,
            device_id_type=pl.DeviceIdType.MESH,
        )

    lanes = lane_ids(layers)
    zero = jnp.zeros((layers, LANES), jnp.float32)

    def turn_by(value, amount):
        amount = amount % LANES
        return right_by(value, amount) if amount else value

    for tile in range(tiles):
        place = pl.ds(tile * LANES, LANES)
        kind = node_class[:, :, place]
        resist = jnp.full(kind.shape, 0.5 / node_table[0], jnp.float32)
        for k in range(1, len(node_table)):
            resist = jnp.where(kind == k, jnp.float32(0.5 / node_table[k]), resist)
        via = jnp.where(via_sites[:, :, place] == 1, jnp.float32(via_conductance), 0.0)
        ball = jnp.where(ball_sites[:, place] == 1, jnp.float32(ball_conductance), 0.0)
        sites = jnp.concatenate([via, ball[None]], axis=0)
        for k, value in enumerate((voltage[:, :, place], capacity[:, :, place], resist, sites)):
            swapped = jnp.swapaxes(value, 0, 1)
            for r in range(block):
                planes[4 * r + k, :, place] = swapped[r]
        planes[4 * block, :, place] = load_type[:, place].astype(jnp.float32)

    share = LANES // margin
    packs = edge.shape[1]
    for side, begin in ((0, LANES - margin), (1, 0)):
        place = pl.ds((tiles - 1) * LANES if side == 0 else 0, LANES)
        for q in range(packs):
            joint = zero
            for t in range(share):
                plane = q + packs * t
                if plane < count:
                    moved = turn_by(planes[plane, :, place], margin * t - begin)
                    joint = jnp.where(lanes // margin == t, moved, joint)
            edge[side, q] = joint
    pl.semaphore_wait(barrier, greeted)
    edges = [
        (exists, came, remote(edge.at[i], edge_in.at[i], edge_send.at[i], edge_recv.at[i], place))
        for i, exists, came, place in (
            (0, has_right, has_left, right),
            (1, has_left, has_right, left),
        )
    ]
    for side, (exists, came, copy) in enumerate(edges):

        @pl.when(exists)
        def _():
            copy.start()

        @pl.when(jnp.logical_not(came))
        def _():
            edge_in[side] = jnp.zeros(edge_in.shape[1:], jnp.float32)

    def build(k):
        start = width * k - margin
        for plane in range(count):
            q, t = plane % packs, plane // packs
            joint = None
            for tile in range(-1, tiles + 1):
                low = tile * LANES if tile >= 0 else -margin
                high = (tile + 1) * LANES if tile >= 0 else 0
                if tile == tiles:
                    high = low + margin
                if high <= start or low >= start + LANES:
                    continue
                if tile < 0:
                    moved = turn_by(edge_in[0, q], -margin - start - margin * t)
                elif tile == tiles:
                    moved = turn_by(edge_in[1, q], wide - start - margin * t)
                else:
                    moved = turn_by(planes[plane, :, pl.ds(low, LANES)], low - start)
                joint = moved if joint is None else jnp.where(lanes >= low - start, moved, joint)
            send[k, plane] = joint

    def direct(d, k):
        owner_section, owner_gx = owner(k, gy_here)
        return remote(
            send.at[k], recv.at[mine], send_sem.at[d], recv_sem.at[d],
            {"section": owner_section, "gx": owner_gx},
        )

    def handed(d, source, slot):
        return remote(source, recv.at[slot], pass_send.at[d], pass_recv.at[d], partner)

    own = pltpu.make_async_copy(send.at[spot], recv.at[mine], own_sem.at[0])

    def dispatch(k):
        d = (k - spot + regions) % regions

        @pl.when(d != 0)
        def _():
            direct(d, k).start()

        @pl.when(d == 0)
        def _():
            own.start()
            handed(0, send.at[k], mine).start()

    inner = [k for k in range(regions) if margin <= width * k <= wide - LANES + margin]
    outer = [k for k in range(regions) if k not in inner]
    for k in inner:
        build(k)
    for k in inner:
        dispatch(k)
    for exists, came, copy in edges:

        @pl.when(exists)
        def _():
            copy.wait_send()

        @pl.when(came)
        def _():
            copy.wait_recv()

    for k in outer:
        build(k)
    for k in outer:
        dispatch(k)

    def pick(table):
        return [
            jnp.where(system == 0, jnp.float32(table[a]), jnp.float32(table[b]))
            for a, b in ((0, 0), (1, 3), (2, 4))
        ]

    shifts = pick(diagonal)
    lam0, alpha, beta = shifts[0], shifts[1], pick(coupling)[1]
    shares = pick([sum(row) for row in inverse_transform])
    mixing = [pick([row[j] for row in inverse_transform]) for j in range(SECTIONS)]
    scal = (lam0, alpha, beta)
    for slot in range(2):
        for k in range(3):
            x0[slot, k, 0] = zero
            x0[slot, k, x0.shape[2] - 1] = zero
    e0[0] = zero
    passes = [handed(0, send.at[spot], mine)]
    for d in range(1, regions):
        direct(d, (spot + d) % regions).wait()
        owner_section, owner_gx = owner((spot - d + regions) % regions, gy_here)
        slot = owner_section * gx_count + owner_gx
        copy = handed(d, recv.at[slot], slot)
        copy.start()
        passes.append(copy)
    own.wait()
    for copy in passes:
        copy.wait()

    def loads(b, carry):
        kind = recv[b, 4 * block]
        currents = [zero] * SECTIONS
        for t in range(LOADS):
            here = kind == float(t)
            for j in range(SECTIONS):
                currents[j] = jnp.where(here, load_table[j, t], currents[j])
        for k in range(3):
            surf[k, b] = sum(mixing[j][k] * currents[j] for j in range(SECTIONS))
        return carry

    lax.fori_loop(0, parts, loads, 0)

    rows = parts * block
    level_of = layer_ids(layers)
    column = region * width - margin + lanes
    inside = (column >= 0) & (column < columns)
    joined = inside & (column < columns - 1) & (lanes < LANES - 1)

    def fine(b, carry):
        behind_gx, volt_behind = carry
        following = jnp.minimum(b + 1, parts - 1)
        for r in range(block):
            i = b * block + r
            volt, cap = recv[b, 4 * r], recv[b, 4 * r + 1]
            resist = jnp.where(inside, recv[b, 4 * r + 2], 0.5)
            sites = recv[b, 4 * r + 3]
            if r + 1 < block:
                volt_ahead, resist_ahead = recv[b, 4 * r + 4], recv[b, 4 * r + 6]
            else:
                volt_ahead, resist_ahead = recv[following, 0], recv[following, 2]
            resist_ahead = jnp.where(inside, resist_ahead, 0.5)
            gx = 1.0 / (resist + resist_ahead)
            if r + 1 == block:
                gx = gx * (b < parts - 1).astype(jnp.float32)
            gy = jnp.where(joined, 1.0 / (resist + left_by(resist, 1)), 0.0)
            gv = jnp.where(level_of < layers - 1, sites, 0.0)
            ground = jnp.where(level_of == 0, from_below(sites), 0.0)
            gy_low, gv_low = right_by(gy, 1), from_below(gv)
            total = (gx + behind_gx) + (gy + gy_low) + (gv + gv_low) + ground
            found = weights(cap, total, *scal)
            pulled = (gx * volt_ahead + behind_gx * volt_behind) + (
                gy * left_by(volt, 1) + gy_low * right_by(volt, 1)
            ) + (gv * from_above(volt) + gv_low * from_below(volt))
            leak = total * volt - pulled
            e0[i + 1] = gx
            for k, entry in enumerate((gy, gv, gy_low, gv_low) + found + (ground, cap)):
                g0[k + 1, i] = entry
            source = [
                jnp.where(
                    level_of == layers - 1,
                    jnp.broadcast_to(surf[k, b, r : r + 1, :], (layers, LANES)),
                    0.0,
                )
                - shares[k] * leak
                for k in range(3)
            ]
            first = solve_node(REAL, found, source[:1]) + solve_node(PAIR, found, source[1:])
            for k in range(3):
                f0[k, i] = source[k]
                x0[0, k, i + 1] = first[k]
            behind_gx, volt_behind = gx, volt
        return behind_gx, volt_behind

    lax.fori_loop(0, parts, fine, (zero, zero))
    refs = ((e0, g0, x0, f0), (e1, g1, x1, f1), (e2, g2, x2, f2))
    coarsen(0, refs, scal)
    coarsen(1, refs, scal)

    ringed = margin < BOTH_CYCLES
    ring_share = LANES // margin
    ring_groups = rows // ring_share

    def exchange(fields):
        def pack(start):
            for q in range(min(8, ring_groups)):
                for side, begin in ((0, width), (1, margin)):
                    for k in fields:
                        joint = zero
                        for t in range(ring_share):
                            held = x0[1, k, start + q + ring_groups * t + 1]
                            moved = turn_by(held, margin * t - begin)
                            joint = jnp.where(lanes // margin == t, moved, joint)
                        packed[side, k, start + q] = joint

        blocks(ring_groups, min(8, ring_groups), pack)
        span = pl.ds(fields[0], len(fields))
        copies = []
        for side, exists, came, place in (
            (0, has_after, has_before, after),
            (1, has_before, has_after, before),
        ):
            slot = 2 * (len(fields) - 1) + side
            copy = remote(
                packed.at[side, span], landed.at[side, span],
                ring_send.at[slot], ring_recv.at[slot], place,
            )
            copies.append((exists, came, copy))

            @pl.when(exists)
            def _():
                copy.start()

        return copies

    def finish(fields, copies):
        for exists, came, copy in copies:

            @pl.when(exists)
            def _():
                copy.wait_send()

            @pl.when(came)
            def _():
                copy.wait_recv()

        low_end = jnp.where(has_before, margin, 0)
        high_end = jnp.where(has_after, margin + width, LANES)

        def unpack(start):
            for q in range(min(8, ring_groups)):
                for k in fields:
                    low, high = landed[0, k, start + q], landed[1, k, start + q]
                    for t in range(ring_share):
                        row = start + q + ring_groups * t + 1
                        below = turn_by(low, -margin * t)
                        above = turn_by(high, margin + width - margin * t)
                        held = jnp.where(lanes < high_end, x0[1, k, row], above)
                        x0[1, k, row] = jnp.where(lanes < low_end, below, held)

        blocks(ring_groups, min(8, ring_groups), unpack)

    share = LANES // width
    groups = block // share
    half = max(groups // 2, 1)
    halves = groups // half
    slot_out = spot * 2 + system

    def give(fields, buf, into, sends, recvs, own):
        copies = []
        for d in range(parts):
            peer = (mine + d) % parts
            for n, k in enumerate(fields):
                for index in range(half if fields == REAL else groups):
                    q = index
                    if fields == REAL and halves > 1:
                        q = index + system * half
                    joint = zero
                    for t in range(share):
                        held = x0[1, k, peer * block + q + groups * t + 1]
                        moved = turn_by(held, width * t - margin)
                        joint = jnp.where(lanes // width == t, moved, joint)
                    buf[d, n * groups + index] = joint
            if d == 0:
                copy = pltpu.make_async_copy(buf.at[0], into.at[slot_out], own)
            else:
                copy = remote(
                    buf.at[d], into.at[slot_out], sends.at[d], recvs.at[d], group_device(peer)
                )
            copy.start()
            copies.append(copy)
        return copies

    cycle(refs, PAIR)
    pair_ring = exchange(PAIR) if ringed else []
    cycle(refs, REAL)
    real_ring = exchange(REAL) if ringed else []
    if ringed:
        finish(PAIR, pair_ring)
    sweep(0, refs, PAIR, 1)
    cycle(refs, PAIR)
    given = give(PAIR, pair_buf, pair_in, pair_send, pair_recv, own_sem.at[1])
    if ringed:
        finish(REAL, real_ring)
    sweep(0, refs, REAL, 1)
    cycle(refs, REAL)
    given += give(REAL, real_buf, real_in, real_send, real_recv, own_sem.at[2])
    for copy in given:
        copy.wait()

    for tile in range(regions // share):
        mixed = [[None] * block for _ in range(SECTIONS)]
        for q in range(groups):
            fields = []
            for n in range(share):
                first = 2 * (tile * share + n)
                fields.append(
                    [real_in[first + q // half, q % half]]
                    + [pair_in[first, k * groups + q] for k in (0, 1)]
                    + [pair_in[first + 1, k * groups + q] for k in (0, 1)]
                )
            for s in range(SECTIONS):
                sums = [
                    sum(transform[s][k] * fields[n][k] for k in range(SECTIONS))
                    for n in range(share)
                ]
                for t in range(share):
                    joint = zero
                    for n in range(share):
                        turn = (width * (n - t)) % LANES
                        moved = right_by(sums[n], turn) if turn else sums[n]
                        joint = jnp.where(lanes // width == n, moved, joint)
                    mixed[s][q + groups * t] = joint
        place = pl.ds(tile * LANES, LANES)
        for s in range(SECTIONS):
            turned = jnp.swapaxes(jnp.stack(mixed[s]), 0, 1)
            sections[s, :, :, place] = turned
            if s == SECTIONS - 1:
                next_voltage[:, :, place] = voltage[:, :, place] + turned


def local(voltage, capacity, node_class, via_sites, ball_sites, load_type, load_table):
    layers, block, wide = voltage.shape
    gx_count = lax.axis_size("gx")
    gy_count = lax.axis_size("gy")
    parts = lax.axis_size("section") * gx_count
    regions = parts // 2
    width = wide // regions
    margin = (LANES - width) // 2
    sizes = (parts, gx_count, gy_count, width, margin, wide * gy_count)
    rows = parts * block
    count = 4 * block + 1
    packs = -(-count // (LANES // margin))

    def vmem(*shape):
        return pltpu.VMEM(shape, jnp.float32)

    def levels(extra, *lead):
        return [vmem(*lead, rows // 4**m + extra, layers, LANES) for m in range(LEVELS)]

    mid = rows * margin // LANES if margin < BOTH_CYCLES else 1
    groups = block * width // LANES
    return pl.pallas_call(
        functools.partial(kernel, sizes, radau_tables()),
        out_shape=(
            jax.ShapeDtypeStruct((SECTIONS, layers, block, wide), jnp.float32),
            jax.ShapeDtypeStruct((layers, block, wide), jnp.float32),
        ),
        in_specs=[
            pl.BlockSpec(memory_space=pltpu.SMEM),
            *[pl.BlockSpec(memory_space=pl.ANY)] * 6,
        ],
        out_specs=(
            pl.BlockSpec(memory_space=pltpu.VMEM),
            pl.BlockSpec(memory_space=pltpu.VMEM),
        ),
        scratch_shapes=[
            vmem(*voltage.shape),
            vmem(*capacity.shape),
            pltpu.VMEM(node_class.shape, jnp.int32),
            pltpu.VMEM(via_sites.shape, jnp.int32),
            pltpu.VMEM(ball_sites.shape, jnp.int32),
            pltpu.VMEM(load_type.shape, jnp.int32),
            vmem(count, layers, wide),
            vmem(2, packs, layers, LANES),
            vmem(2, packs, layers, LANES),
            vmem(regions, count, layers, LANES),
            vmem(parts, count, layers, LANES),
            vmem(3, parts, block, LANES),
            *levels(1),
            *levels(0, COEFFS),
            *levels(2, 2, 3),
            *levels(0, 3),
            vmem(2, 3, mid, layers, LANES),
            vmem(2, 3, mid, layers, LANES),
            *[vmem(parts, 2 * groups, layers, LANES)] * 2,
            *[vmem(parts, max(groups // 2, 1), layers, LANES)] * 2,
            pltpu.SemaphoreType.DMA((6,)),
            pltpu.SemaphoreType.DMA((2,)),
            pltpu.SemaphoreType.DMA((2,)),
            pltpu.SemaphoreType.DMA((regions,)),
            pltpu.SemaphoreType.DMA((regions,)),
            pltpu.SemaphoreType.DMA((regions,)),
            pltpu.SemaphoreType.DMA((regions,)),
            pltpu.SemaphoreType.DMA((4,)),
            pltpu.SemaphoreType.DMA((4,)),
            *[pltpu.SemaphoreType.DMA((parts,))] * 4,
            pltpu.SemaphoreType.DMA((3,)),
        ],
        compiler_params=pltpu.CompilerParams(
            collective_id=0, has_side_effects=True, vmem_limit_bytes=60 * 1024 * 1024
        ),
    )(load_table.T, voltage, capacity, node_class, via_sites, ball_sites, load_type)


def solution(mesh):
    return jax.shard_map(
        local,
        mesh=mesh,
        in_specs=(
            P(None, row_axes, "gy"),
            P(None, row_axes, "gy"),
            P(None, row_axes, "gy"),
            P(None, row_axes, "gy"),
            P(row_axes, "gy"),
            P(row_axes, "gy"),
            P(),
        ),
        out_specs=(P(None, None, row_axes, "gy"), P(None, row_axes, "gy")),
        check_vma=False,
    )
```

```python
import functools

import jax
import jax.numpy as jnp
from jax import lax
from jax.experimental import pallas as pl
from jax.experimental.pallas import tpu as pltpu
from jax.sharding import PartitionSpec as P

SECTIONS = 5
LEVELS = 3
LOADS = 16
LANES = 128
BOTH_CYCLES = 56
STEP = 32
REAL = (0,)
PAIR = (1, 2)
GX, GY, GV, GY_LOW, GV_LOW, W_REAL, W_SAME, W_MATE, D_REAL, D_SAME, D_MATE, GROUND, CAP = range(13)
COEFFS = 13

node_table = (0.35, 0.55, 0.8, 1.1, 1.5, 2.0, 2.7, 3.6)
via_conductance = 2.5
ball_conductance = 4.0
damping = 0.8
slab_partner = (0, 2, 1, 4, 3)
row_axes = ("section", "gx")


def pair_times(first, second):
    return (
        first[0] * second[0] - first[1] * second[1],
        first[0] * second[1] + first[1] * second[0],
    )


def pair_over(first, second):
    divisor = second[0] * second[0] + second[1] * second[1]
    return (
        (first[0] * second[0] + first[1] * second[1]) / divisor,
        (first[1] * second[0] - first[0] * second[1]) / divisor,
    )


def pair_minus(first, second):
    return (first[0] - second[0], first[1] - second[1])


def poly_value(coeffs, point):
    total = (0.0, 0.0)
    for c in reversed(coeffs):
        total = pair_times(total, point)
        total = (total[0] + c, total[1])
    return total


def poly_product(first, second):
    result = [0.0] * (len(first) + len(second) - 1)
    for i in range(len(first)):
        for j in range(len(second)):
            result[i + j] = result[i + j] + first[i] * second[j]
    return result


def poly_roots(coeffs):
    leading = coeffs[-1]
    scaled = [c / leading for c in coeffs]
    degree = len(coeffs) - 1
    guesses = []
    current = (1.0, 0.0)
    for k in range(degree):
        guesses.append(current)
        current = pair_times(current, (0.4, 0.9))
    for repeat_index in range(800):
        for k in range(degree):
            divisor = (1.0, 0.0)
            for j in range(degree):
                if j != k:
                    divisor = pair_times(divisor, pair_minus(guesses[k], guesses[j]))
            guesses[k] = pair_minus(guesses[k], pair_over(poly_value(scaled, guesses[k]), divisor))
    return guesses


def matrix_product(first, second):
    return [
        [
            sum((first[i][k] * second[k][j] for k in range(len(second))))
            for j in range(len(second[0]))
        ]
        for i in range(len(first))
    ]


def matrix_inverse(matrix):
    order = len(matrix)
    work = [list(matrix[i]) + [1.0 if i == j else 0.0 for j in range(order)] for i in range(order)]
    for column in range(order):
        pivot = column
        for i in range(column + 1, order):
            if abs(work[i][column]) > abs(work[pivot][column]):
                pivot = i
        work[column], work[pivot] = (work[pivot], work[column])
        factor = work[column][column]
        work[column] = [entry / factor for entry in work[column]]
        for i in range(order):
            if i != column:
                scale_row = work[i][column]
                work[i] = [work[i][j] - scale_row * work[column][j] for j in range(2 * order)]
    return [row[order:] for row in work]


def eigen_vector(matrix, value):
    order = len(matrix)
    size_inner = order - 1
    system = []
    for i in range(size_inner):
        row = []
        for j in range(order):
            entry = (matrix[i][j], 0.0)
            if i == j:
                entry = pair_minus(entry, value)
            row.append(entry)
        row[order - 1] = (-row[order - 1][0], -row[order - 1][1])
        system.append(row)
    for column in range(size_inner):
        pivot = column
        for i in range(column + 1, size_inner):
            left_size = system[i][column][0] ** 2 + system[i][column][1] ** 2
            right_size = system[pivot][column][0] ** 2 + system[pivot][column][1] ** 2
            if left_size > right_size:
                pivot = i
        system[column], system[pivot] = (system[pivot], system[column])
        for i in range(size_inner):
            if i != column:
                factor = pair_over(system[i][column], system[column][column])
                system[i] = [
                    pair_minus(system[i][j], pair_times(factor, system[column][j]))
                    for j in range(order)
                ]
    vector = [pair_over(system[i][order - 1], system[i][i]) for i in range(size_inner)]
    vector.append((1.0, 0.0))
    return vector


def radau_tables():
    section_count = 5
    generator = [1.0]
    for k in range(section_count - 1):
        generator = poly_product(generator, [0.0, 1.0])
    for k in range(section_count):
        generator = poly_product(generator, [-1.0, 1.0])
    for k in range(section_count - 1):
        generator = [j * generator[j] for j in range(1, len(generator))]
    abscissae = sorted((root[0] for root in poly_roots(generator)))
    vander = [[abscissae[i] ** j for j in range(section_count)] for i in range(section_count)]
    integrals = [
        [abscissae[i] ** (j + 1) / (j + 1) for j in range(section_count)]
        for i in range(section_count)
    ]
    butcher = matrix_product(integrals, matrix_inverse(vander))
    inverse = matrix_inverse(butcher)
    coeffs = [0.0] * (section_count + 1)
    coeffs[section_count] = 1.0
    current = [[0.0] * section_count for _ in range(section_count)]
    for k in range(1, section_count + 1):
        current = matrix_product(inverse, current)
        for i in range(section_count):
            current[i][i] = current[i][i] + coeffs[section_count - k + 1]
        applied = matrix_product(inverse, current)
        coeffs[section_count - k] = -sum((applied[i][i] for i in range(section_count))) / k
    eigen_values = poly_roots(coeffs)
    real_pick = 0
    for k in range(section_count):
        if abs(eigen_values[k][1]) < abs(eigen_values[real_pick][1]):
            real_pick = k
    upper_half = [k for k in range(section_count) if eigen_values[k][1] > 1e-09]
    upper_half = sorted(upper_half, key=lambda k: -eigen_values[k][0])
    columns = [[entry[0] for entry in eigen_vector(inverse, (eigen_values[real_pick][0], 0.0))]]
    for k in upper_half:
        vector = eigen_vector(inverse, eigen_values[k])
        columns.append([entry[0] for entry in vector])
        columns.append([entry[1] for entry in vector])
    transform = [[columns[j][i] for j in range(section_count)] for i in range(section_count)]
    inverse_transform = matrix_inverse(transform)
    blocks = matrix_product(matrix_product(inverse_transform, inverse), transform)
    diagonal = [blocks[k][k] for k in range(section_count)]
    coupling = [
        blocks[k][slab_partner[k]] if slab_partner[k] != k else 0.0 for k in range(section_count)
    ]
    return (transform, inverse_transform, diagonal, coupling)


def left_by(value, count):
    return pltpu.roll(value, LANES - count, axis=1)


def right_by(value, count):
    return pltpu.roll(value, count, axis=1)


def from_above(value):
    return pltpu.roll(value, value.shape[0] - 1, axis=0)


def from_below(value):
    return pltpu.roll(value, 1, axis=0)


def lane_ids(layers):
    return lax.broadcasted_iota(jnp.int32, (layers, LANES), 1)


def layer_ids(layers):
    return lax.broadcasted_iota(jnp.int32, (layers, LANES), 0)


def is_low(layers, stride):
    return (lane_ids(layers) // stride) % 2 == 0


def blocks(count, step, body):
    if count <= step:
        body(0)
        return

    def one(b, carry):
        body(b * step)
        return carry

    lax.fori_loop(0, count // step, one, 0)


def seam_low(level, value):
    if level == 1:
        return right_by(value, 1)
    return jnp.where(is_low(value.shape[0], 2), left_by(value, 1), right_by(value, 2))


def seam_high(level, value):
    if level == 1:
        return left_by(value, 1)
    return jnp.where(is_low(value.shape[0], 2), left_by(value, 2), right_by(value, 1))


def merge(low, stride, first, second):
    return jnp.where(low, first + left_by(first, stride), second + right_by(second, stride))


def weights(cap, total, lam0, alpha, beta):
    real = lam0 * cap + total
    mate = beta * cap
    both = alpha * cap + total
    scale = damping / (both * both + mate * mate)
    return damping / real, both * scale, mate * scale, real, both, mate


def solve_node(fields, weight, values):
    if fields == REAL:
        return (weight[0] * values[0],)
    return (
        weight[1] * values[0] - weight[2] * values[1],
        weight[1] * values[1] + weight[2] * values[0],
    )


def sweep(level, refs, fields, source, restrict=False):
    edge, g, x, f = refs[level]
    tiles, layers = f.shape[1], f.shape[2]
    stride = 2**level
    half = tiles // 2
    step = min(STEP, half)
    target = 1 - source
    if level:
        for k in fields:
            x[source, k, 0] = seam_low(level, x[source, k, tiles])
            x[source, k, tiles + 1] = seam_high(level, x[source, k, 1])

    def part(begin):
        found = []
        xs = [[x[source, k, begin + r] for r in range(step + 2)] for k in fields]
        for r in range(step):
            i = begin + r
            ahead, behind = edge[i + 1], edge[i]
            gy, gy_low, gv, gv_low = g[GY, i], g[GY_LOW, i], g[GV, i], g[GV_LOW, i]
            here = [xs[n][r + 1] for n in range(len(fields))]
            values = []
            for n, k in enumerate(fields):
                along = ahead * xs[n][r + 2] + behind * xs[n][r]
                across = gy * left_by(here[n], stride) + gy_low * right_by(here[n], stride)
                through = gv * from_above(here[n]) + gv_low * from_below(here[n])
                values.append((f[k, i] + along) + (across + through))
            if not restrict:
                if fields == REAL:
                    weight = (g[W_REAL, i],)
                else:
                    weight = (None, g[W_SAME, i], g[W_MATE, i])
                change = solve_node(fields, weight, values)
                found.append([(1.0 - damping) * here[n] + change[n] for n in range(len(fields))])
            elif fields == REAL:
                found.append([values[0] - g[D_REAL, i] * here[0]])
            else:
                same, mate = g[D_SAME, i], g[D_MATE, i]
                found.append(
                    [
                        values[0] - same * here[0] - mate * here[1],
                        values[1] - same * here[1] + mate * here[0],
                    ]
                )
        return found

    def body(start):
        parts = [part(start), part(half + start)]
        if not restrict:
            for p in range(2):
                for r in range(step):
                    for n, k in enumerate(fields):
                        x[target, k, p * half + start + r + 1] = parts[p][r][n]
            return
        edge_next, g_next, x_next, f_next = refs[level + 1]
        low = is_low(layers, stride)
        for r in range(0, step, 2):
            i = start // 2 + r // 2
            summed = [
                merge(
                    low,
                    stride,
                    parts[0][r][n] + parts[0][r + 1][n],
                    parts[1][r][n] + parts[1][r + 1][n],
                )
                for n in range(len(fields))
            ]
            weight = [g_next[w, i] for w in (W_REAL, W_SAME, W_MATE)]
            first = solve_node(fields, weight, summed)
            for n, k in enumerate(fields):
                f_next[k, i] = summed[n]
                x_next[0, k, i + 1] = first[n]

    blocks(half, step, body)


def prolong(level, refs, fields, target):
    x, f = refs[level][2:]
    x_next, f_next = refs[level + 1][2:]
    layers = f.shape[2]
    stride = 2**level
    half = f.shape[1] // 2
    count = f_next.shape[1]
    step = min(STEP, count)

    def body(start):
        low = is_low(layers, stride)
        for r in range(step):
            for k in fields:
                coarse = x_next[1, k, start + r + 1]
                both = (
                    jnp.where(low, coarse, right_by(coarse, stride)),
                    jnp.where(low, left_by(coarse, stride), coarse),
                )
                for p in range(2):
                    for t in range(2):
                        row = p * half + 2 * (start + r) + t + 1
                        x[target, k, row] = x[target, k, row] + both[p]

    blocks(count, step, body)


def coarsen(level, refs, scal):
    edge, g = refs[level][:2]
    edge_next, g_next = refs[level + 1][:2]
    layers = g.shape[2]
    stride = 2**level
    half = g.shape[1] // 2
    count = g_next.shape[1]
    step = min(STEP, count)

    def cross(start):
        low = is_low(layers, stride)
        for r in range(step):
            j = 2 * (start + r) + 2
            edge_next[start + r + 1] = merge(low, stride, edge[j], edge[half + j])

    blocks(count, step, cross)
    first = seam_low(level + 1, edge_next[count])
    edge_next[0] = jnp.where(lane_ids(layers) % (2 * stride) == 0, 0.0, first)

    def body(start):
        low = is_low(layers, stride)
        for r in range(step):
            i = start + r
            j = 2 * i

            def summed(plane, p):
                return g[plane, p * half + j] + g[plane, p * half + j + 1]

            def joined(plane):
                return merge(low, stride, summed(plane, 0), summed(plane, 1))

            gy = jnp.where(low, left_by(summed(GY, 0), stride), summed(GY, 1))
            gv, ground, cap = joined(GV), joined(GROUND), joined(CAP)
            gy_low, gv_low = right_by(gy, 2 * stride), from_below(gv)
            total = (edge_next[i + 1] + edge_next[i]) + (gy + gy_low) + (gv + gv_low) + ground
            found = weights(cap, total, *scal)
            for k, entry in enumerate((gy, gv, gy_low, gv_low) + found + (ground, cap)):
                g_next[k + 1, i] = entry

    blocks(count, step, body)


def cycle(refs, fields):
    sweep(0, refs, fields, 0)
    sweep(0, refs, fields, 1, restrict=True)
    sweep(1, refs, fields, 0)
    sweep(1, refs, fields, 1, restrict=True)
    for n in range(3):
        sweep(2, refs, fields, n % 2)
    prolong(1, refs, fields, 1)
    sweep(1, refs, fields, 1)
    sweep(1, refs, fields, 0)
    prolong(0, refs, fields, 1)
    sweep(0, refs, fields, 1)
    sweep(0, refs, fields, 0)


def kernel(
    sizes, tables, load_table_in, voltage_in, capacity_in, node_class_in, via_sites_in,
    ball_sites_in, load_type_in, sections, next_voltage,
    load_table, voltage, capacity, node_class, via_sites, ball_sites, load_type,
    planes, edge, edge_in, send, recv, surf, e0, e1, e2, g0, g1, g2, x0, x1, x2, f0, f1, f2,
    packed, landed, pair_buf, pair_in, real_buf, real_in,
    load_sem, edge_send, edge_recv, edge_pass_send, edge_pass_recv, send_sem, recv_sem, pass_send, pass_recv,
    ring_send, ring_recv, pair_send, pair_recv, real_send, real_recv, own_sem,
):
    parts, gx_count, gy_count, width, margin, columns = sizes
    transform, inverse_transform, diagonal, coupling = tables
    layers = voltage.shape[0]
    block = voltage.shape[1]
    wide = voltage.shape[2]
    tiles = wide // LANES
    regions = parts // 2
    count = 4 * block + 1
    section_here = lax.axis_index("section")
    gx_here = lax.axis_index("gx")
    gy_here = lax.axis_index("gy")
    mine = section_here * gx_count + gx_here
    system = section_here % 2
    all_regions = regions * gy_count

    def snake(place, row):
        return place + (row % 2) * (gx_count - 1 - 2 * place)

    def turned(place, column):
        return place + (column % 2) * (regions - 1 - 2 * place)

    pair = section_here // 2
    spot = turned(pair * gx_count + snake(gx_here, pair), gy_here)
    region = gy_here * regions + spot

    def owner(place, column):
        found = turned(place, column)
        row = found // gx_count
        return row * 2 + system, snake(found % gx_count, row)

    def group_device(index):
        return {"section": index // gx_count, "gx": index % gx_count}

    def region_device(index):
        column = index // regions
        owner_section, owner_gx = owner(index % regions, column)
        return {"section": owner_section, "gx": owner_gx, "gy": column}

    after = region_device((region + 1) % all_regions)
    before = region_device((region + all_regions - 1) % all_regions)
    has_after = region < all_regions - 1
    has_before = region > 0
    seat = pair * gx_count + gx_here
    over = -(-margin // width)
    sides = (
        (gy_here < gy_count - 1, gy_here + 1, range(over), gy_here > 0, gy_here - 1, spot < over),
        (
            gy_here > 0, gy_here - 1, range(regions - over, regions),
            gy_here < gy_count - 1, gy_here + 1, spot >= regions - over,
        ),
    )
    partner = {"section": section_here + 1 - 2 * system}

    barrier = pltpu.get_barrier_semaphore()

    def greet(place):
        pl.semaphore_signal(
            barrier, inc=1, device_id=place, device_id_type=pl.DeviceIdType.MESH
        )

    for d in range(1, parts):
        greet(group_device((mine + d) % parts))
    greeted = parts - 1
    for sends, to_column, reach, comes, from_column, reached in sides:
        greeted = greeted + jnp.where(sends, over, 0)

        @pl.when(jnp.logical_and(comes, reached))
        def _():
            for place in range(regions):
                greet(
                    {
                        "section": place // gx_count * 2 + system,
                        "gx": place % gx_count,
                        "gy": from_column,
                    }
                )

    if margin < BOTH_CYCLES:
        for exists, place in ((has_after, after), (has_before, before)):
            greeted = greeted + exists.astype(jnp.int32)

            @pl.when(exists)
            def _():
                greet(place)

    fetches = []
    for n, (whole, here) in enumerate(
        (
            (node_class_in, node_class),
            (via_sites_in, via_sites),
            (ball_sites_in, ball_sites),
            (load_type_in, load_type),
            (voltage_in, voltage),
            (capacity_in, capacity),
            (load_table_in, load_table),
        )
    ):
        copy = pltpu.make_async_copy(whole, here, load_sem.at[n])
        copy.start()
        fetches.append(copy)
    for copy in fetches:
        copy.wait()

    def remote(source, target, source_sem, target_sem, place):
        return pltpu.make_async_remote_copy(
            src_ref=source,
            dst_ref=target,
            send_sem=source_sem,
            recv_sem=target_sem,
            device_id=place,
            device_id_type=pl.DeviceIdType.MESH,
        )

    lanes = lane_ids(layers)
    zero = jnp.zeros((layers, LANES), jnp.float32)

    def turn_by(value, amount):
        amount = amount % LANES
        return right_by(value, amount) if amount else value

    for tile in range(tiles):
        place = pl.ds(tile * LANES, LANES)
        kind = node_class[:, :, place]
        resist = jnp.full(kind.shape, 0.5 / node_table[0], jnp.float32)
        for k in range(1, len(node_table)):
            resist = jnp.where(kind == k, jnp.float32(0.5 / node_table[k]), resist)
        via = jnp.where(via_sites[:, :, place] == 1, jnp.float32(via_conductance), 0.0)
        ball = jnp.where(ball_sites[:, place] == 1, jnp.float32(ball_conductance), 0.0)
        sites = jnp.concatenate([via, ball[None]], axis=0)
        for k, value in enumerate((voltage[:, :, place], capacity[:, :, place], resist, sites)):
            swapped = jnp.swapaxes(value, 0, 1)
            for r in range(block):
                planes[4 * r + k, :, place] = swapped[r]
        planes[4 * block, :, place] = load_type[:, place].astype(jnp.float32)

    share = LANES // margin
    packs = edge.shape[1]
    for side, begin in ((0, LANES - margin), (1, 0)):
        place = pl.ds((tiles - 1) * LANES if side == 0 else 0, LANES)
        for q in range(packs):
            joint = zero
            for t in range(share):
                plane = q + packs * t
                if plane < count:
                    moved = turn_by(planes[plane, :, place], margin * t - begin)
                    joint = jnp.where(lanes // margin == t, moved, joint)
            edge[side, q] = joint
    pl.semaphore_wait(barrier, greeted)

    def edge_copy(side, n, place):
        return remote(
            edge.at[side], edge_in.at[side, mine], edge_send.at[side, n],
            edge_recv.at[side, seat], place,
        )

    def edge_places(side):
        to_column, reach = sides[side][1:3]
        for n, k in enumerate(reach):
            owner_section, owner_gx = owner(k, to_column)
            yield n, {"section": owner_section, "gx": owner_gx, "gy": to_column}

    for side in range(2):

        @pl.when(sides[side][0])
        def _():
            for n, place in edge_places(side):
                edge_copy(side, n, place).start()

    def build(k):
        start = width * k - margin
        for plane in range(count):
            q, t = plane % packs, plane // packs
            joint = None
            for tile in range(tiles):
                low = tile * LANES
                if low + LANES <= start or low >= start + LANES:
                    continue
                moved = turn_by(planes[plane, :, pl.ds(low, LANES)], low - start)
                joint = moved if joint is None else jnp.where(lanes >= low - start, moved, joint)
            send[k, plane] = joint

    def direct(d, k):
        owner_section, owner_gx = owner(k, gy_here)
        return remote(
            send.at[k], recv.at[mine], send_sem.at[d], recv_sem.at[d],
            {"section": owner_section, "gx": owner_gx},
        )

    def handed(d, source, slot):
        return remote(source, recv.at[slot], pass_send.at[d], pass_recv.at[d], partner)

    own = pltpu.make_async_copy(send.at[spot], recv.at[mine], own_sem.at[0])

    def dispatch(k):
        d = (k - spot + regions) % regions

        @pl.when(d != 0)
        def _():
            direct(d, k).start()

        @pl.when(d == 0)
        def _():
            own.start()
            handed(0, send.at[k], mine).start()

    for k in range(regions):
        build(k)
        dispatch(k)

    def pick(table):
        return [
            jnp.where(system == 0, jnp.float32(table[a]), jnp.float32(table[b]))
            for a, b in ((0, 0), (1, 3), (2, 4))
        ]

    shifts = pick(diagonal)
    lam0, alpha, beta = shifts[0], shifts[1], pick(coupling)[1]
    shares = pick([sum(row) for row in inverse_transform])
    mixing = [pick([row[j] for row in inverse_transform]) for j in range(SECTIONS)]
    scal = (lam0, alpha, beta)
    for slot in range(2):
        for k in range(3):
            x0[slot, k, 0] = zero
            x0[slot, k, x0.shape[2] - 1] = zero
    e0[0] = zero
    def edge_handed(side, place):
        slot = (place // gx_count * 2 + system) * gx_count + place % gx_count
        return remote(
            edge_in.at[side, slot], edge_in.at[side, slot],
            edge_pass_send.at[side, place], edge_pass_recv.at[side, place], partner,
        )

    for side, (sends, _, _, comes, _, reached) in enumerate(sides):

        @pl.when(jnp.logical_and(comes, reached))
        def _():
            for place in range(regions):
                slot = (place // gx_count * 2 + system) * gx_count + place % gx_count
                remote(
                    edge.at[side], edge_in.at[side, slot], edge_send.at[side, 0],
                    edge_recv.at[side, place], partner,
                ).wait_recv()
                edge_handed(side, place).start()

    passes = [handed(0, send.at[spot], mine)]
    for d in range(1, regions):
        direct(d, (spot + d) % regions).wait()
        owner_section, owner_gx = owner((spot - d + regions) % regions, gy_here)
        slot = owner_section * gx_count + owner_gx
        copy = handed(d, recv.at[slot], slot)
        copy.start()
        passes.append(copy)
    own.wait()
    for copy in passes:
        copy.wait()
    for side, (sends, _, _, comes, _, reached) in enumerate(sides):

        @pl.when(sends)
        def _():
            for n, place in edge_places(side):
                edge_copy(side, n, place).wait_send()

        @pl.when(jnp.logical_and(comes, reached))
        def _():
            for place in range(regions):
                edge_handed(side, place).wait()

        for k in sides[side][2]:
            start = width * k - margin

            @pl.when(jnp.logical_and(comes, spot == k))
            def _():
                def patch(b, carry):
                    for plane in range(count):
                        q, t = plane % packs, plane // packs
                        if side == 0:
                            moved = turn_by(edge_in[0, b, q], -margin - start - margin * t)
                            outside = lanes < -start
                        else:
                            moved = turn_by(edge_in[1, b, q], wide - start - margin * t)
                            outside = lanes >= wide - start
                        recv[b, plane] = jnp.where(outside, moved, recv[b, plane])
                    return carry

                lax.fori_loop(0, parts, patch, 0)

    def loads(b, carry):
        kind = recv[b, 4 * block]
        currents = [zero] * SECTIONS
        for t in range(LOADS):
            here = kind == float(t)
            for j in range(SECTIONS):
                currents[j] = jnp.where(here, load_table[j, t], currents[j])
        for k in range(3):
            surf[k, b] = sum(mixing[j][k] * currents[j] for j in range(SECTIONS))
        return carry

    lax.fori_loop(0, parts, loads, 0)

    rows = parts * block
    level_of = layer_ids(layers)
    column = region * width - margin + lanes
    inside = (column >= 0) & (column < columns)
    joined = inside & (column < columns - 1) & (lanes < LANES - 1)

    def fine(b, carry):
        behind_gx, volt_behind = carry
        following = jnp.minimum(b + 1, parts - 1)
        for r in range(block):
            i = b * block + r
            volt, cap = recv[b, 4 * r], recv[b, 4 * r + 1]
            resist = jnp.where(inside, recv[b, 4 * r + 2], 0.5)
            sites = recv[b, 4 * r + 3]
            if r + 1 < block:
                volt_ahead, resist_ahead = recv[b, 4 * r + 4], recv[b, 4 * r + 6]
            else:
                volt_ahead, resist_ahead = recv[following, 0], recv[following, 2]
            resist_ahead = jnp.where(inside, resist_ahead, 0.5)
            gx = 1.0 / (resist + resist_ahead)
            if r + 1 == block:
                gx = gx * (b < parts - 1).astype(jnp.float32)
            gy = jnp.where(joined, 1.0 / (resist + left_by(resist, 1)), 0.0)
            gv = jnp.where(level_of < layers - 1, sites, 0.0)
            ground = jnp.where(level_of == 0, from_below(sites), 0.0)
            gy_low, gv_low = right_by(gy, 1), from_below(gv)
            total = (gx + behind_gx) + (gy + gy_low) + (gv + gv_low) + ground
            found = weights(cap, total, *scal)
            pulled = (gx * volt_ahead + behind_gx * volt_behind) + (
                gy * left_by(volt, 1) + gy_low * right_by(volt, 1)
            ) + (gv * from_above(volt) + gv_low * from_below(volt))
            leak = total * volt - pulled
            e0[i + 1] = gx
            for k, entry in enumerate((gy, gv, gy_low, gv_low) + found + (ground, cap)):
                g0[k + 1, i] = entry
            source = [
                jnp.where(
                    level_of == layers - 1,
                    jnp.broadcast_to(surf[k, b, r : r + 1, :], (layers, LANES)),
                    0.0,
                )
                - shares[k] * leak
                for k in range(3)
            ]
            first = solve_node(REAL, found, source[:1]) + solve_node(PAIR, found, source[1:])
            for k in range(3):
                f0[k, i] = source[k]
                x0[0, k, i + 1] = first[k]
            behind_gx, volt_behind = gx, volt
        return behind_gx, volt_behind

    lax.fori_loop(0, parts, fine, (zero, zero))
    refs = ((e0, g0, x0, f0), (e1, g1, x1, f1), (e2, g2, x2, f2))
    coarsen(0, refs, scal)
    coarsen(1, refs, scal)

    ringed = margin < BOTH_CYCLES
    ring_share = LANES // margin
    ring_groups = rows // ring_share

    def exchange(fields):
        def pack(start):
            for q in range(min(STEP, ring_groups)):
                for side, begin in ((0, width), (1, margin)):
                    for k in fields:
                        joint = zero
                        for t in range(ring_share):
                            held = x0[1, k, start + q + ring_groups * t + 1]
                            moved = turn_by(held, margin * t - begin)
                            joint = jnp.where(lanes // margin == t, moved, joint)
                        packed[side, k, start + q] = joint

        blocks(ring_groups, min(STEP, ring_groups), pack)
        span = pl.ds(fields[0], len(fields))
        copies = []
        for side, exists, came, place in (
            (0, has_after, has_before, after),
            (1, has_before, has_after, before),
        ):
            slot = 2 * (len(fields) - 1) + side
            copy = remote(
                packed.at[side, span], landed.at[side, span],
                ring_send.at[slot], ring_recv.at[slot], place,
            )
            copies.append((exists, came, copy))

            @pl.when(exists)
            def _():
                copy.start()

        return copies

    def finish(fields, copies):
        for exists, came, copy in copies:

            @pl.when(exists)
            def _():
                copy.wait_send()

            @pl.when(came)
            def _():
                copy.wait_recv()

        low_end = jnp.where(has_before, margin, 0)
        high_end = jnp.where(has_after, margin + width, LANES)

        def unpack(start):
            for q in range(min(STEP, ring_groups)):
                for k in fields:
                    low, high = landed[0, k, start + q], landed[1, k, start + q]
                    for t in range(ring_share):
                        row = start + q + ring_groups * t + 1
                        below = turn_by(low, -margin * t)
                        above = turn_by(high, margin + width - margin * t)
                        held = jnp.where(lanes < high_end, x0[1, k, row], above)
                        x0[1, k, row] = jnp.where(lanes < low_end, below, held)

        blocks(ring_groups, min(STEP, ring_groups), unpack)

    share = LANES // width
    groups = block // share
    half = max(groups // 2, 1)
    halves = groups // half
    slot_out = spot * 2 + system

    def give(fields, buf, into, sends, recvs, own):
        chosen = half if fields == REAL else groups

        def pack(b, carry):
            for n, k in enumerate(fields):
                for index in range(chosen):
                    joint = zero
                    for t in range(share):
                        row = b * block + index + groups * t + 1
                        held = x0[1, k, row]
                        if fields == REAL and halves > 1:
                            held = jnp.where(system == 0, held, x0[1, k, row + half])
                        moved = turn_by(held, width * t - margin)
                        joint = jnp.where(lanes // width == t, moved, joint)
                    buf[b, n * groups + index] = joint
            return carry

        if parts <= 8:
            for b in range(parts):
                pack(b, 0)
        else:
            lax.fori_loop(0, parts, pack, 0)
        copies = []
        for d in range(parts):
            peer = (mine + d) % parts
            if d == 0:
                copy = pltpu.make_async_copy(buf.at[peer], into.at[slot_out], own)
            else:
                copy = remote(
                    buf.at[peer], into.at[slot_out], sends.at[d], recvs.at[d], group_device(peer)
                )
            copy.start()
            copies.append(copy)
        return copies

    cycle(refs, PAIR)
    pair_ring = exchange(PAIR) if ringed else []
    cycle(refs, REAL)
    real_ring = exchange(REAL) if ringed else []
    if ringed:
        finish(PAIR, pair_ring)
    sweep(0, refs, PAIR, 1)
    cycle(refs, PAIR)
    given = give(PAIR, pair_buf, pair_in, pair_send, pair_recv, own_sem.at[1])
    if ringed:
        finish(REAL, real_ring)
    sweep(0, refs, REAL, 1)
    cycle(refs, REAL)
    given += give(REAL, real_buf, real_in, real_send, real_recv, own_sem.at[2])
    for copy in given:
        copy.wait()

    for tile in range(regions // share):
        mixed = [[None] * block for _ in range(SECTIONS)]
        for q in range(groups):
            fields = []
            for n in range(share):
                first = 2 * (tile * share + n)
                fields.append(
                    [real_in[first + q // half, q % half]]
                    + [pair_in[first, k * groups + q] for k in (0, 1)]
                    + [pair_in[first + 1, k * groups + q] for k in (0, 1)]
                )
            for s in range(SECTIONS):
                sums = [
                    sum(transform[s][k] * fields[n][k] for k in range(SECTIONS))
                    for n in range(share)
                ]
                for t in range(share):
                    joint = zero
                    for n in range(share):
                        turn = (width * (n - t)) % LANES
                        moved = right_by(sums[n], turn) if turn else sums[n]
                        joint = jnp.where(lanes // width == n, moved, joint)
                    mixed[s][q + groups * t] = joint
        place = pl.ds(tile * LANES, LANES)
        for s in range(SECTIONS):
            turned = jnp.swapaxes(jnp.stack(mixed[s]), 0, 1)
            sections[s, :, :, place] = turned
            if s == SECTIONS - 1:
                next_voltage[:, :, place] = voltage[:, :, place] + turned


def local(voltage, capacity, node_class, via_sites, ball_sites, load_type, load_table):
    layers, block, wide = voltage.shape
    gx_count = lax.axis_size("gx")
    gy_count = lax.axis_size("gy")
    parts = lax.axis_size("section") * gx_count
    regions = parts // 2
    width = wide // regions
    margin = (LANES - width) // 2
    sizes = (parts, gx_count, gy_count, width, margin, wide * gy_count)
    rows = parts * block
    count = 4 * block + 1
    packs = -(-count // (LANES // margin))

    def vmem(*shape):
        return pltpu.VMEM(shape, jnp.float32)

    def levels(extra, *lead):
        return [vmem(*lead, rows // 4**m + extra, layers, LANES) for m in range(LEVELS)]

    mid = rows * margin // LANES if margin < BOTH_CYCLES else 1
    groups = block * width // LANES
    return pl.pallas_call(
        functools.partial(kernel, sizes, radau_tables()),
        out_shape=(
            jax.ShapeDtypeStruct((SECTIONS, layers, block, wide), jnp.float32),
            jax.ShapeDtypeStruct((layers, block, wide), jnp.float32),
        ),
        in_specs=[
            *[pl.BlockSpec(memory_space=pl.ANY)] * 7,
        ],
        out_specs=(
            pl.BlockSpec(memory_space=pltpu.VMEM),
            pl.BlockSpec(memory_space=pltpu.VMEM),
        ),
        scratch_shapes=[
            pltpu.SMEM(load_table.shape[::-1], jnp.float32),
            vmem(*voltage.shape),
            vmem(*capacity.shape),
            pltpu.VMEM(node_class.shape, jnp.int32),
            pltpu.VMEM(via_sites.shape, jnp.int32),
            pltpu.VMEM(ball_sites.shape, jnp.int32),
            pltpu.VMEM(load_type.shape, jnp.int32),
            vmem(count, layers, wide),
            vmem(2, packs, layers, LANES),
            vmem(2, parts, packs, layers, LANES),
            vmem(regions, count, layers, LANES),
            vmem(parts, count, layers, LANES),
            vmem(3, parts, block, LANES),
            *levels(1),
            *levels(0, COEFFS),
            *levels(2, 2, 3),
            *levels(0, 3),
            vmem(2, 3, mid, layers, LANES),
            vmem(2, 3, mid, layers, LANES),
            *[vmem(parts, 2 * groups, layers, LANES)] * 2,
            *[vmem(parts, max(groups // 2, 1), layers, LANES)] * 2,
            pltpu.SemaphoreType.DMA((7,)),
            pltpu.SemaphoreType.DMA((2, -(-margin // width))),
            *[pltpu.SemaphoreType.DMA((2, regions))] * 3,
            pltpu.SemaphoreType.DMA((regions,)),
            pltpu.SemaphoreType.DMA((regions,)),
            pltpu.SemaphoreType.DMA((regions,)),
            pltpu.SemaphoreType.DMA((regions,)),
            pltpu.SemaphoreType.DMA((4,)),
            pltpu.SemaphoreType.DMA((4,)),
            *[pltpu.SemaphoreType.DMA((parts,))] * 4,
            pltpu.SemaphoreType.DMA((3,)),
        ],
        compiler_params=pltpu.CompilerParams(
            collective_id=0, has_side_effects=True, vmem_limit_bytes=60 * 1024 * 1024
        ),
    )(load_table.T, voltage, capacity, node_class, via_sites, ball_sites, load_type)


def solution(mesh):
    return jax.shard_map(
        local,
        mesh=mesh,
        in_specs=(
            P(None, row_axes, "gy"),
            P(None, row_axes, "gy"),
            P(None, row_axes, "gy"),
            P(None, row_axes, "gy"),
            P(row_axes, "gy"),
            P(row_axes, "gy"),
            P(),
        ),
        out_specs=(P(None, None, row_axes, "gy"), P(None, row_axes, "gy")),
        check_vma=False,
    )
```

```python
import functools
import math

import jax
import jax.numpy as jnp
from jax import lax
from jax.experimental import pallas as pl
from jax.experimental.pallas import tpu as pltpu
from jax.sharding import PartitionSpec as P

SECTIONS = 5
LEVELS = 3
LOADS = 16
LANES = 128
BOTH_CYCLES = 56
STEP = 32
REAL = (0,)
PAIR = (1, 2)
GX, GY, GV, GY_LOW, GV_LOW, W_REAL, W_SAME, W_MATE, D_REAL, D_SAME, D_MATE, GROUND, CAP, TOTAL = range(14)
COEFFS = 14

node_table = (0.35, 0.55, 0.8, 1.1, 1.5, 2.0, 2.7, 3.6)
via_conductance = 2.5
ball_conductance = 4.0
damping = 0.8
slab_partner = (0, 2, 1, 4, 3)
row_axes = ("section", "gx")


def pair_times(first, second):
    return (
        first[0] * second[0] - first[1] * second[1],
        first[0] * second[1] + first[1] * second[0],
    )


def pair_over(first, second):
    divisor = second[0] * second[0] + second[1] * second[1]
    return (
        (first[0] * second[0] + first[1] * second[1]) / divisor,
        (first[1] * second[0] - first[0] * second[1]) / divisor,
    )


def pair_minus(first, second):
    return (first[0] - second[0], first[1] - second[1])


def poly_value(coeffs, point):
    total = (0.0, 0.0)
    for c in reversed(coeffs):
        total = pair_times(total, point)
        total = (total[0] + c, total[1])
    return total


def poly_product(first, second):
    result = [0.0] * (len(first) + len(second) - 1)
    for i in range(len(first)):
        for j in range(len(second)):
            result[i + j] = result[i + j] + first[i] * second[j]
    return result


def poly_roots(coeffs):
    leading = coeffs[-1]
    scaled = [c / leading for c in coeffs]
    degree = len(coeffs) - 1
    guesses = []
    current = (1.0, 0.0)
    for k in range(degree):
        guesses.append(current)
        current = pair_times(current, (0.4, 0.9))
    for repeat_index in range(800):
        for k in range(degree):
            divisor = (1.0, 0.0)
            for j in range(degree):
                if j != k:
                    divisor = pair_times(divisor, pair_minus(guesses[k], guesses[j]))
            guesses[k] = pair_minus(guesses[k], pair_over(poly_value(scaled, guesses[k]), divisor))
    return guesses


def matrix_product(first, second):
    return [
        [
            sum((first[i][k] * second[k][j] for k in range(len(second))))
            for j in range(len(second[0]))
        ]
        for i in range(len(first))
    ]


def matrix_inverse(matrix):
    order = len(matrix)
    work = [list(matrix[i]) + [1.0 if i == j else 0.0 for j in range(order)] for i in range(order)]
    for column in range(order):
        pivot = column
        for i in range(column + 1, order):
            if abs(work[i][column]) > abs(work[pivot][column]):
                pivot = i
        work[column], work[pivot] = (work[pivot], work[column])
        factor = work[column][column]
        work[column] = [entry / factor for entry in work[column]]
        for i in range(order):
            if i != column:
                scale_row = work[i][column]
                work[i] = [work[i][j] - scale_row * work[column][j] for j in range(2 * order)]
    return [row[order:] for row in work]


def eigen_vector(matrix, value):
    order = len(matrix)
    size_inner = order - 1
    system = []
    for i in range(size_inner):
        row = []
        for j in range(order):
            entry = (matrix[i][j], 0.0)
            if i == j:
                entry = pair_minus(entry, value)
            row.append(entry)
        row[order - 1] = (-row[order - 1][0], -row[order - 1][1])
        system.append(row)
    for column in range(size_inner):
        pivot = column
        for i in range(column + 1, size_inner):
            left_size = system[i][column][0] ** 2 + system[i][column][1] ** 2
            right_size = system[pivot][column][0] ** 2 + system[pivot][column][1] ** 2
            if left_size > right_size:
                pivot = i
        system[column], system[pivot] = (system[pivot], system[column])
        for i in range(size_inner):
            if i != column:
                factor = pair_over(system[i][column], system[column][column])
                system[i] = [
                    pair_minus(system[i][j], pair_times(factor, system[column][j]))
                    for j in range(order)
                ]
    vector = [pair_over(system[i][order - 1], system[i][i]) for i in range(size_inner)]
    vector.append((1.0, 0.0))
    return vector


def radau_tables():
    section_count = 5
    generator = [1.0]
    for k in range(section_count - 1):
        generator = poly_product(generator, [0.0, 1.0])
    for k in range(section_count):
        generator = poly_product(generator, [-1.0, 1.0])
    for k in range(section_count - 1):
        generator = [j * generator[j] for j in range(1, len(generator))]
    abscissae = sorted((root[0] for root in poly_roots(generator)))
    vander = [[abscissae[i] ** j for j in range(section_count)] for i in range(section_count)]
    integrals = [
        [abscissae[i] ** (j + 1) / (j + 1) for j in range(section_count)]
        for i in range(section_count)
    ]
    butcher = matrix_product(integrals, matrix_inverse(vander))
    inverse = matrix_inverse(butcher)
    coeffs = [0.0] * (section_count + 1)
    coeffs[section_count] = 1.0
    current = [[0.0] * section_count for _ in range(section_count)]
    for k in range(1, section_count + 1):
        current = matrix_product(inverse, current)
        for i in range(section_count):
            current[i][i] = current[i][i] + coeffs[section_count - k + 1]
        applied = matrix_product(inverse, current)
        coeffs[section_count - k] = -sum((applied[i][i] for i in range(section_count))) / k
    eigen_values = poly_roots(coeffs)
    real_pick = 0
    for k in range(section_count):
        if abs(eigen_values[k][1]) < abs(eigen_values[real_pick][1]):
            real_pick = k
    upper_half = [k for k in range(section_count) if eigen_values[k][1] > 1e-09]
    upper_half = sorted(upper_half, key=lambda k: -eigen_values[k][0])
    columns = [[entry[0] for entry in eigen_vector(inverse, (eigen_values[real_pick][0], 0.0))]]
    for k in upper_half:
        vector = eigen_vector(inverse, eigen_values[k])
        columns.append([entry[0] for entry in vector])
        columns.append([entry[1] for entry in vector])
    transform = [[columns[j][i] for j in range(section_count)] for i in range(section_count)]
    inverse_transform = matrix_inverse(transform)
    blocks = matrix_product(matrix_product(inverse_transform, inverse), transform)
    diagonal = [blocks[k][k] for k in range(section_count)]
    coupling = [
        blocks[k][slab_partner[k]] if slab_partner[k] != k else 0.0 for k in range(section_count)
    ]
    return (transform, inverse_transform, diagonal, coupling)


def left_by(value, count):
    return pltpu.roll(value, LANES - count, axis=1)


def right_by(value, count):
    return pltpu.roll(value, count, axis=1)


def from_above(value):
    return pltpu.roll(value, value.shape[0] - 1, axis=0)


def from_below(value):
    return pltpu.roll(value, 1, axis=0)


def lane_ids(layers):
    return lax.broadcasted_iota(jnp.int32, (layers, LANES), 1)


def layer_ids(layers):
    return lax.broadcasted_iota(jnp.int32, (layers, LANES), 0)


def is_low(layers, stride):
    return (lane_ids(layers) // stride) % 2 == 0


def blocks(count, step, body):
    if count <= step:
        body(0)
        return

    def one(b, carry):
        body(b * step)
        return carry

    lax.fori_loop(0, count // step, one, 0)


def seam_low(level, value):
    if level == 1:
        return right_by(value, 1)
    return jnp.where(is_low(value.shape[0], 2), left_by(value, 1), right_by(value, 2))


def seam_high(level, value):
    if level == 1:
        return left_by(value, 1)
    return jnp.where(is_low(value.shape[0], 2), left_by(value, 2), right_by(value, 1))


def merge(low, stride, first, second):
    return jnp.where(low, first + left_by(first, stride), second + right_by(second, stride))


def weights(cap, total, lam0, alpha, beta):
    real = lam0 * cap + total
    mate = beta * cap
    both = alpha * cap + total
    scale = damping / (both * both + mate * mate)
    return damping / real, both * scale, mate * scale, real, both, mate


def reach(valid):
    once = -(-(valid + 2) // 2)
    twice = -(-(once + 2) // 2)
    return 2 * (2 * (twice + 3) + 2) + 2


def exchanged(margin):
    first = 0
    while reach(first + 2) <= margin:
        first += 1
    return first, reach(1)


def solve_node(fields, weight, values):
    if fields == REAL:
        return (weight[0] * values[0],)
    return (
        weight[1] * values[0] - weight[2] * values[1],
        weight[1] * values[1] + weight[2] * values[0],
    )


def sweep(level, refs, fields, source, restrict=False):
    edge, g, x, f = refs[level]
    tiles, layers = f.shape[1], f.shape[2]
    stride = 2**level
    half = tiles // 2
    step = min(STEP, half)
    target = 1 - source
    if level:
        for k in fields:
            x[source, k, 0] = seam_low(level, x[source, k, tiles])
            x[source, k, tiles + 1] = seam_high(level, x[source, k, 1])

    def part(begin):
        found = []
        xs = [[x[source, k, begin + r] for r in range(step + 2)] for k in fields]
        for r in range(step):
            i = begin + r
            ahead, behind = edge[i + 1], edge[i]
            gy, gy_low, gv, gv_low = g[GY, i], g[GY_LOW, i], g[GV, i], g[GV_LOW, i]
            here = [xs[n][r + 1] for n in range(len(fields))]
            values = []
            for n, k in enumerate(fields):
                along = ahead * xs[n][r + 2] + behind * xs[n][r]
                across = gy * left_by(here[n], stride) + gy_low * right_by(here[n], stride)
                through = gv * from_above(here[n]) + gv_low * from_below(here[n])
                values.append((f[k, i] + along) + (across + through))
            if not restrict:
                if fields == REAL:
                    weight = (g[W_REAL, i],)
                else:
                    weight = (None, g[W_SAME, i], g[W_MATE, i])
                change = solve_node(fields, weight, values)
                found.append([(1.0 - damping) * here[n] + change[n] for n in range(len(fields))])
            elif fields == REAL:
                found.append([values[0] - g[D_REAL, i] * here[0]])
            else:
                same, mate = g[D_SAME, i], g[D_MATE, i]
                found.append(
                    [
                        values[0] - same * here[0] - mate * here[1],
                        values[1] - same * here[1] + mate * here[0],
                    ]
                )
        return found

    def body(start):
        parts = [part(start), part(half + start)]
        if not restrict:
            for p in range(2):
                for r in range(step):
                    for n, k in enumerate(fields):
                        x[target, k, p * half + start + r + 1] = parts[p][r][n]
            return
        edge_next, g_next, x_next, f_next = refs[level + 1]
        low = is_low(layers, stride)
        for r in range(0, step, 2):
            i = start // 2 + r // 2
            summed = [
                merge(
                    low,
                    stride,
                    parts[0][r][n] + parts[0][r + 1][n],
                    parts[1][r][n] + parts[1][r + 1][n],
                )
                for n in range(len(fields))
            ]
            weight = [g_next[w, i] for w in (W_REAL, W_SAME, W_MATE)]
            first = solve_node(fields, weight, summed)
            for n, k in enumerate(fields):
                f_next[k, i] = summed[n]
                x_next[0, k, i + 1] = first[n]

    blocks(half, step, body)


def prolong(level, refs, fields, target):
    x, f = refs[level][2:]
    x_next, f_next = refs[level + 1][2:]
    layers = f.shape[2]
    stride = 2**level
    half = f.shape[1] // 2
    count = f_next.shape[1]
    step = min(STEP, count)

    def body(start):
        low = is_low(layers, stride)
        for r in range(step):
            for k in fields:
                coarse = x_next[1, k, start + r + 1]
                both = (
                    jnp.where(low, coarse, right_by(coarse, stride)),
                    jnp.where(low, left_by(coarse, stride), coarse),
                )
                for p in range(2):
                    for t in range(2):
                        row = p * half + 2 * (start + r) + t + 1
                        x[target, k, row] = x[target, k, row] + both[p]

    blocks(count, step, body)


def coarsen(level, refs, scal):
    edge, g = refs[level][:2]
    edge_next, g_next = refs[level + 1][:2]
    layers = g.shape[2]
    stride = 2**level
    half = g.shape[1] // 2
    count = g_next.shape[1]
    step = min(STEP, count)

    def cross(start):
        low = is_low(layers, stride)
        for r in range(step):
            j = 2 * (start + r) + 2
            edge_next[start + r + 1] = merge(low, stride, edge[j], edge[half + j])

    blocks(count, step, cross)
    first = seam_low(level + 1, edge_next[count])
    edge_next[0] = jnp.where(lane_ids(layers) % (2 * stride) == 0, 0.0, first)

    def body(start):
        low = is_low(layers, stride)
        for r in range(step):
            i = start + r
            j = 2 * i

            def summed(plane, p):
                return g[plane, p * half + j] + g[plane, p * half + j + 1]

            def joined(plane):
                return merge(low, stride, summed(plane, 0), summed(plane, 1))

            gy = jnp.where(low, left_by(summed(GY, 0), stride), summed(GY, 1))
            gv, ground, cap = joined(GV), joined(GROUND), joined(CAP)
            gy_low, gv_low = right_by(gy, 2 * stride), from_below(gv)
            total = (edge_next[i + 1] + edge_next[i]) + (gy + gy_low) + (gv + gv_low) + ground
            found = weights(cap, total, *scal)
            for k, entry in enumerate((gy, gv, gy_low, gv_low) + found + (ground, cap)):
                g_next[k + 1, i] = entry

    blocks(count, step, body)


def cycle(refs, fields):
    sweep(0, refs, fields, 0)
    sweep(0, refs, fields, 1, restrict=True)
    sweep(1, refs, fields, 0)
    sweep(1, refs, fields, 1, restrict=True)
    for n in range(3):
        sweep(2, refs, fields, n % 2)
    prolong(1, refs, fields, 1)
    sweep(1, refs, fields, 1)
    sweep(1, refs, fields, 0)
    prolong(0, refs, fields, 1)
    sweep(0, refs, fields, 1)
    sweep(0, refs, fields, 0)


def kernel(
    sizes, tables, load_table_in, voltage_in, capacity_in, node_class_in, via_sites_in,
    ball_sites_in, load_type_in, sections, next_voltage,
    load_table, voltage, capacity, node_class, via_sites, ball_sites, load_type,
    planes, edge, edge_in, send, recv, surf, e0, e1, e2, g0, g1, g2, x0, x1, x2, f0, f1, f2,
    packed, landed, pair_buf, pair_in, real_buf, real_in,
    load_sem, edge_send, edge_recv, edge_pass_send, edge_pass_recv, send_sem, recv_sem, pass_send, pass_recv,
    ring_send, ring_recv, pair_send, pair_recv, real_send, real_recv, own_sem,
):
    parts, gx_count, gy_count, width, margin, columns = sizes
    transform, inverse_transform, diagonal, coupling = tables
    layers = voltage.shape[0]
    block = voltage.shape[1]
    wide = voltage.shape[2]
    tiles = wide // LANES
    regions = parts // 2
    count = 4 * block + 1
    section_here = lax.axis_index("section")
    gx_here = lax.axis_index("gx")
    gy_here = lax.axis_index("gy")
    mine = section_here * gx_count + gx_here
    system = section_here % 2
    all_regions = regions * gy_count

    def snake(place, row):
        return place + (row % 2) * (gx_count - 1 - 2 * place)

    def turned(place, column):
        return place + (column % 2) * (regions - 1 - 2 * place)

    pair = section_here // 2
    spot = turned(pair * gx_count + snake(gx_here, pair), gy_here)
    region = gy_here * regions + spot

    def owner(place, column):
        found = turned(place, column)
        row = found // gx_count
        return row * 2 + system, snake(found % gx_count, row)

    def group_device(index):
        return {"section": index // gx_count, "gx": index % gx_count}

    def region_device(index):
        column = index // regions
        owner_section, owner_gx = owner(index % regions, column)
        return {"section": owner_section, "gx": owner_gx, "gy": column}

    after = region_device((region + 1) % all_regions)
    before = region_device((region + all_regions - 1) % all_regions)
    has_after = region < all_regions - 1
    has_before = region > 0
    seat = pair * gx_count + gx_here
    over = -(-margin // width)
    sides = (
        (gy_here < gy_count - 1, gy_here + 1, range(over), gy_here > 0, gy_here - 1, spot < over),
        (
            gy_here > 0, gy_here - 1, range(regions - over, regions),
            gy_here < gy_count - 1, gy_here + 1, spot >= regions - over,
        ),
    )
    partner = {"section": section_here + 1 - 2 * system}

    barrier = pltpu.get_barrier_semaphore()

    def greet(place):
        pl.semaphore_signal(
            barrier, inc=1, device_id=place, device_id_type=pl.DeviceIdType.MESH
        )

    for d in range(1, parts):
        greet(group_device((mine + d) % parts))
    greeted = parts - 1
    for sends, to_column, reach, comes, from_column, reached in sides:
        greeted = greeted + jnp.where(sends, over, 0)

        @pl.when(jnp.logical_and(comes, reached))
        def _():
            for place in range(regions):
                greet(
                    {
                        "section": place // gx_count * 2 + system,
                        "gx": place % gx_count,
                        "gy": from_column,
                    }
                )

    if margin < BOTH_CYCLES:
        for exists, place in ((has_after, after), (has_before, before)):
            greeted = greeted + exists.astype(jnp.int32)

            @pl.when(exists)
            def _():
                greet(place)

    fetches = []
    for n, (whole, here) in enumerate(
        (
            (node_class_in, node_class),
            (via_sites_in, via_sites),
            (ball_sites_in, ball_sites),
            (load_type_in, load_type),
            (voltage_in, voltage),
            (capacity_in, capacity),
            (load_table_in, load_table),
        )
    ):
        copy = pltpu.make_async_copy(whole, here, load_sem.at[n])
        copy.start()
        fetches.append(copy)
    for copy in fetches:
        copy.wait()

    def remote(source, target, source_sem, target_sem, place):
        return pltpu.make_async_remote_copy(
            src_ref=source,
            dst_ref=target,
            send_sem=source_sem,
            recv_sem=target_sem,
            device_id=place,
            device_id_type=pl.DeviceIdType.MESH,
        )

    lanes = lane_ids(layers)
    zero = jnp.zeros((layers, LANES), jnp.float32)

    def turn_by(value, amount):
        amount = amount % LANES
        return right_by(value, amount) if amount else value

    for tile in range(tiles):
        place = pl.ds(tile * LANES, LANES)
        kind = node_class[:, :, place]
        resist = jnp.full(kind.shape, 0.5 / node_table[0], jnp.float32)
        for k in range(1, len(node_table)):
            resist = jnp.where(kind == k, jnp.float32(0.5 / node_table[k]), resist)
        via = jnp.where(via_sites[:, :, place] == 1, jnp.float32(via_conductance), 0.0)
        ball = jnp.where(ball_sites[:, place] == 1, jnp.float32(ball_conductance), 0.0)
        sites = jnp.concatenate([via, ball[None]], axis=0)
        for k, value in enumerate((capacity[:, :, place], resist, sites, voltage[:, :, place])):
            swapped = jnp.swapaxes(value, 0, 1)
            for r in range(block):
                planes[k * block + r, :, place] = swapped[r]
        planes[4 * block, :, place] = load_type[:, place].astype(jnp.float32)

    share = LANES // margin
    lots = []
    begin = 0
    for first, size in ((0, 3 * block), (3 * block, block + 1)):
        packs = -(-size // share)
        lots.append((first, size, begin, packs))
        begin += packs

    def pack_edges(lot):
        first, size, base, packs = lots[lot]
        for side, begin in ((0, LANES - margin), (1, 0)):
            place = pl.ds((tiles - 1) * LANES if side == 0 else 0, LANES)
            for q in range(packs):
                joint = zero
                for t in range(share):
                    plane = q + packs * t
                    if plane < size:
                        moved = turn_by(planes[first + plane, :, place], margin * t - begin)
                        joint = jnp.where(lanes // margin == t, moved, joint)
                edge[side, base + q] = joint

    def edge_copy(lot, side, n, place):
        tiles_here = pl.ds(*lots[lot][2:])
        return remote(
            edge.at[side, tiles_here], edge_in.at[side, mine, tiles_here],
            edge_send.at[lot, side, n], edge_recv.at[lot, side, seat], place,
        )

    def edge_places(side):
        to_column, reach = sides[side][1:3]
        for n, k in enumerate(reach):
            owner_section, owner_gx = owner(k, to_column)
            yield n, {"section": owner_section, "gx": owner_gx, "gy": to_column}

    def send_edges(lot):
        for side in range(2):

            @pl.when(sides[side][0])
            def _():
                for n, place in edge_places(side):
                    edge_copy(lot, side, n, place).start()

    def build(lot, k):
        start = width * k - margin
        for plane in range(lots[lot][0], lots[lot][0] + lots[lot][1]):
            joint = None
            for tile in range(tiles):
                low = tile * LANES
                if low + LANES <= start or low >= start + LANES:
                    continue
                moved = turn_by(planes[plane, :, pl.ds(low, LANES)], low - start)
                joint = moved if joint is None else jnp.where(lanes >= low - start, moved, joint)
            send[k, plane] = joint

    def direct(lot, d, k):
        owner_section, owner_gx = owner(k, gy_here)
        span = pl.ds(*lots[lot][:2])
        return remote(
            send.at[k, span], recv.at[mine, span], send_sem.at[lot, d], recv_sem.at[lot, d],
            {"section": owner_section, "gx": owner_gx},
        )

    def handed(lot, d, source, slot):
        span = pl.ds(*lots[lot][:2])
        return remote(
            source.at[span], recv.at[slot, span], pass_send.at[lot, d], pass_recv.at[lot, d],
            partner,
        )

    def own(lot):
        span = pl.ds(*lots[lot][:2])
        return pltpu.make_async_copy(send.at[spot, span], recv.at[mine, span], own_sem.at[lot])

    def dispatch(lot, k):
        d = (k - spot + regions) % regions

        @pl.when(d != 0)
        def _():
            direct(lot, d, k).start()

        @pl.when(d == 0)
        def _():
            own(lot).start()
            handed(lot, 0, send.at[k], mine).start()

    ends = [k for k in range(regions) if k < over or k >= regions - over]
    order = ends + [k for k in range(regions) if k not in ends]
    pack_edges(0)
    build(0, order[0])
    pl.semaphore_wait(barrier, greeted)
    send_edges(0)
    dispatch(0, order[0])
    for k in order[1:]:
        build(0, k)
        dispatch(0, k)
    pack_edges(1)
    send_edges(1)
    for k in order:
        build(1, k)
        dispatch(1, k)

    def pick(table):
        return [
            jnp.where(system == 0, jnp.float32(table[a]), jnp.float32(table[b]))
            for a, b in ((0, 0), (1, 3), (2, 4))
        ]

    shifts = pick(diagonal)
    lam0, alpha, beta = shifts[0], shifts[1], pick(coupling)[1]
    shares = pick([sum(row) for row in inverse_transform])
    mixing = [pick([row[j] for row in inverse_transform]) for j in range(SECTIONS)]
    scal = (lam0, alpha, beta)
    for slot in range(2):
        for k in range(3):
            x0[slot, k, 0] = zero
            x0[slot, k, x0.shape[2] - 1] = zero
    e0[0] = zero

    def edge_slot(place):
        return (place // gx_count * 2 + system) * gx_count + place % gx_count

    def edge_handed(lot, side, place):
        landing = edge_in.at[side, edge_slot(place), pl.ds(*lots[lot][2:])]
        return remote(
            landing, landing, edge_pass_send.at[lot, side, place],
            edge_pass_recv.at[lot, side, place], partner,
        )

    def take(lot):
        for side, (sends, _, _, comes, _, reached) in enumerate(sides):

            @pl.when(jnp.logical_and(comes, reached))
            def _():
                tiles_here = pl.ds(*lots[lot][2:])
                for place in range(regions):
                    remote(
                        edge.at[side, tiles_here], edge_in.at[side, edge_slot(place), tiles_here],
                        edge_send.at[lot, side, 0], edge_recv.at[lot, side, place], partner,
                    ).wait_recv()
                    edge_handed(lot, side, place).start()

        passes = [handed(lot, 0, send.at[spot], mine)]
        for d in range(1, regions):
            direct(lot, d, (spot + d) % regions).wait()
            owner_section, owner_gx = owner((spot - d + regions) % regions, gy_here)
            slot = owner_section * gx_count + owner_gx
            copy = handed(lot, d, recv.at[slot], slot)
            copy.start()
            passes.append(copy)
        return passes

    def settle(lot, passes):
        first, size, base, packs = lots[lot]
        own(lot).wait()
        for copy in passes:
            copy.wait()
        for side, (sends, _, _, comes, _, reached) in enumerate(sides):

            @pl.when(sends)
            def _():
                for n, place in edge_places(side):
                    edge_copy(lot, side, n, place).wait_send()

            @pl.when(jnp.logical_and(comes, reached))
            def _():
                for place in range(regions):
                    edge_handed(lot, side, place).wait()

            for k in sides[side][2]:
                start = width * k - margin

                @pl.when(jnp.logical_and(comes, spot == k))
                def _():
                    def patch(c, carry):
                        for b in (4 * c, 4 * c + 1, 4 * c + 2, 4 * c + 3):
                            for plane in range(size):
                                q, t = plane % packs, plane // packs
                                low = -margin if side == 0 else wide
                                moved = turn_by(edge_in[side, b, base + q], low - start - margin * t)
                                if side == 0:
                                    outside = lanes < -start
                                else:
                                    outside = lanes >= wide - start
                                held = recv[b, first + plane]
                                recv[b, first + plane] = jnp.where(outside, moved, held)
                        return carry

                    lax.fori_loop(0, parts // 4, patch, 0)

    rows = parts * block
    level_of = layer_ids(layers)
    column = region * width - margin + lanes
    inside = (column >= 0) & (column < columns)
    joined = inside & (column < columns - 1) & (lanes < LANES - 1)

    def coefficients(c, behind_gx):
        for b in (2 * c, 2 * c + 1):
            following = jnp.minimum(b + 1, parts - 1)
            for r in range(block):
                i = b * block + r
                cap, sites = recv[b, r], recv[b, 2 * block + r]
                resist = jnp.where(inside, recv[b, block + r], 0.5)
                if r + 1 < block:
                    resist_ahead = recv[b, block + r + 1]
                else:
                    resist_ahead = recv[following, block]
                resist_ahead = jnp.where(inside, resist_ahead, 0.5)
                gx = 1.0 / (resist + resist_ahead)
                if r + 1 == block:
                    gx = gx * (b < parts - 1).astype(jnp.float32)
                gy = jnp.where(joined, 1.0 / (resist + left_by(resist, 1)), 0.0)
                gv = jnp.where(level_of < layers - 1, sites, 0.0)
                ground = jnp.where(level_of == 0, from_below(sites), 0.0)
                gy_low, gv_low = right_by(gy, 1), from_below(gv)
                total = (gx + behind_gx) + (gy + gy_low) + (gv + gv_low) + ground
                found = weights(cap, total, *scal)
                e0[i + 1] = gx
                for k, entry in enumerate((gy, gv, gy_low, gv_low) + found + (ground, cap, total)):
                    g0[k + 1, i] = entry
                behind_gx = gx
        return behind_gx

    def forcing(c, volt_behind):
        for b in (2 * c, 2 * c + 1):
            kind = recv[b, 4 * block]
            currents = [zero] * SECTIONS
            for t in range(LOADS):
                here = kind == float(t)
                for j in range(SECTIONS):
                    currents[j] = jnp.where(here, load_table[j, t], currents[j])
            for k in range(3):
                surf[k, b] = sum(mixing[j][k] * currents[j] for j in range(SECTIONS))
        for b in (2 * c, 2 * c + 1):
            following = jnp.minimum(b + 1, parts - 1)
            for r in range(block):
                i = b * block + r
                volt = recv[b, 3 * block + r]
                if r + 1 < block:
                    volt_ahead = recv[b, 3 * block + r + 1]
                else:
                    volt_ahead = recv[following, 3 * block]
                pulled = (
                    (e0[i + 1] * volt_ahead + e0[i] * volt_behind)
                    + (g0[GY, i] * left_by(volt, 1) + g0[GY_LOW, i] * right_by(volt, 1))
                    + (g0[GV, i] * from_above(volt) + g0[GV_LOW, i] * from_below(volt))
                )
                leak = g0[TOTAL, i] * volt - pulled
                source = [
                    jnp.where(
                        level_of == layers - 1,
                        jnp.broadcast_to(surf[k, b, r : r + 1, :], (layers, LANES)),
                        0.0,
                    )
                    - shares[k] * leak
                    for k in range(3)
                ]
                found = [g0[w, i] for w in (W_REAL, W_SAME, W_MATE)]
                first = solve_node(REAL, found, source[:1]) + solve_node(PAIR, found, source[1:])
                for k in range(3):
                    f0[k, i] = source[k]
                    x0[0, k, i + 1] = first[k]
                volt_behind = volt
        return volt_behind

    settle(0, take(0))
    behind = lax.fori_loop(0, parts // 4, coefficients, zero)
    second = take(1)
    lax.fori_loop(parts // 4, parts // 2, coefficients, behind)
    refs = ((e0, g0, x0, f0), (e1, g1, x1, f1), (e2, g2, x2, f2))
    coarsen(0, refs, scal)
    coarsen(1, refs, scal)
    settle(1, second)
    lax.fori_loop(0, parts // 2, forcing, zero)

    ringed = margin < BOTH_CYCLES
    first_sent, last_sent = exchanged(margin) if ringed else (0, margin)
    sent = last_sent - first_sent
    ring_share = LANES // sent
    ring_groups = -(-rows // ring_share)

    def ring_copies(fields):
        span = pl.ds(fields[0], len(fields))
        for side, exists, came, place in (
            (0, has_after, has_before, after),
            (1, has_before, has_after, before),
        ):
            slot = 2 * (len(fields) - 1) + side
            yield exists, came, remote(
                packed.at[side, span], landed.at[side, span],
                ring_send.at[slot], ring_recv.at[slot], place,
            )

    def exchange(fields):
        for q in range(ring_groups):
            for side, begin in ((0, width + first_sent), (1, LANES - width - last_sent)):
                for k in fields:
                    joint = None
                    for t in range(ring_share):
                        row = q + ring_groups * t
                        if row < rows:
                            moved = turn_by(x0[1, k, row + 1], sent * t - begin)
                            joint = moved if t == 0 else jnp.where(lanes >= sent * t, moved, joint)
                    packed[side, k, q] = joint
        for exists, came, copy in ring_copies(fields):

            @pl.when(exists)
            def _():
                copy.start()

    def finish(fields):
        for exists, came, copy in ring_copies(fields):

            @pl.when(exists)
            def _():
                copy.wait_send()

            @pl.when(came)
            def _():
                copy.wait_recv()

        low = (lanes >= first_sent) & (lanes < jnp.where(has_before, last_sent, 0))
        high = (lanes < LANES - first_sent) & (
            lanes >= jnp.where(has_after, LANES - last_sent, LANES)
        )
        for q in range(ring_groups):
            for k in fields:
                from_low, from_high = landed[0, k, q], landed[1, k, q]
                for t in range(ring_share):
                    row = q + ring_groups * t
                    if row < rows:
                        below = turn_by(from_low, first_sent - sent * t)
                        above = turn_by(from_high, LANES - last_sent - sent * t)
                        held = jnp.where(high, above, x0[1, k, row + 1])
                        x0[1, k, row + 1] = jnp.where(low, below, held)

    share = LANES // width
    groups = block // share
    half = max(groups // 2, 1)
    halves = groups // half
    slot_out = spot * 2 + system

    def gifts(fields, buf, into, sends, recvs, own):
        for d in range(parts):
            peer = (mine + d) % parts
            if d == 0:
                yield pltpu.make_async_copy(buf.at[peer], into.at[slot_out], own)
            else:
                yield remote(
                    buf.at[peer], into.at[slot_out], sends.at[d], recvs.at[d], group_device(peer)
                )

    def give(fields, buf, *rest):
        chosen = half if fields == REAL else groups

        def pack(b, carry):
            for n, k in enumerate(fields):
                for index in range(chosen):
                    joint = zero
                    for t in range(share):
                        row = b * block + index + groups * t + 1
                        held = x0[1, k, row]
                        if fields == REAL and halves > 1:
                            held = jnp.where(system == 0, held, x0[1, k, row + half])
                        moved = turn_by(held, width * t - margin)
                        joint = jnp.where(lanes // width == t, moved, joint)
                    buf[b, n * groups + index] = joint
            return carry

        if parts <= 8:
            for b in range(parts):
                pack(b, 0)
        else:
            lax.fori_loop(0, parts, pack, 0)
        for copy in gifts(fields, buf, *rest):
            copy.start()

    outputs = (
        (PAIR, pair_buf, pair_in, pair_send, pair_recv, own_sem.at[2]),
        (REAL, real_buf, real_in, real_send, real_recv, own_sem.at[3]),
    )

    def both(step, carry):
        for output in outputs:
            fields = output[0]

            @pl.when(step > 0)
            def _():
                if ringed:
                    finish(fields)
                sweep(0, refs, fields, 1)

            cycle(refs, fields)

            @pl.when(step == 0)
            def _():
                if ringed:
                    exchange(fields)

            @pl.when(step > 0)
            def _():
                give(*output)

        return carry

    lax.fori_loop(0, 2, both, 0)
    for output in outputs:
        for copy in gifts(*output):
            copy.wait()

    for tile in range(regions // share):
        mixed = [[None] * block for _ in range(SECTIONS)]
        for q in range(groups):
            fields = []
            for n in range(share):
                first = 2 * (tile * share + n)
                fields.append(
                    [real_in[first + q // half, q % half]]
                    + [pair_in[first, k * groups + q] for k in (0, 1)]
                    + [pair_in[first + 1, k * groups + q] for k in (0, 1)]
                )
            for s in range(SECTIONS):
                sums = [
                    sum(transform[s][k] * fields[n][k] for k in range(SECTIONS))
                    for n in range(share)
                ]
                for t in range(share):
                    joint = zero
                    for n in range(share):
                        turn = (width * (n - t)) % LANES
                        moved = right_by(sums[n], turn) if turn else sums[n]
                        joint = jnp.where(lanes // width == n, moved, joint)
                    mixed[s][q + groups * t] = joint
        place = pl.ds(tile * LANES, LANES)
        for s in range(SECTIONS):
            turned = jnp.swapaxes(jnp.stack(mixed[s]), 0, 1)
            sections[s, :, :, place] = turned
            if s == SECTIONS - 1:
                next_voltage[:, :, place] = voltage[:, :, place] + turned


def local(voltage, capacity, node_class, via_sites, ball_sites, load_type, load_table):
    layers, block, wide = voltage.shape
    gx_count = lax.axis_size("gx")
    gy_count = lax.axis_size("gy")
    parts = lax.axis_size("section") * gx_count
    regions = parts // 2
    width = wide // regions
    margin = (LANES - width) // 2
    sizes = (parts, gx_count, gy_count, width, margin, wide * gy_count)
    rows = parts * block
    count = 4 * block + 1
    per_tile = LANES // margin
    packs = -(-3 * block // per_tile) - (-(block + 1) // per_tile)

    def vmem(*shape):
        return pltpu.VMEM(shape, jnp.float32)

    def levels(extra, *lead):
        return [vmem(*lead, rows // 4**m + extra, layers, LANES) for m in range(LEVELS)]

    mid = 1
    if margin < BOTH_CYCLES:
        first_sent, last_sent = exchanged(margin)
        mid = -(-rows // (LANES // (last_sent - first_sent)))
    groups = block * width // LANES
    scratch = [
        pltpu.SMEM(load_table.shape[::-1], jnp.float32),
        vmem(*voltage.shape),
        vmem(*capacity.shape),
        pltpu.VMEM(node_class.shape, jnp.int32),
        pltpu.VMEM(via_sites.shape, jnp.int32),
        pltpu.VMEM(ball_sites.shape, jnp.int32),
        pltpu.VMEM(load_type.shape, jnp.int32),
        vmem(count, layers, wide),
        vmem(2, packs, layers, LANES),
        vmem(2, parts, packs, layers, LANES),
        vmem(regions, count, layers, LANES),
        vmem(parts, count, layers, LANES),
        vmem(3, parts, block, LANES),
        *levels(1),
        *levels(0, COEFFS),
        *levels(2, 2, 3),
        *levels(0, 3),
        vmem(2, 3, mid, layers, LANES),
        vmem(2, 3, mid, layers, LANES),
        *[vmem(parts, 2 * groups, layers, LANES)] * 2,
        *[vmem(parts, max(groups // 2, 1), layers, LANES)] * 2,
        pltpu.SemaphoreType.DMA((7,)),
        pltpu.SemaphoreType.DMA((2, 2, -(-margin // width))),
        *[pltpu.SemaphoreType.DMA((2, 2, regions))] * 3,
        *[pltpu.SemaphoreType.DMA((2, regions))] * 4,
        pltpu.SemaphoreType.DMA((4,)),
        pltpu.SemaphoreType.DMA((4,)),
        *[pltpu.SemaphoreType.DMA((parts,))] * 4,
        pltpu.SemaphoreType.DMA((4,)),
    ]
    grant = 4 * 1024 * 1024
    for part in scratch:
        if "vmem" in str(part.memory_space).lower():
            grant += 4 * math.prod(part.shape)
    arguments = (load_table.T, voltage, capacity, node_class, via_sites, ball_sites, load_type)
    return pl.pallas_call(
        functools.partial(kernel, sizes, radau_tables()),
        out_shape=(
            jax.ShapeDtypeStruct((SECTIONS, layers, block, wide), jnp.float32),
            jax.ShapeDtypeStruct((layers, block, wide), jnp.float32),
        ),
        in_specs=[
            *[pl.BlockSpec(memory_space=pl.ANY)] * 7,
        ],
        out_specs=(
            pl.BlockSpec(memory_space=pltpu.VMEM),
            pl.BlockSpec(memory_space=pltpu.VMEM),
        ),
        scratch_shapes=scratch,
        compiler_params=pltpu.CompilerParams(
            collective_id=0, has_side_effects=True, vmem_limit_bytes=grant
        ),
    )(*[pltpu.with_memory_space_constraint(a, pltpu.MemorySpace.HBM) for a in arguments])


def solution(mesh):
    return jax.shard_map(
        local,
        mesh=mesh,
        in_specs=(
            P(None, row_axes, "gy"),
            P(None, row_axes, "gy"),
            P(None, row_axes, "gy"),
            P(None, row_axes, "gy"),
            P(row_axes, "gy"),
            P(row_axes, "gy"),
            P(),
        ),
        out_specs=(P(None, None, row_axes, "gy"), P(None, row_axes, "gy")),
        check_vma=False,
    )
```

```python
import functools
import math

import jax
import jax.numpy as jnp
from jax import lax
from jax.experimental import pallas as pl
from jax.experimental.pallas import tpu as pltpu
from jax.sharding import PartitionSpec as P

SECTIONS = 5
LEVELS = 3
LOADS = 16
LANES = 128
BOTH_CYCLES = 56
STEP = 32
REAL = (0,)
PAIR = (1, 2)
GX, GY, GV, GY_LOW, GV_LOW, W_REAL, W_SAME, W_MATE, D_REAL, D_SAME, D_MATE, GROUND, CAP, TOTAL = range(14)
COEFFS = 14

node_table = (0.35, 0.55, 0.8, 1.1, 1.5, 2.0, 2.7, 3.6)
via_conductance = 2.5
ball_conductance = 4.0
damping = 0.8
slab_partner = (0, 2, 1, 4, 3)
row_axes = ("section", "gx")


def pair_times(first, second):
    return (
        first[0] * second[0] - first[1] * second[1],
        first[0] * second[1] + first[1] * second[0],
    )


def pair_over(first, second):
    divisor = second[0] * second[0] + second[1] * second[1]
    return (
        (first[0] * second[0] + first[1] * second[1]) / divisor,
        (first[1] * second[0] - first[0] * second[1]) / divisor,
    )


def pair_minus(first, second):
    return (first[0] - second[0], first[1] - second[1])


def poly_value(coeffs, point):
    total = (0.0, 0.0)
    for c in reversed(coeffs):
        total = pair_times(total, point)
        total = (total[0] + c, total[1])
    return total


def poly_product(first, second):
    result = [0.0] * (len(first) + len(second) - 1)
    for i in range(len(first)):
        for j in range(len(second)):
            result[i + j] = result[i + j] + first[i] * second[j]
    return result


def poly_roots(coeffs):
    leading = coeffs[-1]
    scaled = [c / leading for c in coeffs]
    degree = len(coeffs) - 1
    guesses = []
    current = (1.0, 0.0)
    for k in range(degree):
        guesses.append(current)
        current = pair_times(current, (0.4, 0.9))
    for repeat_index in range(800):
        for k in range(degree):
            divisor = (1.0, 0.0)
            for j in range(degree):
                if j != k:
                    divisor = pair_times(divisor, pair_minus(guesses[k], guesses[j]))
            guesses[k] = pair_minus(guesses[k], pair_over(poly_value(scaled, guesses[k]), divisor))
    return guesses


def matrix_product(first, second):
    return [
        [
            sum((first[i][k] * second[k][j] for k in range(len(second))))
            for j in range(len(second[0]))
        ]
        for i in range(len(first))
    ]


def matrix_inverse(matrix):
    order = len(matrix)
    work = [list(matrix[i]) + [1.0 if i == j else 0.0 for j in range(order)] for i in range(order)]
    for column in range(order):
        pivot = column
        for i in range(column + 1, order):
            if abs(work[i][column]) > abs(work[pivot][column]):
                pivot = i
        work[column], work[pivot] = (work[pivot], work[column])
        factor = work[column][column]
        work[column] = [entry / factor for entry in work[column]]
        for i in range(order):
            if i != column:
                scale_row = work[i][column]
                work[i] = [work[i][j] - scale_row * work[column][j] for j in range(2 * order)]
    return [row[order:] for row in work]


def eigen_vector(matrix, value):
    order = len(matrix)
    size_inner = order - 1
    system = []
    for i in range(size_inner):
        row = []
        for j in range(order):
            entry = (matrix[i][j], 0.0)
            if i == j:
                entry = pair_minus(entry, value)
            row.append(entry)
        row[order - 1] = (-row[order - 1][0], -row[order - 1][1])
        system.append(row)
    for column in range(size_inner):
        pivot = column
        for i in range(column + 1, size_inner):
            left_size = system[i][column][0] ** 2 + system[i][column][1] ** 2
            right_size = system[pivot][column][0] ** 2 + system[pivot][column][1] ** 2
            if left_size > right_size:
                pivot = i
        system[column], system[pivot] = (system[pivot], system[column])
        for i in range(size_inner):
            if i != column:
                factor = pair_over(system[i][column], system[column][column])
                system[i] = [
                    pair_minus(system[i][j], pair_times(factor, system[column][j]))
                    for j in range(order)
                ]
    vector = [pair_over(system[i][order - 1], system[i][i]) for i in range(size_inner)]
    vector.append((1.0, 0.0))
    return vector


def radau_tables():
    section_count = 5
    generator = [1.0]
    for k in range(section_count - 1):
        generator = poly_product(generator, [0.0, 1.0])
    for k in range(section_count):
        generator = poly_product(generator, [-1.0, 1.0])
    for k in range(section_count - 1):
        generator = [j * generator[j] for j in range(1, len(generator))]
    abscissae = sorted((root[0] for root in poly_roots(generator)))
    vander = [[abscissae[i] ** j for j in range(section_count)] for i in range(section_count)]
    integrals = [
        [abscissae[i] ** (j + 1) / (j + 1) for j in range(section_count)]
        for i in range(section_count)
    ]
    butcher = matrix_product(integrals, matrix_inverse(vander))
    inverse = matrix_inverse(butcher)
    coeffs = [0.0] * (section_count + 1)
    coeffs[section_count] = 1.0
    current = [[0.0] * section_count for _ in range(section_count)]
    for k in range(1, section_count + 1):
        current = matrix_product(inverse, current)
        for i in range(section_count):
            current[i][i] = current[i][i] + coeffs[section_count - k + 1]
        applied = matrix_product(inverse, current)
        coeffs[section_count - k] = -sum((applied[i][i] for i in range(section_count))) / k
    eigen_values = poly_roots(coeffs)
    real_pick = 0
    for k in range(section_count):
        if abs(eigen_values[k][1]) < abs(eigen_values[real_pick][1]):
            real_pick = k
    upper_half = [k for k in range(section_count) if eigen_values[k][1] > 1e-09]
    upper_half = sorted(upper_half, key=lambda k: -eigen_values[k][0])
    columns = [[entry[0] for entry in eigen_vector(inverse, (eigen_values[real_pick][0], 0.0))]]
    for k in upper_half:
        vector = eigen_vector(inverse, eigen_values[k])
        columns.append([entry[0] for entry in vector])
        columns.append([entry[1] for entry in vector])
    transform = [[columns[j][i] for j in range(section_count)] for i in range(section_count)]
    inverse_transform = matrix_inverse(transform)
    blocks = matrix_product(matrix_product(inverse_transform, inverse), transform)
    diagonal = [blocks[k][k] for k in range(section_count)]
    coupling = [
        blocks[k][slab_partner[k]] if slab_partner[k] != k else 0.0 for k in range(section_count)
    ]
    return (transform, inverse_transform, diagonal, coupling)


def left_by(value, count):
    return pltpu.roll(value, LANES - count, axis=1)


def right_by(value, count):
    return pltpu.roll(value, count, axis=1)


def from_above(value):
    return pltpu.roll(value, value.shape[0] - 1, axis=0)


def from_below(value):
    return pltpu.roll(value, 1, axis=0)


def lane_ids(layers):
    return lax.broadcasted_iota(jnp.int32, (layers, LANES), 1)


def layer_ids(layers):
    return lax.broadcasted_iota(jnp.int32, (layers, LANES), 0)


def is_low(layers, stride):
    return (lane_ids(layers) // stride) % 2 == 0


def blocks(count, step, body):
    if count <= step:
        body(0)
        return

    def one(b, carry):
        body(b * step)
        return carry

    lax.fori_loop(0, count // step, one, 0)


def seam_low(level, value):
    if level == 1:
        return right_by(value, 1)
    return jnp.where(is_low(value.shape[0], 2), left_by(value, 1), right_by(value, 2))


def seam_high(level, value):
    if level == 1:
        return left_by(value, 1)
    return jnp.where(is_low(value.shape[0], 2), left_by(value, 2), right_by(value, 1))


def merge(low, stride, first, second):
    return jnp.where(low, first + left_by(first, stride), second + right_by(second, stride))


def weights(cap, total, lam0, alpha, beta):
    real = lam0 * cap + total
    mate = beta * cap
    both = alpha * cap + total
    scale = damping / (both * both + mate * mate)
    return damping / real, both * scale, mate * scale, real, both, mate


def reach(valid):
    once = -(-(valid + 2) // 2)
    twice = -(-(once + 2) // 2)
    return 2 * (2 * (twice + 3) + 2) + 2


def exchanged(margin):
    first = 0
    while reach(first + 2) <= margin:
        first += 1
    return first, reach(1)


def solve_node(fields, weight, values):
    if fields == REAL:
        return (weight[0] * values[0],)
    return (
        weight[1] * values[0] - weight[2] * values[1],
        weight[1] * values[1] + weight[2] * values[0],
    )


def sweep(level, refs, fields, source, restrict=False):
    edge, g, x, f = refs[level]
    tiles, layers = f.shape[1], f.shape[2]
    stride = 2**level
    half = tiles // 2
    step = min(STEP, half)
    target = 1 - source
    if level:
        for k in fields:
            x[source, k, 0] = seam_low(level, x[source, k, tiles])
            x[source, k, tiles + 1] = seam_high(level, x[source, k, 1])

    def part(begin):
        found = []
        xs = [[x[source, k, begin + r] for r in range(step + 2)] for k in fields]
        for r in range(step):
            i = begin + r
            ahead, behind = edge[i + 1], edge[i]
            gy, gy_low, gv, gv_low = g[GY, i], g[GY_LOW, i], g[GV, i], g[GV_LOW, i]
            here = [xs[n][r + 1] for n in range(len(fields))]
            values = []
            for n, k in enumerate(fields):
                along = ahead * xs[n][r + 2] + behind * xs[n][r]
                across = gy * left_by(here[n], stride) + gy_low * right_by(here[n], stride)
                through = gv * from_above(here[n]) + gv_low * from_below(here[n])
                values.append((f[k, i] + along) + (across + through))
            if not restrict:
                if fields == REAL:
                    weight = (g[W_REAL, i],)
                else:
                    weight = (None, g[W_SAME, i], g[W_MATE, i])
                change = solve_node(fields, weight, values)
                found.append([(1.0 - damping) * here[n] + change[n] for n in range(len(fields))])
            elif fields == REAL:
                found.append([values[0] - g[D_REAL, i] * here[0]])
            else:
                same, mate = g[D_SAME, i], g[D_MATE, i]
                found.append(
                    [
                        values[0] - same * here[0] - mate * here[1],
                        values[1] - same * here[1] + mate * here[0],
                    ]
                )
        return found

    def body(start):
        parts = [part(start), part(half + start)]
        if not restrict:
            for p in range(2):
                for r in range(step):
                    for n, k in enumerate(fields):
                        x[target, k, p * half + start + r + 1] = parts[p][r][n]
            return
        edge_next, g_next, x_next, f_next = refs[level + 1]
        low = is_low(layers, stride)
        for r in range(0, step, 2):
            i = start // 2 + r // 2
            summed = [
                merge(
                    low,
                    stride,
                    parts[0][r][n] + parts[0][r + 1][n],
                    parts[1][r][n] + parts[1][r + 1][n],
                )
                for n in range(len(fields))
            ]
            weight = [g_next[w, i] for w in (W_REAL, W_SAME, W_MATE)]
            first = solve_node(fields, weight, summed)
            for n, k in enumerate(fields):
                f_next[k, i] = summed[n]
                x_next[0, k, i + 1] = first[n]

    blocks(half, step, body)


def prolong(level, refs, fields, target):
    x, f = refs[level][2:]
    x_next, f_next = refs[level + 1][2:]
    layers = f.shape[2]
    stride = 2**level
    half = f.shape[1] // 2
    count = f_next.shape[1]
    step = min(STEP, count)

    def body(start):
        low = is_low(layers, stride)
        for r in range(step):
            for k in fields:
                coarse = x_next[1, k, start + r + 1]
                both = (
                    jnp.where(low, coarse, right_by(coarse, stride)),
                    jnp.where(low, left_by(coarse, stride), coarse),
                )
                for p in range(2):
                    for t in range(2):
                        row = p * half + 2 * (start + r) + t + 1
                        x[target, k, row] = x[target, k, row] + both[p]

    blocks(count, step, body)


def coarsen(level, refs, scal):
    edge, g = refs[level][:2]
    edge_next, g_next = refs[level + 1][:2]
    layers = g.shape[2]
    stride = 2**level
    half = g.shape[1] // 2
    count = g_next.shape[1]
    step = min(STEP, count)

    def cross(start):
        low = is_low(layers, stride)
        for r in range(step):
            j = 2 * (start + r) + 2
            edge_next[start + r + 1] = merge(low, stride, edge[j], edge[half + j])

    blocks(count, step, cross)
    first = seam_low(level + 1, edge_next[count])
    edge_next[0] = jnp.where(lane_ids(layers) % (2 * stride) == 0, 0.0, first)

    def body(start):
        low = is_low(layers, stride)
        for r in range(step):
            i = start + r
            j = 2 * i

            def summed(plane, p):
                return g[plane, p * half + j] + g[plane, p * half + j + 1]

            def joined(plane):
                return merge(low, stride, summed(plane, 0), summed(plane, 1))

            gy = jnp.where(low, left_by(summed(GY, 0), stride), summed(GY, 1))
            gv, ground, cap = joined(GV), joined(GROUND), joined(CAP)
            gy_low, gv_low = right_by(gy, 2 * stride), from_below(gv)
            total = (edge_next[i + 1] + edge_next[i]) + (gy + gy_low) + (gv + gv_low) + ground
            found = weights(cap, total, *scal)
            for k, entry in enumerate((gy, gv, gy_low, gv_low) + found + (ground, cap)):
                g_next[k + 1, i] = entry

    blocks(count, step, body)


def cycle(refs, fields):
    sweep(0, refs, fields, 0)
    sweep(0, refs, fields, 1, restrict=True)
    sweep(1, refs, fields, 0)
    sweep(1, refs, fields, 1, restrict=True)
    for n in range(3):
        sweep(2, refs, fields, n % 2)
    prolong(1, refs, fields, 1)
    sweep(1, refs, fields, 1)
    sweep(1, refs, fields, 0)
    prolong(0, refs, fields, 1)
    sweep(0, refs, fields, 1)
    sweep(0, refs, fields, 0)


def kernel(
    sizes, tables, load_table_in, voltage_in, capacity_in, node_class_in, via_sites_in,
    ball_sites_in, load_type_in, sections, next_voltage,
    load_table, voltage, capacity, node_class, via_sites, ball_sites, load_type,
    planes, edge, edge_in, send, recv, surf, e0, e1, e2, g0, g1, g2, x0, x1, x2, f0, f1, f2,
    packed, landed, pair_buf, pair_in, real_buf, real_in,
    load_sem, edge_send, edge_recv, edge_pass_send, edge_pass_recv, send_sem, recv_sem, pass_send, pass_recv,
    ring_send, ring_recv, pair_send, pair_recv, real_send, real_recv, own_sem,
):
    parts, gx_count, gy_count, width, margin, columns = sizes
    transform, inverse_transform, diagonal, coupling = tables
    layers = voltage.shape[0]
    block = voltage.shape[1]
    wide = voltage.shape[2]
    tiles = wide // LANES
    regions = parts // 2
    count = 4 * block + 1
    section_here = lax.axis_index("section")
    gx_here = lax.axis_index("gx")
    gy_here = lax.axis_index("gy")
    mine = section_here * gx_count + gx_here
    system = section_here % 2
    all_regions = regions * gy_count

    def snake(place, row):
        return place + (row % 2) * (gx_count - 1 - 2 * place)

    def turned(place, column):
        return place + (column % 2) * (regions - 1 - 2 * place)

    pair = section_here // 2
    spot = turned(pair * gx_count + snake(gx_here, pair), gy_here)
    region = gy_here * regions + spot

    def owner(place, column):
        found = turned(place, column)
        row = found // gx_count
        return row * 2 + system, snake(found % gx_count, row)

    def group_device(index):
        return {"section": index // gx_count, "gx": index % gx_count}

    def region_device(index):
        column = index // regions
        owner_section, owner_gx = owner(index % regions, column)
        return {"section": owner_section, "gx": owner_gx, "gy": column}

    after = region_device((region + 1) % all_regions)
    before = region_device((region + all_regions - 1) % all_regions)
    has_after = region < all_regions - 1
    has_before = region > 0
    seat = pair * gx_count + gx_here
    over = -(-margin // width)
    sides = (
        (gy_here < gy_count - 1, gy_here + 1, range(over), gy_here > 0, gy_here - 1, spot < over),
        (
            gy_here > 0, gy_here - 1, range(regions - over, regions),
            gy_here < gy_count - 1, gy_here + 1, spot >= regions - over,
        ),
    )
    partner = {"section": section_here + 1 - 2 * system}

    barrier = pltpu.get_barrier_semaphore()

    def greet(place):
        pl.semaphore_signal(
            barrier, inc=1, device_id=place, device_id_type=pl.DeviceIdType.MESH
        )

    for d in range(1, parts):
        greet(group_device((mine + d) % parts))
    greeted = parts - 1
    for sends, to_column, reach, comes, from_column, reached in sides:
        greeted = greeted + jnp.where(sends, over, 0)

        @pl.when(jnp.logical_and(comes, reached))
        def _():
            for place in range(regions):
                greet(
                    {
                        "section": place // gx_count * 2 + system,
                        "gx": place % gx_count,
                        "gy": from_column,
                    }
                )

    if margin < BOTH_CYCLES:
        for exists, place in ((has_after, after), (has_before, before)):
            greeted = greeted + exists.astype(jnp.int32)

            @pl.when(exists)
            def _():
                greet(place)

    fetches = []
    for n, (whole, here) in enumerate(
        (
            (node_class_in, node_class),
            (via_sites_in, via_sites),
            (ball_sites_in, ball_sites),
            (load_type_in, load_type),
            (voltage_in, voltage),
            (capacity_in, capacity),
            (load_table_in, load_table),
        )
    ):
        copy = pltpu.make_async_copy(whole, here, load_sem.at[n])
        copy.start()
        fetches.append(copy)
    for copy in fetches:
        copy.wait()

    def remote(source, target, source_sem, target_sem, place):
        return pltpu.make_async_remote_copy(
            src_ref=source,
            dst_ref=target,
            send_sem=source_sem,
            recv_sem=target_sem,
            device_id=place,
            device_id_type=pl.DeviceIdType.MESH,
        )

    lanes = lane_ids(layers)
    zero = jnp.zeros((layers, LANES), jnp.float32)

    def turn_by(value, amount):
        amount = amount % LANES
        return right_by(value, amount) if amount else value

    for tile in range(tiles):
        place = pl.ds(tile * LANES, LANES)
        kind = node_class[:, :, place]
        resist = jnp.full(kind.shape, 0.5 / node_table[0], jnp.float32)
        for k in range(1, len(node_table)):
            resist = jnp.where(kind == k, jnp.float32(0.5 / node_table[k]), resist)
        via = jnp.where(via_sites[:, :, place] == 1, jnp.float32(via_conductance), 0.0)
        ball = jnp.where(ball_sites[:, place] == 1, jnp.float32(ball_conductance), 0.0)
        sites = jnp.concatenate([via, ball[None]], axis=0)
        for k, value in enumerate((capacity[:, :, place], resist, sites, voltage[:, :, place])):
            swapped = jnp.swapaxes(value, 0, 1)
            for r in range(block):
                planes[k * block + r, :, place] = swapped[r]
        planes[4 * block, :, place] = load_type[:, place].astype(jnp.float32)

    share = LANES // margin
    lots = []
    begin = 0
    for first, size in ((0, 3 * block), (3 * block, block + 1)):
        packs = -(-size // share)
        lots.append((first, size, begin, packs))
        begin += packs

    def pack_edges(lot):
        first, size, base, packs = lots[lot]
        for side, begin in ((0, LANES - margin), (1, 0)):
            place = pl.ds((tiles - 1) * LANES if side == 0 else 0, LANES)
            for q in range(packs):
                joint = zero
                for t in range(share):
                    plane = q + packs * t
                    if plane < size:
                        moved = turn_by(planes[first + plane, :, place], margin * t - begin)
                        joint = jnp.where(lanes // margin == t, moved, joint)
                edge[side, base + q] = joint

    def edge_copy(lot, side, n, place):
        tiles_here = pl.ds(*lots[lot][2:])
        return remote(
            edge.at[side, tiles_here], edge_in.at[side, mine, tiles_here],
            edge_send.at[lot, side, n], edge_recv.at[lot, side, seat], place,
        )

    def edge_places(side):
        to_column, reach = sides[side][1:3]
        for n, k in enumerate(reach):
            owner_section, owner_gx = owner(k, to_column)
            yield n, {"section": owner_section, "gx": owner_gx, "gy": to_column}

    def send_edges(lot):
        for side in range(2):

            @pl.when(sides[side][0])
            def _():
                for n, place in edge_places(side):
                    edge_copy(lot, side, n, place).start()

    quarter = LANES // 4
    slim = [
        k
        for k in range(regions)
        if quarter in (margin - width * k, margin - width * (regions - 1 - k))
    ]

    def piece(k, t):
        if margin - width * k == quarter:
            return quarter * (t + 1), 0
        return quarter * t, LANES - quarter

    def carriers(lot):
        return lots[lot][1] - lots[lot][1] // 4

    def part(lot, thin):
        return pl.ds(lots[lot][0], carriers(lot) if thin else lots[lot][1])

    def by_kind(place, act):
        if not slim:
            act(False)
            return
        thin = place == slim[0]
        for k in slim[1:]:
            thin = jnp.logical_or(thin, place == k)

        @pl.when(thin)
        def _():
            act(True)

        @pl.when(jnp.logical_not(thin))
        def _():
            act(False)

    def build(lot, k):
        start = width * k - margin
        first, size = lots[lot][:2]
        window = []
        for plane in range(first, first + size):
            joint = None
            for tile in range(tiles):
                low = tile * LANES
                if low + LANES <= start or low >= start + LANES:
                    continue
                moved = turn_by(planes[plane, :, pl.ds(low, LANES)], low - start)
                joint = moved if joint is None else jnp.where(lanes >= low - start, moved, joint)
            window.append(joint)
        count_sent = carriers(lot) if k in slim else size
        for c in range(count_sent):
            joint = window[c]
            if k in slim and count_sent + c // 3 < size:
                source, target = piece(k, c % 3)
                carried = turn_by(window[count_sent + c // 3], target - source)
                joint = jnp.where(lanes // quarter == target // quarter, carried, joint)
            send[k, first + c] = joint

    def direct(lot, d, k, thin):
        owner_section, owner_gx = owner(k, gy_here)
        return remote(
            send.at[k, part(lot, thin)], recv.at[mine, part(lot, thin)],
            send_sem.at[lot, d], recv_sem.at[lot, d],
            {"section": owner_section, "gx": owner_gx},
        )

    def handed(lot, d, source, slot, thin):
        return remote(
            source.at[part(lot, thin)], recv.at[slot, part(lot, thin)],
            pass_send.at[lot, d], pass_recv.at[lot, d], partner,
        )

    def own(lot, thin):
        return pltpu.make_async_copy(
            send.at[spot, part(lot, thin)], recv.at[mine, part(lot, thin)], own_sem.at[lot]
        )

    def dispatch(lot, k):
        d = (k - spot + regions) % regions

        @pl.when(d != 0)
        def _():
            direct(lot, d, k, k in slim).start()

        @pl.when(d == 0)
        def _():
            own(lot, k in slim).start()
            handed(lot, 0, send.at[k], mine, k in slim).start()

    ends = [k for k in range(regions) if k < over or k >= regions - over]
    order = ends + [k for k in range(regions) if k not in ends]
    for lot in range(2):
        pack_edges(lot)
        for k in order:
            build(lot, k)
    pl.semaphore_wait(barrier, greeted)
    for lot in range(2):
        send_edges(lot)
        for k in order:
            dispatch(lot, k)

    def pick(table):
        return [
            jnp.where(system == 0, jnp.float32(table[a]), jnp.float32(table[b]))
            for a, b in ((0, 0), (1, 3), (2, 4))
        ]

    shifts = pick(diagonal)
    lam0, alpha, beta = shifts[0], shifts[1], pick(coupling)[1]
    shares = pick([sum(row) for row in inverse_transform])
    mixing = [pick([row[j] for row in inverse_transform]) for j in range(SECTIONS)]
    scal = (lam0, alpha, beta)
    for slot in range(2):
        for k in range(3):
            x0[slot, k, 0] = zero
            x0[slot, k, x0.shape[2] - 1] = zero
    e0[0] = zero

    def edge_slot(place):
        return (place // gx_count * 2 + system) * gx_count + place % gx_count

    def edge_handed(lot, side, place):
        landing = edge_in.at[side, edge_slot(place), pl.ds(*lots[lot][2:])]
        return remote(
            landing, landing, edge_pass_send.at[lot, side, place],
            edge_pass_recv.at[lot, side, place], partner,
        )

    nearest = [*range(1, regions, 2), *range(2, regions, 2)]

    def slot_from(d):
        owner_section, owner_gx = owner((spot - d + regions) % regions, gy_here)
        return owner_section * gx_count + owner_gx

    def take(lot):
        for side, (sends, _, _, comes, _, reached) in enumerate(sides):

            @pl.when(jnp.logical_and(comes, reached))
            def _():
                tiles_here = pl.ds(*lots[lot][2:])
                for place in range(regions):
                    remote(
                        edge.at[side, tiles_here], edge_in.at[side, edge_slot(place), tiles_here],
                        edge_send.at[lot, side, 0], edge_recv.at[lot, side, place], partner,
                    ).wait_recv()
                    edge_handed(lot, side, place).start()

        for d in nearest:

            def act(thin):
                direct(lot, d, (spot + d) % regions, thin).wait_recv()
                slot = slot_from(d)
                handed(lot, d, recv.at[slot], slot, thin).start()

            by_kind(spot, act)

    def settle(lot):
        first, size, base, packs = lots[lot]
        for d in nearest:
            target = (spot + d) % regions
            by_kind(target, lambda thin: direct(lot, d, target, thin).wait_send())

        def act(thin):
            own(lot, thin).wait()
            handed(lot, 0, send.at[spot], mine, thin).wait()
            for d in nearest:
                slot = slot_from(d)
                handed(lot, d, recv.at[slot], slot, thin).wait()

        by_kind(spot, act)
        for side, (sends, _, _, comes, _, reached) in enumerate(sides):

            @pl.when(sends)
            def _():
                for n, place in edge_places(side):
                    edge_copy(lot, side, n, place).wait_send()

            @pl.when(jnp.logical_and(comes, reached))
            def _():
                for place in range(regions):
                    edge_handed(lot, side, place).wait()

            for k in sides[side][2]:
                start = width * k - margin
                outside = lanes < -start if side == 0 else lanes >= wide - start

                def patch(b, edged):
                    held = [recv[b, first + c] for c in range(size)]
                    if k in slim:
                        count_sent = carriers(lot)
                        for c in range(3 * (size - count_sent)):
                            source, target = piece(k, c % 3)
                            moved = turn_by(held[c], source - target)
                            base_tile = held[count_sent + c // 3] if c % 3 else held[c]
                            held[count_sent + c // 3] = jnp.where(
                                lanes // quarter == source // quarter, moved, base_tile
                            )
                    changed = range(size) if edged else range(carriers(lot), size)
                    for plane in changed:
                        joint = held[plane]
                        if edged:
                            q, t = plane % packs, plane // packs
                            low = -margin if side == 0 else wide
                            moved = turn_by(edge_in[side, b, base + q], low - start - margin * t)
                            joint = jnp.where(outside, moved, joint)
                        recv[b, first + plane] = joint

                def run(edged):
                    def pair_of_blocks(c, carry):
                        patch(2 * c, edged)
                        patch(2 * c + 1, edged)
                        return carry

                    lax.fori_loop(0, parts // 2, pair_of_blocks, 0)

                @pl.when(jnp.logical_and(comes, spot == k))
                def _():
                    run(True)

                if k in slim:

                    @pl.when(jnp.logical_and(jnp.logical_not(comes), spot == k))
                    def _():
                        run(False)

    rows = parts * block
    level_of = layer_ids(layers)
    column = region * width - margin + lanes
    inside = (column >= 0) & (column < columns)
    joined = inside & (column < columns - 1) & (lanes < LANES - 1)

    def coefficients(c, behind_gx):
        for b in (2 * c, 2 * c + 1):
            following = jnp.minimum(b + 1, parts - 1)
            for r in range(block):
                i = b * block + r
                cap, sites = recv[b, r], recv[b, 2 * block + r]
                resist = jnp.where(inside, recv[b, block + r], 0.5)
                if r + 1 < block:
                    resist_ahead = recv[b, block + r + 1]
                else:
                    resist_ahead = recv[following, block]
                resist_ahead = jnp.where(inside, resist_ahead, 0.5)
                gx = 1.0 / (resist + resist_ahead)
                if r + 1 == block:
                    gx = gx * (b < parts - 1).astype(jnp.float32)
                gy = jnp.where(joined, 1.0 / (resist + left_by(resist, 1)), 0.0)
                gv = jnp.where(level_of < layers - 1, sites, 0.0)
                ground = jnp.where(level_of == 0, from_below(sites), 0.0)
                gy_low, gv_low = right_by(gy, 1), from_below(gv)
                total = (gx + behind_gx) + (gy + gy_low) + (gv + gv_low) + ground
                found = weights(cap, total, *scal)
                e0[i + 1] = gx
                for k, entry in enumerate((gy, gv, gy_low, gv_low) + found + (ground, cap, total)):
                    g0[k + 1, i] = entry
                behind_gx = gx
        return behind_gx

    def forcing(c, volt_behind):
        for b in (2 * c, 2 * c + 1):
            kind = recv[b, 4 * block]
            currents = [zero] * SECTIONS
            for t in range(LOADS):
                here = kind == float(t)
                for j in range(SECTIONS):
                    currents[j] = jnp.where(here, load_table[j, t], currents[j])
            for k in range(3):
                surf[k, b] = sum(mixing[j][k] * currents[j] for j in range(SECTIONS))
        for b in (2 * c, 2 * c + 1):
            following = jnp.minimum(b + 1, parts - 1)
            for r in range(block):
                i = b * block + r
                volt = recv[b, 3 * block + r]
                if r + 1 < block:
                    volt_ahead = recv[b, 3 * block + r + 1]
                else:
                    volt_ahead = recv[following, 3 * block]
                pulled = (
                    (e0[i + 1] * volt_ahead + e0[i] * volt_behind)
                    + (g0[GY, i] * left_by(volt, 1) + g0[GY_LOW, i] * right_by(volt, 1))
                    + (g0[GV, i] * from_above(volt) + g0[GV_LOW, i] * from_below(volt))
                )
                leak = g0[TOTAL, i] * volt - pulled
                source = [
                    jnp.where(
                        level_of == layers - 1,
                        jnp.broadcast_to(surf[k, b, r : r + 1, :], (layers, LANES)),
                        0.0,
                    )
                    - shares[k] * leak
                    for k in range(3)
                ]
                found = [g0[w, i] for w in (W_REAL, W_SAME, W_MATE)]
                first = solve_node(REAL, found, source[:1]) + solve_node(PAIR, found, source[1:])
                for k in range(3):
                    f0[k, i] = source[k]
                    x0[0, k, i + 1] = first[k]
                volt_behind = volt
        return volt_behind

    take(0)
    settle(0)
    behind = lax.fori_loop(0, parts // 4, coefficients, zero)
    take(1)
    lax.fori_loop(parts // 4, parts // 2, coefficients, behind)
    refs = ((e0, g0, x0, f0), (e1, g1, x1, f1), (e2, g2, x2, f2))
    coarsen(0, refs, scal)
    coarsen(1, refs, scal)
    settle(1)
    lax.fori_loop(0, parts // 2, forcing, zero)

    ringed = margin < BOTH_CYCLES
    first_sent, last_sent = exchanged(margin) if ringed else (0, margin)
    sent = last_sent - first_sent
    ring_share = LANES // sent
    ring_groups = -(-rows // ring_share)

    def ring_copies(fields):
        span = pl.ds(fields[0], len(fields))
        for side, exists, came, place in (
            (0, has_after, has_before, after),
            (1, has_before, has_after, before),
        ):
            slot = 2 * (len(fields) - 1) + side
            yield exists, came, remote(
                packed.at[side, span], landed.at[side, span],
                ring_send.at[slot], ring_recv.at[slot], place,
            )

    def exchange(fields):
        for q in range(ring_groups):
            for side, begin in ((0, width + first_sent), (1, LANES - width - last_sent)):
                for k in fields:
                    joint = None
                    for t in range(ring_share):
                        row = q + ring_groups * t
                        if row < rows:
                            moved = turn_by(x0[1, k, row + 1], sent * t - begin)
                            joint = moved if t == 0 else jnp.where(lanes >= sent * t, moved, joint)
                    packed[side, k, q] = joint
        for exists, came, copy in ring_copies(fields):

            @pl.when(exists)
            def _():
                copy.start()

    def finish(fields):
        for exists, came, copy in ring_copies(fields):

            @pl.when(exists)
            def _():
                copy.wait_send()

            @pl.when(came)
            def _():
                copy.wait_recv()

        low = (lanes >= first_sent) & (lanes < jnp.where(has_before, last_sent, 0))
        high = (lanes < LANES - first_sent) & (
            lanes >= jnp.where(has_after, LANES - last_sent, LANES)
        )
        for q in range(ring_groups):
            for k in fields:
                from_low, from_high = landed[0, k, q], landed[1, k, q]
                for t in range(ring_share):
                    row = q + ring_groups * t
                    if row < rows:
                        below = turn_by(from_low, first_sent - sent * t)
                        above = turn_by(from_high, LANES - last_sent - sent * t)
                        held = jnp.where(high, above, x0[1, k, row + 1])
                        x0[1, k, row + 1] = jnp.where(low, below, held)

    share = LANES // width
    groups = block // share
    half = max(groups // 2, 1)
    halves = groups // half
    slot_out = spot * 2 + system

    def gifts(fields, buf, into, sends, recvs, own):
        for d in range(parts):
            peer = (mine + d) % parts
            if d == 0:
                yield pltpu.make_async_copy(buf.at[peer], into.at[slot_out], own)
            else:
                yield remote(
                    buf.at[peer], into.at[slot_out], sends.at[d], recvs.at[d], group_device(peer)
                )

    def give(fields, buf, *rest):
        chosen = half if fields == REAL else groups

        def pack(b, carry):
            for n, k in enumerate(fields):
                for index in range(chosen):
                    joint = zero
                    for t in range(share):
                        row = b * block + index + groups * t + 1
                        held = x0[1, k, row]
                        if fields == REAL and halves > 1:
                            held = jnp.where(system == 0, held, x0[1, k, row + half])
                        moved = turn_by(held, width * t - margin)
                        joint = jnp.where(lanes // width == t, moved, joint)
                    buf[b, n * groups + index] = joint
            return carry

        if parts <= 8:
            for b in range(parts):
                pack(b, 0)
        else:
            lax.fori_loop(0, parts, pack, 0)
        for copy in gifts(fields, buf, *rest):
            copy.start()

    outputs = (
        (PAIR, pair_buf, pair_in, pair_send, pair_recv, own_sem.at[2]),
        (REAL, real_buf, real_in, real_send, real_recv, own_sem.at[3]),
    )

    def both(step, carry):
        for output in outputs:
            fields = output[0]

            @pl.when(step > 0)
            def _():
                if ringed:
                    finish(fields)
                sweep(0, refs, fields, 1)

            cycle(refs, fields)

            @pl.when(step == 0)
            def _():
                if ringed:
                    exchange(fields)

            @pl.when(step > 0)
            def _():
                give(*output)

        return carry

    lax.fori_loop(0, 2, both, 0)
    for output in outputs:
        for copy in gifts(*output):
            copy.wait()

    for tile in range(regions // share):
        mixed = [[None] * block for _ in range(SECTIONS)]
        for q in range(groups):
            fields = []
            for n in range(share):
                first = 2 * (tile * share + n)
                fields.append(
                    [real_in[first + q // half, q % half]]
                    + [pair_in[first, k * groups + q] for k in (0, 1)]
                    + [pair_in[first + 1, k * groups + q] for k in (0, 1)]
                )
            for s in range(SECTIONS):
                sums = [
                    sum(transform[s][k] * fields[n][k] for k in range(SECTIONS))
                    for n in range(share)
                ]
                for t in range(share):
                    joint = zero
                    for n in range(share):
                        turn = (width * (n - t)) % LANES
                        moved = right_by(sums[n], turn) if turn else sums[n]
                        joint = jnp.where(lanes // width == n, moved, joint)
                    mixed[s][q + groups * t] = joint
        place = pl.ds(tile * LANES, LANES)
        for s in range(SECTIONS):
            turned = jnp.swapaxes(jnp.stack(mixed[s]), 0, 1)
            sections[s, :, :, place] = turned
            if s == SECTIONS - 1:
                next_voltage[:, :, place] = voltage[:, :, place] + turned


def local(voltage, capacity, node_class, via_sites, ball_sites, load_type, load_table):
    layers, block, wide = voltage.shape
    gx_count = lax.axis_size("gx")
    gy_count = lax.axis_size("gy")
    parts = lax.axis_size("section") * gx_count
    regions = parts // 2
    width = wide // regions
    margin = (LANES - width) // 2
    sizes = (parts, gx_count, gy_count, width, margin, wide * gy_count)
    rows = parts * block
    count = 4 * block + 1
    per_tile = LANES // margin
    packs = -(-3 * block // per_tile) - (-(block + 1) // per_tile)

    def vmem(*shape):
        return pltpu.VMEM(shape, jnp.float32)

    def levels(extra, *lead):
        return [vmem(*lead, rows // 4**m + extra, layers, LANES) for m in range(LEVELS)]

    mid = 1
    if margin < BOTH_CYCLES:
        first_sent, last_sent = exchanged(margin)
        mid = -(-rows // (LANES // (last_sent - first_sent)))
    groups = block * width // LANES
    scratch = [
        pltpu.SMEM(load_table.shape[::-1], jnp.float32),
        vmem(*voltage.shape),
        vmem(*capacity.shape),
        pltpu.VMEM(node_class.shape, jnp.int32),
        pltpu.VMEM(via_sites.shape, jnp.int32),
        pltpu.VMEM(ball_sites.shape, jnp.int32),
        pltpu.VMEM(load_type.shape, jnp.int32),
        vmem(count, layers, wide),
        vmem(2, packs, layers, LANES),
        vmem(2, parts, packs, layers, LANES),
        vmem(regions, count, layers, LANES),
        vmem(parts, count, layers, LANES),
        vmem(3, parts, block, LANES),
        *levels(1),
        *levels(0, COEFFS),
        *levels(2, 2, 3),
        *levels(0, 3),
        vmem(2, 3, mid, layers, LANES),
        vmem(2, 3, mid, layers, LANES),
        *[vmem(parts, 2 * groups, layers, LANES)] * 2,
        *[vmem(parts, max(groups // 2, 1), layers, LANES)] * 2,
        pltpu.SemaphoreType.DMA((7,)),
        pltpu.SemaphoreType.DMA((2, 2, -(-margin // width))),
        *[pltpu.SemaphoreType.DMA((2, 2, regions))] * 3,
        *[pltpu.SemaphoreType.DMA((2, regions))] * 4,
        pltpu.SemaphoreType.DMA((4,)),
        pltpu.SemaphoreType.DMA((4,)),
        *[pltpu.SemaphoreType.DMA((parts,))] * 4,
        pltpu.SemaphoreType.DMA((4,)),
    ]
    grant = 4 * 1024 * 1024
    for part in scratch:
        if "vmem" in str(part.memory_space).lower():
            grant += 4 * math.prod(part.shape)
    arguments = (load_table.T, voltage, capacity, node_class, via_sites, ball_sites, load_type)
    return pl.pallas_call(
        functools.partial(kernel, sizes, radau_tables()),
        out_shape=(
            jax.ShapeDtypeStruct((SECTIONS, layers, block, wide), jnp.float32),
            jax.ShapeDtypeStruct((layers, block, wide), jnp.float32),
        ),
        in_specs=[
            *[pl.BlockSpec(memory_space=pl.ANY)] * 7,
        ],
        out_specs=(
            pl.BlockSpec(memory_space=pltpu.VMEM),
            pl.BlockSpec(memory_space=pltpu.VMEM),
        ),
        scratch_shapes=scratch,
        compiler_params=pltpu.CompilerParams(
            collective_id=0, has_side_effects=True, vmem_limit_bytes=grant
        ),
    )(*[pltpu.with_memory_space_constraint(a, pltpu.MemorySpace.HBM) for a in arguments])


def solution(mesh):
    return jax.shard_map(
        local,
        mesh=mesh,
        in_specs=(
            P(None, row_axes, "gy"),
            P(None, row_axes, "gy"),
            P(None, row_axes, "gy"),
            P(None, row_axes, "gy"),
            P(row_axes, "gy"),
            P(row_axes, "gy"),
            P(),
        ),
        out_specs=(P(None, None, row_axes, "gy"), P(None, row_axes, "gy")),
        check_vma=False,
    )
```

```python
import functools
import math

import jax
import jax.numpy as jnp
from jax import lax
from jax.experimental import pallas as pl
from jax.experimental.pallas import tpu as pltpu
from jax.sharding import PartitionSpec as P

SECTIONS = 5
LEVELS = 3
LOADS = 16
LANES = 128
BOTH_CYCLES = 56
STEP = 32
REAL = (0,)
PAIR = (1, 2)
GX, GY, GV, GY_LOW, GV_LOW, W_REAL, W_SAME, W_MATE, D_REAL, D_SAME, D_MATE, GROUND, CAP, TOTAL = range(14)
COEFFS = 14

node_table = (0.35, 0.55, 0.8, 1.1, 1.5, 2.0, 2.7, 3.6)
via_conductance = 2.5
ball_conductance = 4.0
damping = 0.8
slab_partner = (0, 2, 1, 4, 3)
row_axes = ("section", "gx")


def pair_times(first, second):
    return (
        first[0] * second[0] - first[1] * second[1],
        first[0] * second[1] + first[1] * second[0],
    )


def pair_over(first, second):
    divisor = second[0] * second[0] + second[1] * second[1]
    return (
        (first[0] * second[0] + first[1] * second[1]) / divisor,
        (first[1] * second[0] - first[0] * second[1]) / divisor,
    )


def pair_minus(first, second):
    return (first[0] - second[0], first[1] - second[1])


def poly_value(coeffs, point):
    total = (0.0, 0.0)
    for c in reversed(coeffs):
        total = pair_times(total, point)
        total = (total[0] + c, total[1])
    return total


def poly_product(first, second):
    result = [0.0] * (len(first) + len(second) - 1)
    for i in range(len(first)):
        for j in range(len(second)):
            result[i + j] = result[i + j] + first[i] * second[j]
    return result


def poly_roots(coeffs):
    leading = coeffs[-1]
    scaled = [c / leading for c in coeffs]
    degree = len(coeffs) - 1
    guesses = []
    current = (1.0, 0.0)
    for k in range(degree):
        guesses.append(current)
        current = pair_times(current, (0.4, 0.9))
    for repeat_index in range(800):
        for k in range(degree):
            divisor = (1.0, 0.0)
            for j in range(degree):
                if j != k:
                    divisor = pair_times(divisor, pair_minus(guesses[k], guesses[j]))
            guesses[k] = pair_minus(guesses[k], pair_over(poly_value(scaled, guesses[k]), divisor))
    return guesses


def matrix_product(first, second):
    return [
        [
            sum((first[i][k] * second[k][j] for k in range(len(second))))
            for j in range(len(second[0]))
        ]
        for i in range(len(first))
    ]


def matrix_inverse(matrix):
    order = len(matrix)
    work = [list(matrix[i]) + [1.0 if i == j else 0.0 for j in range(order)] for i in range(order)]
    for column in range(order):
        pivot = column
        for i in range(column + 1, order):
            if abs(work[i][column]) > abs(work[pivot][column]):
                pivot = i
        work[column], work[pivot] = (work[pivot], work[column])
        factor = work[column][column]
        work[column] = [entry / factor for entry in work[column]]
        for i in range(order):
            if i != column:
                scale_row = work[i][column]
                work[i] = [work[i][j] - scale_row * work[column][j] for j in range(2 * order)]
    return [row[order:] for row in work]


def eigen_vector(matrix, value):
    order = len(matrix)
    size_inner = order - 1
    system = []
    for i in range(size_inner):
        row = []
        for j in range(order):
            entry = (matrix[i][j], 0.0)
            if i == j:
                entry = pair_minus(entry, value)
            row.append(entry)
        row[order - 1] = (-row[order - 1][0], -row[order - 1][1])
        system.append(row)
    for column in range(size_inner):
        pivot = column
        for i in range(column + 1, size_inner):
            left_size = system[i][column][0] ** 2 + system[i][column][1] ** 2
            right_size = system[pivot][column][0] ** 2 + system[pivot][column][1] ** 2
            if left_size > right_size:
                pivot = i
        system[column], system[pivot] = (system[pivot], system[column])
        for i in range(size_inner):
            if i != column:
                factor = pair_over(system[i][column], system[column][column])
                system[i] = [
                    pair_minus(system[i][j], pair_times(factor, system[column][j]))
                    for j in range(order)
                ]
    vector = [pair_over(system[i][order - 1], system[i][i]) for i in range(size_inner)]
    vector.append((1.0, 0.0))
    return vector


def radau_tables():
    section_count = 5
    generator = [1.0]
    for k in range(section_count - 1):
        generator = poly_product(generator, [0.0, 1.0])
    for k in range(section_count):
        generator = poly_product(generator, [-1.0, 1.0])
    for k in range(section_count - 1):
        generator = [j * generator[j] for j in range(1, len(generator))]
    abscissae = sorted((root[0] for root in poly_roots(generator)))
    vander = [[abscissae[i] ** j for j in range(section_count)] for i in range(section_count)]
    integrals = [
        [abscissae[i] ** (j + 1) / (j + 1) for j in range(section_count)]
        for i in range(section_count)
    ]
    butcher = matrix_product(integrals, matrix_inverse(vander))
    inverse = matrix_inverse(butcher)
    coeffs = [0.0] * (section_count + 1)
    coeffs[section_count] = 1.0
    current = [[0.0] * section_count for _ in range(section_count)]
    for k in range(1, section_count + 1):
        current = matrix_product(inverse, current)
        for i in range(section_count):
            current[i][i] = current[i][i] + coeffs[section_count - k + 1]
        applied = matrix_product(inverse, current)
        coeffs[section_count - k] = -sum((applied[i][i] for i in range(section_count))) / k
    eigen_values = poly_roots(coeffs)
    real_pick = 0
    for k in range(section_count):
        if abs(eigen_values[k][1]) < abs(eigen_values[real_pick][1]):
            real_pick = k
    upper_half = [k for k in range(section_count) if eigen_values[k][1] > 1e-09]
    upper_half = sorted(upper_half, key=lambda k: -eigen_values[k][0])
    columns = [[entry[0] for entry in eigen_vector(inverse, (eigen_values[real_pick][0], 0.0))]]
    for k in upper_half:
        vector = eigen_vector(inverse, eigen_values[k])
        columns.append([entry[0] for entry in vector])
        columns.append([entry[1] for entry in vector])
    transform = [[columns[j][i] for j in range(section_count)] for i in range(section_count)]
    inverse_transform = matrix_inverse(transform)
    blocks = matrix_product(matrix_product(inverse_transform, inverse), transform)
    diagonal = [blocks[k][k] for k in range(section_count)]
    coupling = [
        blocks[k][slab_partner[k]] if slab_partner[k] != k else 0.0 for k in range(section_count)
    ]
    return (transform, inverse_transform, diagonal, coupling)


def left_by(value, count):
    return pltpu.roll(value, LANES - count, axis=1)


def right_by(value, count):
    return pltpu.roll(value, count, axis=1)


def from_above(value):
    return pltpu.roll(value, value.shape[0] - 1, axis=0)


def from_below(value):
    return pltpu.roll(value, 1, axis=0)


def lane_ids(layers):
    return lax.broadcasted_iota(jnp.int32, (layers, LANES), 1)


def layer_ids(layers):
    return lax.broadcasted_iota(jnp.int32, (layers, LANES), 0)


def is_low(layers, stride):
    return (lane_ids(layers) // stride) % 2 == 0


def blocks(count, step, body):
    if count <= step:
        body(0)
        return

    def one(b, carry):
        body(b * step)
        return carry

    lax.fori_loop(0, count // step, one, 0)


def seam_low(level, value):
    if level == 1:
        return right_by(value, 1)
    return jnp.where(is_low(value.shape[0], 2), left_by(value, 1), right_by(value, 2))


def seam_high(level, value):
    if level == 1:
        return left_by(value, 1)
    return jnp.where(is_low(value.shape[0], 2), left_by(value, 2), right_by(value, 1))


def merge(low, stride, first, second):
    return jnp.where(low, first + left_by(first, stride), second + right_by(second, stride))


def weights(cap, total, lam0, alpha, beta):
    real = lam0 * cap + total
    mate = beta * cap
    both = alpha * cap + total
    scale = damping / (both * both + mate * mate)
    return damping / real, both * scale, mate * scale, real, both, mate


def reach(valid):
    once = -(-(valid + 2) // 2)
    twice = -(-(once + 2) // 2)
    return 2 * (2 * (twice + 3) + 2) + 2


def exchanged(margin):
    first = 0
    while reach(first + 2) <= margin:
        first += 1
    return first, reach(1)


def solve_node(fields, weight, values):
    if fields == REAL:
        return (weight[0] * values[0],)
    return (
        weight[1] * values[0] - weight[2] * values[1],
        weight[1] * values[1] + weight[2] * values[0],
    )


def sweep(level, refs, fields, source, restrict=False):
    edge, g, x, f = refs[level]
    tiles, layers = f.shape[1], f.shape[2]
    stride = 2**level
    half = tiles // 2
    step = min(STEP, half)
    target = 1 - source
    if level:
        for k in fields:
            x[source, k, 0] = seam_low(level, x[source, k, tiles])
            x[source, k, tiles + 1] = seam_high(level, x[source, k, 1])

    def part(begin):
        found = []
        xs = [[x[source, k, begin + r] for r in range(step + 2)] for k in fields]
        for r in range(step):
            i = begin + r
            ahead, behind = edge[i + 1], edge[i]
            gy, gy_low, gv, gv_low = g[GY, i], g[GY_LOW, i], g[GV, i], g[GV_LOW, i]
            here = [xs[n][r + 1] for n in range(len(fields))]
            values = []
            for n, k in enumerate(fields):
                along = ahead * xs[n][r + 2] + behind * xs[n][r]
                across = gy * left_by(here[n], stride) + gy_low * right_by(here[n], stride)
                through = gv * from_above(here[n]) + gv_low * from_below(here[n])
                values.append((f[k, i] + along) + (across + through))
            if not restrict:
                if fields == REAL:
                    weight = (g[W_REAL, i],)
                else:
                    weight = (None, g[W_SAME, i], g[W_MATE, i])
                change = solve_node(fields, weight, values)
                found.append([(1.0 - damping) * here[n] + change[n] for n in range(len(fields))])
            elif fields == REAL:
                found.append([values[0] - g[D_REAL, i] * here[0]])
            else:
                same, mate = g[D_SAME, i], g[D_MATE, i]
                found.append(
                    [
                        values[0] - same * here[0] - mate * here[1],
                        values[1] - same * here[1] + mate * here[0],
                    ]
                )
        return found

    def body(start):
        parts = [part(start), part(half + start)]
        if not restrict:
            for p in range(2):
                for r in range(step):
                    for n, k in enumerate(fields):
                        x[target, k, p * half + start + r + 1] = parts[p][r][n]
            return
        edge_next, g_next, x_next, f_next = refs[level + 1]
        low = is_low(layers, stride)
        for r in range(0, step, 2):
            i = start // 2 + r // 2
            summed = [
                merge(
                    low,
                    stride,
                    parts[0][r][n] + parts[0][r + 1][n],
                    parts[1][r][n] + parts[1][r + 1][n],
                )
                for n in range(len(fields))
            ]
            weight = [g_next[w, i] for w in (W_REAL, W_SAME, W_MATE)]
            first = solve_node(fields, weight, summed)
            for n, k in enumerate(fields):
                f_next[k, i] = summed[n]
                x_next[0, k, i + 1] = first[n]

    blocks(half, step, body)


def prolong(level, refs, fields, target):
    x, f = refs[level][2:]
    x_next, f_next = refs[level + 1][2:]
    layers = f.shape[2]
    stride = 2**level
    half = f.shape[1] // 2
    count = f_next.shape[1]
    step = min(STEP, count)

    def body(start):
        low = is_low(layers, stride)
        for r in range(step):
            for k in fields:
                coarse = x_next[1, k, start + r + 1]
                both = (
                    jnp.where(low, coarse, right_by(coarse, stride)),
                    jnp.where(low, left_by(coarse, stride), coarse),
                )
                for p in range(2):
                    for t in range(2):
                        row = p * half + 2 * (start + r) + t + 1
                        x[target, k, row] = x[target, k, row] + both[p]

    blocks(count, step, body)


def coarsen(level, refs, scal):
    edge, g = refs[level][:2]
    edge_next, g_next = refs[level + 1][:2]
    layers = g.shape[2]
    stride = 2**level
    half = g.shape[1] // 2
    count = g_next.shape[1]
    step = min(STEP, count)

    def cross(start):
        low = is_low(layers, stride)
        for r in range(step):
            j = 2 * (start + r) + 2
            edge_next[start + r + 1] = merge(low, stride, edge[j], edge[half + j])

    blocks(count, step, cross)
    first = seam_low(level + 1, edge_next[count])
    edge_next[0] = jnp.where(lane_ids(layers) % (2 * stride) == 0, 0.0, first)

    def body(start):
        low = is_low(layers, stride)
        for r in range(step):
            i = start + r
            j = 2 * i

            def summed(plane, p):
                return g[plane, p * half + j] + g[plane, p * half + j + 1]

            def joined(plane):
                return merge(low, stride, summed(plane, 0), summed(plane, 1))

            gy = jnp.where(low, left_by(summed(GY, 0), stride), summed(GY, 1))
            gv, ground, cap = joined(GV), joined(GROUND), joined(CAP)
            gy_low, gv_low = right_by(gy, 2 * stride), from_below(gv)
            total = (edge_next[i + 1] + edge_next[i]) + (gy + gy_low) + (gv + gv_low) + ground
            found = weights(cap, total, *scal)
            for k, entry in enumerate((gy, gv, gy_low, gv_low) + found + (ground, cap)):
                g_next[k + 1, i] = entry

    blocks(count, step, body)


def cycle(refs, fields):
    sweep(0, refs, fields, 0)
    sweep(0, refs, fields, 1, restrict=True)
    sweep(1, refs, fields, 0)
    sweep(1, refs, fields, 1, restrict=True)
    for n in range(3):
        sweep(2, refs, fields, n % 2)
    prolong(1, refs, fields, 1)
    sweep(1, refs, fields, 1)
    sweep(1, refs, fields, 0)
    prolong(0, refs, fields, 1)
    sweep(0, refs, fields, 1)
    sweep(0, refs, fields, 0)


def kernel(
    sizes, tables, load_table_in, voltage_in, capacity_in, node_class_in, via_sites_in,
    ball_sites_in, load_type_in, sections, next_voltage,
    load_table, voltage, capacity, node_class, via_sites, ball_sites, load_type,
    planes, edge, edge_in, send, recv, surf, e0, e1, e2, g0, g1, g2, x0, x1, x2, f0, f1, f2,
    packed, landed, pair_buf, pair_in, real_buf, real_in,
    load_sem, edge_send, edge_recv, edge_pass_send, edge_pass_recv, send_sem, recv_sem, pass_send, pass_recv,
    ring_send, ring_recv, pair_send, pair_recv, real_send, real_recv, own_sem,
):
    parts, gx_count, gy_count, width, margin, columns = sizes
    transform, inverse_transform, diagonal, coupling = tables
    layers = voltage.shape[0]
    block = voltage.shape[1]
    wide = voltage.shape[2]
    tiles = wide // LANES
    regions = parts // 2
    count = 4 * block + 1
    section_here = lax.axis_index("section")
    gx_here = lax.axis_index("gx")
    gy_here = lax.axis_index("gy")
    mine = section_here * gx_count + gx_here
    system = section_here % 2
    all_regions = regions * gy_count

    def snake(place, row):
        return place + (row % 2) * (gx_count - 1 - 2 * place)

    def turned(place, column):
        return place + (column % 2) * (regions - 1 - 2 * place)

    pair = section_here // 2
    spot = turned(pair * gx_count + snake(gx_here, pair), gy_here)
    region = gy_here * regions + spot

    def owner(place, column):
        found = turned(place, column)
        row = found // gx_count
        return row * 2 + system, snake(found % gx_count, row)

    def group_device(index):
        return {"section": index // gx_count, "gx": index % gx_count}

    def region_device(index):
        column = index // regions
        owner_section, owner_gx = owner(index % regions, column)
        return {"section": owner_section, "gx": owner_gx, "gy": column}

    after = region_device((region + 1) % all_regions)
    before = region_device((region + all_regions - 1) % all_regions)
    has_after = region < all_regions - 1
    has_before = region > 0
    seat = pair * gx_count + gx_here
    over = -(-margin // width)
    sides = (
        (gy_here < gy_count - 1, gy_here + 1, range(over), gy_here > 0, gy_here - 1, spot < over),
        (
            gy_here > 0, gy_here - 1, range(regions - over, regions),
            gy_here < gy_count - 1, gy_here + 1, spot >= regions - over,
        ),
    )
    partner = {"section": section_here + 1 - 2 * system}

    barrier = pltpu.get_barrier_semaphore()

    def greet(place):
        pl.semaphore_signal(
            barrier, inc=1, device_id=place, device_id_type=pl.DeviceIdType.MESH
        )

    for d in range(1, parts):
        greet(group_device((mine + d) % parts))
    greeted = parts - 1
    for sends, to_column, reach, comes, from_column, reached in sides:
        greeted = greeted + jnp.where(sends, over, 0)

        @pl.when(jnp.logical_and(comes, reached))
        def _():
            for place in range(regions):
                greet(
                    {
                        "section": place // gx_count * 2 + system,
                        "gx": place % gx_count,
                        "gy": from_column,
                    }
                )

    if margin < BOTH_CYCLES:
        for exists, place in ((has_after, after), (has_before, before)):
            greeted = greeted + exists.astype(jnp.int32)

            @pl.when(exists)
            def _():
                greet(place)

    fetches = []
    for n, (whole, here) in enumerate(
        (
            (node_class_in, node_class),
            (via_sites_in, via_sites),
            (ball_sites_in, ball_sites),
            (load_type_in, load_type),
            (voltage_in, voltage),
            (capacity_in, capacity),
            (load_table_in, load_table),
        )
    ):
        copy = pltpu.make_async_copy(whole, here, load_sem.at[n])
        copy.start()
        fetches.append(copy)
    for copy in fetches:
        copy.wait()

    def remote(source, target, source_sem, target_sem, place):
        return pltpu.make_async_remote_copy(
            src_ref=source,
            dst_ref=target,
            send_sem=source_sem,
            recv_sem=target_sem,
            device_id=place,
            device_id_type=pl.DeviceIdType.MESH,
        )

    lanes = lane_ids(layers)
    zero = jnp.zeros((layers, LANES), jnp.float32)

    def turn_by(value, amount):
        amount = amount % LANES
        return right_by(value, amount) if amount else value

    for tile in range(tiles):
        place = pl.ds(tile * LANES, LANES)
        kind = node_class[:, :, place]
        resist = jnp.full(kind.shape, 0.5 / node_table[0], jnp.float32)
        for k in range(1, len(node_table)):
            resist = jnp.where(kind == k, jnp.float32(0.5 / node_table[k]), resist)
        via = jnp.where(via_sites[:, :, place] == 1, jnp.float32(via_conductance), 0.0)
        ball = jnp.where(ball_sites[:, place] == 1, jnp.float32(ball_conductance), 0.0)
        sites = jnp.concatenate([via, ball[None]], axis=0)
        for k, value in enumerate((capacity[:, :, place], resist, sites, voltage[:, :, place])):
            swapped = jnp.swapaxes(value, 0, 1)
            for r in range(block):
                planes[k * block + r, :, place] = swapped[r]
        planes[4 * block, :, place] = load_type[:, place].astype(jnp.float32)

    share = LANES // margin
    lots = []
    begin = 0
    for first, size in ((0, 3 * block), (3 * block, block + 1)):
        packs = -(-size // share)
        lots.append((first, size, begin, packs))
        begin += packs

    def pack_edges(lot):
        first, size, base, packs = lots[lot]
        for side, begin in ((0, LANES - margin), (1, 0)):
            place = pl.ds((tiles - 1) * LANES if side == 0 else 0, LANES)
            for q in range(packs):
                joint = zero
                for t in range(share):
                    plane = q + packs * t
                    if plane < size:
                        moved = turn_by(planes[first + plane, :, place], margin * t - begin)
                        joint = jnp.where(lanes // margin == t, moved, joint)
                edge[side, base + q] = joint

    def edge_copy(lot, side, n, place):
        tiles_here = pl.ds(*lots[lot][2:])
        return remote(
            edge.at[side, tiles_here], edge_in.at[side, mine, tiles_here],
            edge_send.at[lot, side, n], edge_recv.at[lot, side, seat], place,
        )

    def edge_places(side):
        to_column, reach = sides[side][1:3]
        for n, k in enumerate(reach):
            owner_section, owner_gx = owner(k, to_column)
            yield n, {"section": owner_section, "gx": owner_gx, "gy": to_column}

    def send_edges(lot):
        for side in range(2):

            @pl.when(sides[side][0])
            def _():
                for n, place in edge_places(side):
                    edge_copy(lot, side, n, place).start()

    quarter = LANES // 4
    slim = [
        k
        for k in range(regions)
        if quarter in (margin - width * k, margin - width * (regions - 1 - k))
    ]

    def piece(k, t):
        if margin - width * k == quarter:
            return quarter * (t + 1), 0
        return quarter * t, LANES - quarter

    def carriers(lot):
        return lots[lot][1] - lots[lot][1] // 4

    def part(lot, thin):
        return pl.ds(lots[lot][0], carriers(lot) if thin else lots[lot][1])

    def by_kind(place, act):
        if not slim:
            act(False)
            return
        thin = place == slim[0]
        for k in slim[1:]:
            thin = jnp.logical_or(thin, place == k)

        @pl.when(thin)
        def _():
            act(True)

        @pl.when(jnp.logical_not(thin))
        def _():
            act(False)

    def build(lot, k):
        start = width * k - margin
        first, size = lots[lot][:2]
        window = []
        for plane in range(first, first + size):
            joint = None
            for tile in range(tiles):
                low = tile * LANES
                if low + LANES <= start or low >= start + LANES:
                    continue
                moved = turn_by(planes[plane, :, pl.ds(low, LANES)], low - start)
                joint = moved if joint is None else jnp.where(lanes >= low - start, moved, joint)
            window.append(joint)
        count_sent = carriers(lot) if k in slim else size
        for c in range(count_sent):
            joint = window[c]
            if k in slim and count_sent + c // 3 < size:
                source, target = piece(k, c % 3)
                carried = turn_by(window[count_sent + c // 3], target - source)
                joint = jnp.where(lanes // quarter == target // quarter, carried, joint)
            send[k, first + c] = joint

    def direct(lot, d, k, thin):
        owner_section, owner_gx = owner(k, gy_here)
        return remote(
            send.at[k, part(lot, thin)], recv.at[mine, part(lot, thin)],
            send_sem.at[lot, d], recv_sem.at[lot, d],
            {"section": owner_section, "gx": owner_gx},
        )

    def handed(lot, d, source, slot, thin):
        return remote(
            source.at[part(lot, thin)], recv.at[slot, part(lot, thin)],
            pass_send.at[lot, d], pass_recv.at[lot, d], partner,
        )

    def own(lot, thin):
        return pltpu.make_async_copy(
            send.at[spot, part(lot, thin)], recv.at[mine, part(lot, thin)], own_sem.at[lot]
        )

    def dispatch(lot, k):
        d = (k - spot + regions) % regions

        @pl.when(d != 0)
        def _():
            direct(lot, d, k, k in slim).start()

        @pl.when(d == 0)
        def _():
            own(lot, k in slim).start()
            handed(lot, 0, send.at[k], mine, k in slim).start()

    ends = [k for k in range(regions) if k < over or k >= regions - over]
    order = ends + [k for k in range(regions) if k not in ends]
    for lot in range(2):
        pack_edges(lot)
        for k in order:
            build(lot, k)
    pl.semaphore_wait(barrier, greeted)
    for lot in range(2):
        send_edges(lot)
        for k in order:
            dispatch(lot, k)

    def pick(table):
        return [
            jnp.where(system == 0, jnp.float32(table[a]), jnp.float32(table[b]))
            for a, b in ((0, 0), (1, 3), (2, 4))
        ]

    shifts = pick(diagonal)
    lam0, alpha, beta = shifts[0], shifts[1], pick(coupling)[1]
    shares = pick([sum(row) for row in inverse_transform])
    mixing = [pick([row[j] for row in inverse_transform]) for j in range(SECTIONS)]
    scal = (lam0, alpha, beta)
    for slot in range(2):
        for k in range(3):
            x0[slot, k, 0] = zero
            x0[slot, k, x0.shape[2] - 1] = zero
    e0[0] = zero

    def edge_slot(place):
        return (place // gx_count * 2 + system) * gx_count + place % gx_count

    def edge_handed(lot, side, place):
        landing = edge_in.at[side, edge_slot(place), pl.ds(*lots[lot][2:])]
        return remote(
            landing, landing, edge_pass_send.at[lot, side, place],
            edge_pass_recv.at[lot, side, place], partner,
        )

    nearest = [*range(1, regions, 2), *range(2, regions, 2)]

    def slot_from(d):
        owner_section, owner_gx = owner((spot - d + regions) % regions, gy_here)
        return owner_section * gx_count + owner_gx

    def take(lot):
        for side, (sends, _, _, comes, _, reached) in enumerate(sides):

            @pl.when(jnp.logical_and(comes, reached))
            def _():
                tiles_here = pl.ds(*lots[lot][2:])
                for place in range(regions):
                    remote(
                        edge.at[side, tiles_here], edge_in.at[side, edge_slot(place), tiles_here],
                        edge_send.at[lot, side, 0], edge_recv.at[lot, side, place], partner,
                    ).wait_recv()
                    edge_handed(lot, side, place).start()

        for d in nearest:

            def act(thin):
                direct(lot, d, (spot + d) % regions, thin).wait_recv()
                slot = slot_from(d)
                handed(lot, d, recv.at[slot], slot, thin).start()

            by_kind(spot, act)

    def settle(lot):
        first, size, base, packs = lots[lot]
        for d in nearest:
            target = (spot + d) % regions
            by_kind(target, lambda thin: direct(lot, d, target, thin).wait_send())

        def act(thin):
            own(lot, thin).wait()
            handed(lot, 0, send.at[spot], mine, thin).wait()
            for d in nearest:
                slot = slot_from(d)
                handed(lot, d, recv.at[slot], slot, thin).wait()

        by_kind(spot, act)
        for side, (sends, _, _, comes, _, reached) in enumerate(sides):

            @pl.when(sends)
            def _():
                for n, place in edge_places(side):
                    edge_copy(lot, side, n, place).wait_send()

            @pl.when(jnp.logical_and(comes, reached))
            def _():
                for place in range(regions):
                    edge_handed(lot, side, place).wait()

            for k in sides[side][2]:
                start = width * k - margin
                outside = lanes < -start if side == 0 else lanes >= wide - start

                def patch(b, edged):
                    held = [recv[b, first + c] for c in range(size)]
                    if k in slim:
                        count_sent = carriers(lot)
                        for c in range(3 * (size - count_sent)):
                            source, target = piece(k, c % 3)
                            moved = turn_by(held[c], source - target)
                            base_tile = held[count_sent + c // 3] if c % 3 else held[c]
                            held[count_sent + c // 3] = jnp.where(
                                lanes // quarter == source // quarter, moved, base_tile
                            )
                    changed = range(size) if edged else range(carriers(lot), size)
                    for plane in changed:
                        joint = held[plane]
                        if edged:
                            q, t = plane % packs, plane // packs
                            low = -margin if side == 0 else wide
                            moved = turn_by(edge_in[side, b, base + q], low - start - margin * t)
                            joint = jnp.where(outside, moved, joint)
                        recv[b, first + plane] = joint

                def run(edged):
                    def pair_of_blocks(c, carry):
                        patch(2 * c, edged)
                        patch(2 * c + 1, edged)
                        return carry

                    lax.fori_loop(0, parts // 2, pair_of_blocks, 0)

                @pl.when(jnp.logical_and(comes, spot == k))
                def _():
                    run(True)

                if k in slim:

                    @pl.when(jnp.logical_and(jnp.logical_not(comes), spot == k))
                    def _():
                        run(False)

    rows = parts * block
    level_of = layer_ids(layers)
    column = region * width - margin + lanes
    inside = (column >= 0) & (column < columns)
    joined = inside & (column < columns - 1) & (lanes < LANES - 1)

    def coefficients(c, behind_gx):
        for b in (2 * c, 2 * c + 1):
            following = jnp.minimum(b + 1, parts - 1)
            for r in range(block):
                i = b * block + r
                cap, sites = recv[b, r], recv[b, 2 * block + r]
                resist = jnp.where(inside, recv[b, block + r], 0.5)
                if r + 1 < block:
                    resist_ahead = recv[b, block + r + 1]
                else:
                    resist_ahead = recv[following, block]
                resist_ahead = jnp.where(inside, resist_ahead, 0.5)
                gx = 1.0 / (resist + resist_ahead)
                if r + 1 == block:
                    gx = gx * (b < parts - 1).astype(jnp.float32)
                gy = jnp.where(joined, 1.0 / (resist + left_by(resist, 1)), 0.0)
                gv = jnp.where(level_of < layers - 1, sites, 0.0)
                ground = jnp.where(level_of == 0, from_below(sites), 0.0)
                gy_low, gv_low = right_by(gy, 1), from_below(gv)
                total = (gx + behind_gx) + (gy + gy_low) + (gv + gv_low) + ground
                found = weights(cap, total, *scal)
                e0[i + 1] = gx
                for k, entry in enumerate((gy, gv, gy_low, gv_low) + found + (ground, cap, total)):
                    g0[k + 1, i] = entry
                behind_gx = gx
        return behind_gx

    def forcing(c, volt_behind):
        for b in (2 * c, 2 * c + 1):
            kind = recv[b, 4 * block]
            currents = [zero] * SECTIONS
            for t in range(LOADS):
                here = kind == float(t)
                for j in range(SECTIONS):
                    currents[j] = jnp.where(here, load_table[j, t], currents[j])
            for k in range(3):
                surf[k, b] = sum(mixing[j][k] * currents[j] for j in range(SECTIONS))
        for b in (2 * c, 2 * c + 1):
            following = jnp.minimum(b + 1, parts - 1)
            for r in range(block):
                i = b * block + r
                volt = recv[b, 3 * block + r]
                if r + 1 < block:
                    volt_ahead = recv[b, 3 * block + r + 1]
                else:
                    volt_ahead = recv[following, 3 * block]
                pulled = (
                    (e0[i + 1] * volt_ahead + e0[i] * volt_behind)
                    + (g0[GY, i] * left_by(volt, 1) + g0[GY_LOW, i] * right_by(volt, 1))
                    + (g0[GV, i] * from_above(volt) + g0[GV_LOW, i] * from_below(volt))
                )
                leak = g0[TOTAL, i] * volt - pulled
                source = [
                    jnp.where(
                        level_of == layers - 1,
                        jnp.broadcast_to(surf[k, b, r : r + 1, :], (layers, LANES)),
                        0.0,
                    )
                    - shares[k] * leak
                    for k in range(3)
                ]
                found = [g0[w, i] for w in (W_REAL, W_SAME, W_MATE)]
                first = solve_node(REAL, found, source[:1]) + solve_node(PAIR, found, source[1:])
                for k in range(3):
                    f0[k, i] = source[k]
                    x0[0, k, i + 1] = first[k]
                volt_behind = volt
        return volt_behind

    take(0)
    settle(0)
    behind = lax.fori_loop(0, parts // 4, coefficients, zero)
    take(1)
    lax.fori_loop(parts // 4, parts // 2, coefficients, behind)
    refs = ((e0, g0, x0, f0), (e1, g1, x1, f1), (e2, g2, x2, f2))
    coarsen(0, refs, scal)
    coarsen(1, refs, scal)
    settle(1)
    lax.fori_loop(0, parts // 2, forcing, zero)

    ringed = margin < BOTH_CYCLES
    first_sent, last_sent = exchanged(margin) if ringed else (0, margin)
    sent = last_sent - first_sent
    ring_share = LANES // sent
    ring_groups = -(-rows // ring_share)

    def ring_copies(fields):
        span = pl.ds(fields[0], len(fields))
        for side, exists, came, place in (
            (0, has_after, has_before, after),
            (1, has_before, has_after, before),
        ):
            slot = 2 * (len(fields) - 1) + side
            yield exists, came, remote(
                packed.at[side, span], landed.at[side, span],
                ring_send.at[slot], ring_recv.at[slot], place,
            )

    def exchange(fields):
        for q in range(ring_groups):
            for side, begin in ((0, width + first_sent), (1, LANES - width - last_sent)):
                for k in fields:
                    joint = None
                    for t in range(ring_share):
                        row = q + ring_groups * t
                        if row < rows:
                            moved = turn_by(x0[1, k, row + 1], sent * t - begin)
                            joint = moved if t == 0 else jnp.where(lanes >= sent * t, moved, joint)
                    packed[side, k, q] = joint
        for exists, came, copy in ring_copies(fields):

            @pl.when(exists)
            def _():
                copy.start()

    def finish(fields):
        for exists, came, copy in ring_copies(fields):

            @pl.when(exists)
            def _():
                copy.wait_send()

            @pl.when(came)
            def _():
                copy.wait_recv()

        low = (lanes >= first_sent) & (lanes < jnp.where(has_before, last_sent, 0))
        high = (lanes < LANES - first_sent) & (
            lanes >= jnp.where(has_after, LANES - last_sent, LANES)
        )
        for q in range(ring_groups):
            for k in fields:
                from_low, from_high = landed[0, k, q], landed[1, k, q]
                for t in range(ring_share):
                    row = q + ring_groups * t
                    if row < rows:
                        below = turn_by(from_low, first_sent - sent * t)
                        above = turn_by(from_high, LANES - last_sent - sent * t)
                        held = jnp.where(high, above, x0[1, k, row + 1])
                        x0[1, k, row + 1] = jnp.where(low, below, held)

    share = LANES // width
    groups = block // share
    half = max(groups // 2, 1)
    halves = groups // half
    slot_out = spot * 2 + system

    def gifts(fields, buf, into, sends, recvs, own):
        for d in range(parts):
            peer = (mine + d) % parts
            if d == 0:
                yield pltpu.make_async_copy(buf.at[peer], into.at[slot_out], own)
            else:
                yield remote(
                    buf.at[peer], into.at[slot_out], sends.at[d], recvs.at[d], group_device(peer)
                )

    def give(fields, buf, *rest):
        chosen = half if fields == REAL else groups

        def pack(b, carry):
            for n, k in enumerate(fields):
                for index in range(chosen):
                    joint = zero
                    for t in range(share):
                        row = b * block + index + groups * t + 1
                        held = x0[1, k, row]
                        if fields == REAL and halves > 1:
                            held = jnp.where(system == 0, held, x0[1, k, row + half])
                        moved = turn_by(held, width * t - margin)
                        joint = jnp.where(lanes // width == t, moved, joint)
                    buf[b, n * groups + index] = joint
            return carry

        if parts <= 8:
            for b in range(parts):
                pack(b, 0)
        else:
            lax.fori_loop(0, parts, pack, 0)
        for copy in gifts(fields, buf, *rest):
            copy.start()

    outputs = (
        (PAIR, pair_buf, pair_in, pair_send, pair_recv, own_sem.at[2]),
        (REAL, real_buf, real_in, real_send, real_recv, own_sem.at[3]),
    )

    def both(step, carry):
        for output in outputs:
            fields = output[0]

            @pl.when(step > 0)
            def _():
                if ringed:
                    finish(fields)
                sweep(0, refs, fields, 1)

            cycle(refs, fields)

            @pl.when(step == 0)
            def _():
                if ringed:
                    exchange(fields)

            @pl.when(step > 0)
            def _():
                give(*output)

        return carry

    lax.fori_loop(0, 2, both, 0)
    for output in outputs:
        for copy in gifts(*output):
            copy.wait()

    for tile in range(regions // share):
        mixed = [[None] * block for _ in range(SECTIONS)]
        for q in range(groups):
            fields = []
            for n in range(share):
                first = 2 * (tile * share + n)
                fields.append(
                    [real_in[first + q // half, q % half]]
                    + [pair_in[first, k * groups + q] for k in (0, 1)]
                    + [pair_in[first + 1, k * groups + q] for k in (0, 1)]
                )
            for s in range(SECTIONS):
                sums = [
                    sum(transform[s][k] * fields[n][k] for k in range(SECTIONS))
                    for n in range(share)
                ]
                for t in range(share):
                    joint = zero
                    for n in range(share):
                        turn = (width * (n - t)) % LANES
                        moved = right_by(sums[n], turn) if turn else sums[n]
                        joint = jnp.where(lanes // width == n, moved, joint)
                    mixed[s][q + groups * t] = joint
        place = pl.ds(tile * LANES, LANES)
        for s in range(SECTIONS):
            turned = jnp.swapaxes(jnp.stack(mixed[s]), 0, 1)
            sections[s, :, :, place] = turned
            if s == SECTIONS - 1:
                next_voltage[:, :, place] = voltage[:, :, place] + turned


def local(voltage, capacity, node_class, via_sites, ball_sites, load_type, load_table):
    layers, block, wide = voltage.shape
    gx_count = lax.axis_size("gx")
    gy_count = lax.axis_size("gy")
    parts = lax.axis_size("section") * gx_count
    regions = parts // 2
    width = wide // regions
    margin = (LANES - width) // 2
    sizes = (parts, gx_count, gy_count, width, margin, wide * gy_count)
    rows = parts * block
    count = 4 * block + 1
    per_tile = LANES // margin
    packs = -(-3 * block // per_tile) - (-(block + 1) // per_tile)

    def vmem(*shape):
        return pltpu.VMEM(shape, jnp.float32)

    def levels(extra, *lead):
        return [vmem(*lead, rows // 4**m + extra, layers, LANES) for m in range(LEVELS)]

    mid = 1
    if margin < BOTH_CYCLES:
        first_sent, last_sent = exchanged(margin)
        mid = -(-rows // (LANES // (last_sent - first_sent)))
    groups = block * width // LANES
    scratch = [
        pltpu.SMEM(load_table.shape[::-1], jnp.float32),
        vmem(*voltage.shape),
        vmem(*capacity.shape),
        pltpu.VMEM(node_class.shape, jnp.int32),
        pltpu.VMEM(via_sites.shape, jnp.int32),
        pltpu.VMEM(ball_sites.shape, jnp.int32),
        pltpu.VMEM(load_type.shape, jnp.int32),
        vmem(count, layers, wide),
        vmem(2, packs, layers, LANES),
        vmem(2, parts, packs, layers, LANES),
        vmem(regions, count, layers, LANES),
        vmem(parts, count, layers, LANES),
        vmem(3, parts, block, LANES),
        *levels(1),
        *levels(0, COEFFS),
        *levels(2, 2, 3),
        *levels(0, 3),
        vmem(2, 3, mid, layers, LANES),
        vmem(2, 3, mid, layers, LANES),
        *[vmem(parts, 2 * groups, layers, LANES)] * 2,
        *[vmem(parts, max(groups // 2, 1), layers, LANES)] * 2,
        pltpu.SemaphoreType.DMA((7,)),
        pltpu.SemaphoreType.DMA((2, 2, -(-margin // width))),
        *[pltpu.SemaphoreType.DMA((2, 2, regions))] * 3,
        *[pltpu.SemaphoreType.DMA((2, regions))] * 4,
        pltpu.SemaphoreType.DMA((4,)),
        pltpu.SemaphoreType.DMA((4,)),
        *[pltpu.SemaphoreType.DMA((parts,))] * 4,
        pltpu.SemaphoreType.DMA((4,)),
    ]
    grant = 4 * 1024 * 1024
    for part in scratch:
        if "vmem" in str(part.memory_space).lower():
            grant += 4 * math.prod(part.shape)
    arguments = (load_table.T, voltage, capacity, node_class, via_sites, ball_sites, load_type)
    found = pl.pallas_call(
        functools.partial(kernel, sizes, radau_tables()),
        out_shape=(
            jax.ShapeDtypeStruct((SECTIONS, layers, block, wide), jnp.float32),
            jax.ShapeDtypeStruct((layers, block, wide), jnp.float32),
        ),
        in_specs=[
            *[pl.BlockSpec(memory_space=pl.ANY)] * 7,
        ],
        out_specs=(
            pl.BlockSpec(memory_space=pltpu.VMEM),
            pl.BlockSpec(memory_space=pltpu.VMEM),
        ),
        scratch_shapes=scratch,
        compiler_params=pltpu.CompilerParams(
            collective_id=0, has_side_effects=True, vmem_limit_bytes=grant
        ),
    )(*[pltpu.with_memory_space_constraint(a, pltpu.MemorySpace.HBM) for a in arguments])

    def hand_out(first, second, first_out, second_out, sem):
        copies = [
            pltpu.make_async_copy(first, first_out, sem.at[0]),
            pltpu.make_async_copy(second, second_out, sem.at[1]),
        ]
        for copy in copies:
            copy.start()
        for copy in copies:
            copy.wait()

    return pl.pallas_call(
        hand_out,
        out_shape=tuple(jax.ShapeDtypeStruct(a.shape, a.dtype) for a in found),
        in_specs=[pl.BlockSpec(memory_space=pl.ANY)] * 2,
        out_specs=tuple(pl.BlockSpec(memory_space=pl.ANY) for _ in found),
        scratch_shapes=[pltpu.SemaphoreType.DMA((2,))],
        compiler_params=pltpu.CompilerParams(vmem_limit_bytes=1024 * 1024),
    )(*found)


def solution(mesh):
    return jax.shard_map(
        local,
        mesh=mesh,
        in_specs=(
            P(None, row_axes, "gy"),
            P(None, row_axes, "gy"),
            P(None, row_axes, "gy"),
            P(None, row_axes, "gy"),
            P(row_axes, "gy"),
            P(row_axes, "gy"),
            P(),
        ),
        out_specs=(P(None, None, row_axes, "gy"), P(None, row_axes, "gy")),
        check_vma=False,
    )
```

```python
import functools
import math

import jax
import jax.numpy as jnp
from jax import lax
from jax.experimental import pallas as pl
from jax.experimental.pallas import tpu as pltpu
from jax.sharding import PartitionSpec as P

SECTIONS = 5
LEVELS = 3
LOADS = 16
LANES = 128
BOTH_CYCLES = 56
STEP = 32
REAL = (0,)
PAIR = (1, 2)
GX, GY, GV, GY_LOW, GV_LOW, W_REAL, W_SAME, W_MATE, D_REAL, D_SAME, D_MATE, GROUND, CAP, TOTAL = range(14)
COEFFS = 14

node_table = (0.35, 0.55, 0.8, 1.1, 1.5, 2.0, 2.7, 3.6)
via_conductance = 2.5
ball_conductance = 4.0
damping = 0.8
slab_partner = (0, 2, 1, 4, 3)
row_axes = ("section", "gx")


def pair_times(first, second):
    return (
        first[0] * second[0] - first[1] * second[1],
        first[0] * second[1] + first[1] * second[0],
    )


def pair_over(first, second):
    divisor = second[0] * second[0] + second[1] * second[1]
    return (
        (first[0] * second[0] + first[1] * second[1]) / divisor,
        (first[1] * second[0] - first[0] * second[1]) / divisor,
    )


def pair_minus(first, second):
    return (first[0] - second[0], first[1] - second[1])


def poly_value(coeffs, point):
    total = (0.0, 0.0)
    for c in reversed(coeffs):
        total = pair_times(total, point)
        total = (total[0] + c, total[1])
    return total


def poly_product(first, second):
    result = [0.0] * (len(first) + len(second) - 1)
    for i in range(len(first)):
        for j in range(len(second)):
            result[i + j] = result[i + j] + first[i] * second[j]
    return result


def poly_roots(coeffs):
    leading = coeffs[-1]
    scaled = [c / leading for c in coeffs]
    degree = len(coeffs) - 1
    guesses = []
    current = (1.0, 0.0)
    for k in range(degree):
        guesses.append(current)
        current = pair_times(current, (0.4, 0.9))
    for repeat_index in range(800):
        for k in range(degree):
            divisor = (1.0, 0.0)
            for j in range(degree):
                if j != k:
                    divisor = pair_times(divisor, pair_minus(guesses[k], guesses[j]))
            guesses[k] = pair_minus(guesses[k], pair_over(poly_value(scaled, guesses[k]), divisor))
    return guesses


def matrix_product(first, second):
    return [
        [
            sum((first[i][k] * second[k][j] for k in range(len(second))))
            for j in range(len(second[0]))
        ]
        for i in range(len(first))
    ]


def matrix_inverse(matrix):
    order = len(matrix)
    work = [list(matrix[i]) + [1.0 if i == j else 0.0 for j in range(order)] for i in range(order)]
    for column in range(order):
        pivot = column
        for i in range(column + 1, order):
            if abs(work[i][column]) > abs(work[pivot][column]):
                pivot = i
        work[column], work[pivot] = (work[pivot], work[column])
        factor = work[column][column]
        work[column] = [entry / factor for entry in work[column]]
        for i in range(order):
            if i != column:
                scale_row = work[i][column]
                work[i] = [work[i][j] - scale_row * work[column][j] for j in range(2 * order)]
    return [row[order:] for row in work]


def eigen_vector(matrix, value):
    order = len(matrix)
    size_inner = order - 1
    system = []
    for i in range(size_inner):
        row = []
        for j in range(order):
            entry = (matrix[i][j], 0.0)
            if i == j:
                entry = pair_minus(entry, value)
            row.append(entry)
        row[order - 1] = (-row[order - 1][0], -row[order - 1][1])
        system.append(row)
    for column in range(size_inner):
        pivot = column
        for i in range(column + 1, size_inner):
            left_size = system[i][column][0] ** 2 + system[i][column][1] ** 2
            right_size = system[pivot][column][0] ** 2 + system[pivot][column][1] ** 2
            if left_size > right_size:
                pivot = i
        system[column], system[pivot] = (system[pivot], system[column])
        for i in range(size_inner):
            if i != column:
                factor = pair_over(system[i][column], system[column][column])
                system[i] = [
                    pair_minus(system[i][j], pair_times(factor, system[column][j]))
                    for j in range(order)
                ]
    vector = [pair_over(system[i][order - 1], system[i][i]) for i in range(size_inner)]
    vector.append((1.0, 0.0))
    return vector


def radau_tables():
    section_count = 5
    generator = [1.0]
    for k in range(section_count - 1):
        generator = poly_product(generator, [0.0, 1.0])
    for k in range(section_count):
        generator = poly_product(generator, [-1.0, 1.0])
    for k in range(section_count - 1):
        generator = [j * generator[j] for j in range(1, len(generator))]
    abscissae = sorted((root[0] for root in poly_roots(generator)))
    vander = [[abscissae[i] ** j for j in range(section_count)] for i in range(section_count)]
    integrals = [
        [abscissae[i] ** (j + 1) / (j + 1) for j in range(section_count)]
        for i in range(section_count)
    ]
    butcher = matrix_product(integrals, matrix_inverse(vander))
    inverse = matrix_inverse(butcher)
    coeffs = [0.0] * (section_count + 1)
    coeffs[section_count] = 1.0
    current = [[0.0] * section_count for _ in range(section_count)]
    for k in range(1, section_count + 1):
        current = matrix_product(inverse, current)
        for i in range(section_count):
            current[i][i] = current[i][i] + coeffs[section_count - k + 1]
        applied = matrix_product(inverse, current)
        coeffs[section_count - k] = -sum((applied[i][i] for i in range(section_count))) / k
    eigen_values = poly_roots(coeffs)
    real_pick = 0
    for k in range(section_count):
        if abs(eigen_values[k][1]) < abs(eigen_values[real_pick][1]):
            real_pick = k
    upper_half = [k for k in range(section_count) if eigen_values[k][1] > 1e-09]
    upper_half = sorted(upper_half, key=lambda k: -eigen_values[k][0])
    columns = [[entry[0] for entry in eigen_vector(inverse, (eigen_values[real_pick][0], 0.0))]]
    for k in upper_half:
        vector = eigen_vector(inverse, eigen_values[k])
        columns.append([entry[0] for entry in vector])
        columns.append([entry[1] for entry in vector])
    transform = [[columns[j][i] for j in range(section_count)] for i in range(section_count)]
    inverse_transform = matrix_inverse(transform)
    blocks = matrix_product(matrix_product(inverse_transform, inverse), transform)
    diagonal = [blocks[k][k] for k in range(section_count)]
    coupling = [
        blocks[k][slab_partner[k]] if slab_partner[k] != k else 0.0 for k in range(section_count)
    ]
    return (transform, inverse_transform, diagonal, coupling)


def left_by(value, count):
    return pltpu.roll(value, LANES - count, axis=1)


def right_by(value, count):
    return pltpu.roll(value, count, axis=1)


def from_above(value):
    return pltpu.roll(value, value.shape[0] - 1, axis=0)


def from_below(value):
    return pltpu.roll(value, 1, axis=0)


def lane_ids(layers):
    return lax.broadcasted_iota(jnp.int32, (layers, LANES), 1)


def layer_ids(layers):
    return lax.broadcasted_iota(jnp.int32, (layers, LANES), 0)


def is_low(layers, stride):
    return (lane_ids(layers) // stride) % 2 == 0


def blocks(count, step, body):
    if count <= step:
        body(0)
        return

    def one(b, carry):
        body(b * step)
        return carry

    lax.fori_loop(0, count // step, one, 0)


def seam_low(level, value):
    if level == 1:
        return right_by(value, 1)
    return jnp.where(is_low(value.shape[0], 2), left_by(value, 1), right_by(value, 2))


def seam_high(level, value):
    if level == 1:
        return left_by(value, 1)
    return jnp.where(is_low(value.shape[0], 2), left_by(value, 2), right_by(value, 1))


def merge(low, stride, first, second):
    return jnp.where(low, first + left_by(first, stride), second + right_by(second, stride))


def weights(cap, total, lam0, alpha, beta):
    real = lam0 * cap + total
    mate = beta * cap
    both = alpha * cap + total
    scale = damping / (both * both + mate * mate)
    return damping / real, both * scale, mate * scale, real, both, mate


def reach(valid):
    once = -(-(valid + 2) // 2)
    twice = -(-(once + 2) // 2)
    return 2 * (2 * (twice + 3) + 2) + 2


def exchanged(margin):
    first = 0
    while reach(first + 2) <= margin:
        first += 1
    return first, reach(1)


def solve_node(fields, weight, values):
    if fields == REAL:
        return (weight[0] * values[0],)
    return (
        weight[1] * values[0] - weight[2] * values[1],
        weight[1] * values[1] + weight[2] * values[0],
    )


def sweep(level, refs, fields, source, restrict=False):
    edge, g, x, f = refs[level]
    tiles, layers = f.shape[1], f.shape[2]
    stride = 2**level
    half = tiles // 2
    step = min(STEP, half)
    target = 1 - source
    if level:
        for k in fields:
            x[source, k, 0] = seam_low(level, x[source, k, tiles])
            x[source, k, tiles + 1] = seam_high(level, x[source, k, 1])

    def part(begin):
        found = []
        xs = [[x[source, k, begin + r] for r in range(step + 2)] for k in fields]
        for r in range(step):
            i = begin + r
            ahead, behind = edge[i + 1], edge[i]
            gy, gy_low, gv, gv_low = g[GY, i], g[GY_LOW, i], g[GV, i], g[GV_LOW, i]
            here = [xs[n][r + 1] for n in range(len(fields))]
            values = []
            for n, k in enumerate(fields):
                along = ahead * xs[n][r + 2] + behind * xs[n][r]
                across = gy * left_by(here[n], stride) + gy_low * right_by(here[n], stride)
                through = gv * from_above(here[n]) + gv_low * from_below(here[n])
                values.append((f[k, i] + along) + (across + through))
            if not restrict:
                if fields == REAL:
                    weight = (g[W_REAL, i],)
                else:
                    weight = (None, g[W_SAME, i], g[W_MATE, i])
                change = solve_node(fields, weight, values)
                found.append([(1.0 - damping) * here[n] + change[n] for n in range(len(fields))])
            elif fields == REAL:
                found.append([values[0] - g[D_REAL, i] * here[0]])
            else:
                same, mate = g[D_SAME, i], g[D_MATE, i]
                found.append(
                    [
                        values[0] - same * here[0] - mate * here[1],
                        values[1] - same * here[1] + mate * here[0],
                    ]
                )
        return found

    def body(start):
        parts = [part(start), part(half + start)]
        if not restrict:
            for p in range(2):
                for r in range(step):
                    for n, k in enumerate(fields):
                        x[target, k, p * half + start + r + 1] = parts[p][r][n]
            return
        edge_next, g_next, x_next, f_next = refs[level + 1]
        low = is_low(layers, stride)
        for r in range(0, step, 2):
            i = start // 2 + r // 2
            summed = [
                merge(
                    low,
                    stride,
                    parts[0][r][n] + parts[0][r + 1][n],
                    parts[1][r][n] + parts[1][r + 1][n],
                )
                for n in range(len(fields))
            ]
            weight = [g_next[w, i] for w in (W_REAL, W_SAME, W_MATE)]
            first = solve_node(fields, weight, summed)
            for n, k in enumerate(fields):
                f_next[k, i] = summed[n]
                x_next[0, k, i + 1] = first[n]

    blocks(half, step, body)


def prolong(level, refs, fields, target):
    x, f = refs[level][2:]
    x_next, f_next = refs[level + 1][2:]
    layers = f.shape[2]
    stride = 2**level
    half = f.shape[1] // 2
    count = f_next.shape[1]
    step = min(STEP, count)

    def body(start):
        low = is_low(layers, stride)
        for r in range(step):
            for k in fields:
                coarse = x_next[1, k, start + r + 1]
                both = (
                    jnp.where(low, coarse, right_by(coarse, stride)),
                    jnp.where(low, left_by(coarse, stride), coarse),
                )
                for p in range(2):
                    for t in range(2):
                        row = p * half + 2 * (start + r) + t + 1
                        x[target, k, row] = x[target, k, row] + both[p]

    blocks(count, step, body)


def coarsen(level, refs, scal):
    edge, g = refs[level][:2]
    edge_next, g_next = refs[level + 1][:2]
    layers = g.shape[2]
    stride = 2**level
    half = g.shape[1] // 2
    count = g_next.shape[1]
    step = min(STEP, count)

    def cross(start):
        low = is_low(layers, stride)
        for r in range(step):
            j = 2 * (start + r) + 2
            edge_next[start + r + 1] = merge(low, stride, edge[j], edge[half + j])

    blocks(count, step, cross)
    first = seam_low(level + 1, edge_next[count])
    edge_next[0] = jnp.where(lane_ids(layers) % (2 * stride) == 0, 0.0, first)

    def body(start):
        low = is_low(layers, stride)
        for r in range(step):
            i = start + r
            j = 2 * i

            def summed(plane, p):
                return g[plane, p * half + j] + g[plane, p * half + j + 1]

            def joined(plane):
                return merge(low, stride, summed(plane, 0), summed(plane, 1))

            gy = jnp.where(low, left_by(summed(GY, 0), stride), summed(GY, 1))
            gv, ground, cap = joined(GV), joined(GROUND), joined(CAP)
            gy_low, gv_low = right_by(gy, 2 * stride), from_below(gv)
            total = (edge_next[i + 1] + edge_next[i]) + (gy + gy_low) + (gv + gv_low) + ground
            found = weights(cap, total, *scal)
            for k, entry in enumerate((gy, gv, gy_low, gv_low) + found + (ground, cap)):
                g_next[k + 1, i] = entry

    blocks(count, step, body)


def cycle(refs, fields):
    sweep(0, refs, fields, 0)
    sweep(0, refs, fields, 1, restrict=True)
    sweep(1, refs, fields, 0)
    sweep(1, refs, fields, 1, restrict=True)
    for n in range(3):
        sweep(2, refs, fields, n % 2)
    prolong(1, refs, fields, 1)
    sweep(1, refs, fields, 1)
    sweep(1, refs, fields, 0)
    prolong(0, refs, fields, 1)
    sweep(0, refs, fields, 1)
    sweep(0, refs, fields, 0)


def kernel(
    sizes, tables, load_table_in, voltage_in, capacity_in, node_class_in, via_sites_in,
    ball_sites_in, load_type_in, sections, next_voltage,
    load_table, voltage, capacity, node_class, via_sites, ball_sites, load_type,
    planes, edge, edge_in, send, recv, surf, e0, e1, e2, g0, g1, g2, x0, x1, x2, f0, f1, f2,
    packed, landed, pair_buf, pair_in, real_buf, real_in,
    load_sem, edge_send, edge_recv, edge_pass_send, edge_pass_recv, send_sem, recv_sem, pass_send, pass_recv,
    ring_send, ring_recv, pair_send, pair_recv, real_send, real_recv, own_sem,
):
    parts, gx_count, gy_count, width, margin, columns = sizes
    transform, inverse_transform, diagonal, coupling = tables
    layers = voltage.shape[0]
    block = voltage.shape[1]
    wide = voltage.shape[2]
    tiles = wide // LANES
    regions = parts // 2
    count = 4 * block + 1
    section_here = lax.axis_index("section")
    gx_here = lax.axis_index("gx")
    gy_here = lax.axis_index("gy")
    mine = section_here * gx_count + gx_here
    system = section_here % 2
    all_regions = regions * gy_count

    def snake(place, row):
        return place + (row % 2) * (gx_count - 1 - 2 * place)

    def turned(place, column):
        return place + (column % 2) * (regions - 1 - 2 * place)

    pair = section_here // 2
    spot = turned(pair * gx_count + snake(gx_here, pair), gy_here)
    region = gy_here * regions + spot

    def owner(place, column):
        found = turned(place, column)
        row = found // gx_count
        return row * 2 + system, snake(found % gx_count, row)

    def group_device(index):
        return {"section": index // gx_count, "gx": index % gx_count}

    def region_device(index):
        column = index // regions
        owner_section, owner_gx = owner(index % regions, column)
        return {"section": owner_section, "gx": owner_gx, "gy": column}

    after = region_device((region + 1) % all_regions)
    before = region_device((region + all_regions - 1) % all_regions)
    has_after = region < all_regions - 1
    has_before = region > 0
    seat = pair * gx_count + gx_here
    over = -(-margin // width)
    sides = (
        (gy_here < gy_count - 1, gy_here + 1, range(over), gy_here > 0, gy_here - 1, spot < over),
        (
            gy_here > 0, gy_here - 1, range(regions - over, regions),
            gy_here < gy_count - 1, gy_here + 1, spot >= regions - over,
        ),
    )
    partner = {"section": section_here + 1 - 2 * system}

    barrier = pltpu.get_barrier_semaphore()

    def greet(place):
        pl.semaphore_signal(
            barrier, inc=1, device_id=place, device_id_type=pl.DeviceIdType.MESH
        )

    for d in range(1, parts):
        greet(group_device((mine + d) % parts))
    greeted = parts - 1
    for sends, to_column, reach, comes, from_column, reached in sides:
        greeted = greeted + jnp.where(sends, over, 0)

        @pl.when(jnp.logical_and(comes, reached))
        def _():
            for place in range(regions):
                greet(
                    {
                        "section": place // gx_count * 2 + system,
                        "gx": place % gx_count,
                        "gy": from_column,
                    }
                )

    if margin < BOTH_CYCLES:
        for exists, place in ((has_after, after), (has_before, before)):
            greeted = greeted + exists.astype(jnp.int32)

            @pl.when(exists)
            def _():
                greet(place)

    fetches = []
    for n, (whole, here) in enumerate(
        (
            (node_class_in, node_class),
            (via_sites_in, via_sites),
            (ball_sites_in, ball_sites),
            (load_type_in, load_type),
            (voltage_in, voltage),
            (capacity_in, capacity),
            (load_table_in, load_table),
        )
    ):
        copy = pltpu.make_async_copy(whole, here, load_sem.at[n])
        copy.start()
        fetches.append(copy)
    for copy in fetches:
        copy.wait()

    def remote(source, target, source_sem, target_sem, place):
        return pltpu.make_async_remote_copy(
            src_ref=source,
            dst_ref=target,
            send_sem=source_sem,
            recv_sem=target_sem,
            device_id=place,
            device_id_type=pl.DeviceIdType.MESH,
        )

    lanes = lane_ids(layers)
    zero = jnp.zeros((layers, LANES), jnp.float32)

    def turn_by(value, amount):
        amount = amount % LANES
        return right_by(value, amount) if amount else value

    for tile in range(tiles):
        place = pl.ds(tile * LANES, LANES)
        kind = node_class[:, :, place]
        resist = jnp.full(kind.shape, 0.5 / node_table[0], jnp.float32)
        for k in range(1, len(node_table)):
            resist = jnp.where(kind == k, jnp.float32(0.5 / node_table[k]), resist)
        via = jnp.where(via_sites[:, :, place] == 1, jnp.float32(via_conductance), 0.0)
        ball = jnp.where(ball_sites[:, place] == 1, jnp.float32(ball_conductance), 0.0)
        sites = jnp.concatenate([via, ball[None]], axis=0)
        for k, value in enumerate((capacity[:, :, place], resist, sites, voltage[:, :, place])):
            swapped = jnp.swapaxes(value, 0, 1)
            for r in range(block):
                planes[k * block + r, :, place] = swapped[r]
        planes[4 * block, :, place] = load_type[:, place].astype(jnp.float32)

    share = LANES // margin
    lots = []
    begin = 0
    for first, size in ((0, 3 * block), (3 * block, block + 1)):
        packs = -(-size // share)
        lots.append((first, size, begin, packs))
        begin += packs

    def pack_edges(lot):
        first, size, base, packs = lots[lot]
        for side, begin in ((0, LANES - margin), (1, 0)):
            place = pl.ds((tiles - 1) * LANES if side == 0 else 0, LANES)
            for q in range(packs):
                joint = zero
                for t in range(share):
                    plane = q + packs * t
                    if plane < size:
                        moved = turn_by(planes[first + plane, :, place], margin * t - begin)
                        joint = jnp.where(lanes // margin == t, moved, joint)
                edge[side, base + q] = joint

    def edge_copy(lot, side, n, place):
        tiles_here = pl.ds(*lots[lot][2:])
        return remote(
            edge.at[side, tiles_here], edge_in.at[side, mine, tiles_here],
            edge_send.at[lot, side, n], edge_recv.at[lot, side, seat], place,
        )

    def edge_places(side):
        to_column, reach = sides[side][1:3]
        for n, k in enumerate(reach):
            owner_section, owner_gx = owner(k, to_column)
            yield n, {"section": owner_section, "gx": owner_gx, "gy": to_column}

    def send_edges(lot):
        for side in range(2):

            @pl.when(sides[side][0])
            def _():
                for n, place in edge_places(side):
                    edge_copy(lot, side, n, place).start()

    quarter = LANES // 4
    slim = [
        k
        for k in range(regions)
        if quarter in (margin - width * k, margin - width * (regions - 1 - k))
    ]

    def piece(k, t):
        if margin - width * k == quarter:
            return quarter * (t + 1), 0
        return quarter * t, LANES - quarter

    def carriers(lot):
        return lots[lot][1] - lots[lot][1] // 4

    def part(lot, thin):
        return pl.ds(lots[lot][0], carriers(lot) if thin else lots[lot][1])

    def by_kind(place, act):
        if not slim:
            act(False)
            return
        thin = place == slim[0]
        for k in slim[1:]:
            thin = jnp.logical_or(thin, place == k)

        @pl.when(thin)
        def _():
            act(True)

        @pl.when(jnp.logical_not(thin))
        def _():
            act(False)

    def build(lot, k):
        start = width * k - margin
        first, size = lots[lot][:2]
        window = []
        for plane in range(first, first + size):
            joint = None
            for tile in range(tiles):
                low = tile * LANES
                if low + LANES <= start or low >= start + LANES:
                    continue
                moved = turn_by(planes[plane, :, pl.ds(low, LANES)], low - start)
                joint = moved if joint is None else jnp.where(lanes >= low - start, moved, joint)
            window.append(joint)
        count_sent = carriers(lot) if k in slim else size
        for c in range(count_sent):
            joint = window[c]
            if k in slim and count_sent + c // 3 < size:
                source, target = piece(k, c % 3)
                carried = turn_by(window[count_sent + c // 3], target - source)
                joint = jnp.where(lanes // quarter == target // quarter, carried, joint)
            send[k, first + c] = joint

    def direct(lot, d, k, thin):
        owner_section, owner_gx = owner(k, gy_here)
        return remote(
            send.at[k, part(lot, thin)], recv.at[mine, part(lot, thin)],
            send_sem.at[lot, d], recv_sem.at[lot, d],
            {"section": owner_section, "gx": owner_gx},
        )

    def handed(lot, d, source, slot, thin):
        return remote(
            source.at[part(lot, thin)], recv.at[slot, part(lot, thin)],
            pass_send.at[lot, d], pass_recv.at[lot, d], partner,
        )

    def own(lot, thin):
        return pltpu.make_async_copy(
            send.at[spot, part(lot, thin)], recv.at[mine, part(lot, thin)], own_sem.at[lot]
        )

    def dispatch(lot, k):
        d = (k - spot + regions) % regions

        @pl.when(d != 0)
        def _():
            direct(lot, d, k, k in slim).start()

        @pl.when(d == 0)
        def _():
            own(lot, k in slim).start()
            handed(lot, 0, send.at[k], mine, k in slim).start()

    ends = [k for k in range(regions) if k < over or k >= regions - over]
    order = ends + [k for k in range(regions) if k not in ends]
    for lot in range(2):
        pack_edges(lot)
        for k in order:
            build(lot, k)
    pl.semaphore_wait(barrier, greeted)
    for lot in range(2):
        send_edges(lot)
        for k in order:
            dispatch(lot, k)

    def pick(table):
        return [
            jnp.where(system == 0, jnp.float32(table[a]), jnp.float32(table[b]))
            for a, b in ((0, 0), (1, 3), (2, 4))
        ]

    shifts = pick(diagonal)
    lam0, alpha, beta = shifts[0], shifts[1], pick(coupling)[1]
    shares = pick([sum(row) for row in inverse_transform])
    mixing = [pick([row[j] for row in inverse_transform]) for j in range(SECTIONS)]
    scal = (lam0, alpha, beta)
    for slot in range(2):
        for k in range(3):
            x0[slot, k, 0] = zero
            x0[slot, k, x0.shape[2] - 1] = zero
    e0[0] = zero

    def edge_slot(place):
        return (place // gx_count * 2 + system) * gx_count + place % gx_count

    def edge_handed(lot, side, place):
        landing = edge_in.at[side, edge_slot(place), pl.ds(*lots[lot][2:])]
        return remote(
            landing, landing, edge_pass_send.at[lot, side, place],
            edge_pass_recv.at[lot, side, place], partner,
        )

    nearest = [*range(1, regions, 2), *range(2, regions, 2)]

    def slot_from(d):
        owner_section, owner_gx = owner((spot - d + regions) % regions, gy_here)
        return owner_section * gx_count + owner_gx

    def take(lot):
        def block(d):
            def act(thin):
                direct(lot, d, (spot + d) % regions, thin).wait_recv()
                slot = slot_from(d)
                handed(lot, d, recv.at[slot], slot, thin).start()

            by_kind(spot, act)

        for d in nearest[: regions // 2]:
            block(d)
        for side, (sends, _, _, comes, _, reached) in enumerate(sides):

            @pl.when(jnp.logical_and(comes, reached))
            def _():
                tiles_here = pl.ds(*lots[lot][2:])
                for place in range(regions):
                    remote(
                        edge.at[side, tiles_here], edge_in.at[side, edge_slot(place), tiles_here],
                        edge_send.at[lot, side, 0], edge_recv.at[lot, side, place], partner,
                    ).wait_recv()
                    edge_handed(lot, side, place).start()

        for d in nearest[regions // 2 :]:
            block(d)

    def settle(lot):
        first, size, base, packs = lots[lot]
        for d in nearest:
            target = (spot + d) % regions
            by_kind(target, lambda thin: direct(lot, d, target, thin).wait_send())

        def act(thin):
            own(lot, thin).wait()
            handed(lot, 0, send.at[spot], mine, thin).wait()
            for d in nearest:
                slot = slot_from(d)
                handed(lot, d, recv.at[slot], slot, thin).wait()

        by_kind(spot, act)
        for side, (sends, _, _, comes, _, reached) in enumerate(sides):

            @pl.when(sends)
            def _():
                for n, place in edge_places(side):
                    edge_copy(lot, side, n, place).wait_send()

            @pl.when(jnp.logical_and(comes, reached))
            def _():
                for place in range(regions):
                    edge_handed(lot, side, place).wait()

            for k in sides[side][2]:
                start = width * k - margin
                outside = lanes < -start if side == 0 else lanes >= wide - start

                def patch(b, edged):
                    held = [recv[b, first + c] for c in range(size)]
                    if k in slim:
                        count_sent = carriers(lot)
                        for c in range(3 * (size - count_sent)):
                            source, target = piece(k, c % 3)
                            moved = turn_by(held[c], source - target)
                            base_tile = held[count_sent + c // 3] if c % 3 else held[c]
                            held[count_sent + c // 3] = jnp.where(
                                lanes // quarter == source // quarter, moved, base_tile
                            )
                    changed = range(size) if edged else range(carriers(lot), size)
                    for plane in changed:
                        joint = held[plane]
                        if edged:
                            q, t = plane % packs, plane // packs
                            low = -margin if side == 0 else wide
                            moved = turn_by(edge_in[side, b, base + q], low - start - margin * t)
                            joint = jnp.where(outside, moved, joint)
                        recv[b, first + plane] = joint

                def run(edged):
                    once = 8 if lot else 4

                    def some_blocks(c, carry):
                        for b in range(once):
                            patch(once * c + b, edged)
                        return carry

                    lax.fori_loop(0, parts // once, some_blocks, 0)

                @pl.when(jnp.logical_and(comes, spot == k))
                def _():
                    run(True)

                if k in slim:

                    @pl.when(jnp.logical_and(jnp.logical_not(comes), spot == k))
                    def _():
                        run(False)

    rows = parts * block
    level_of = layer_ids(layers)
    column = region * width - margin + lanes
    inside = (column >= 0) & (column < columns)
    joined = inside & (column < columns - 1) & (lanes < LANES - 1)

    def coefficients(c, behind_gx):
        for b in (2 * c, 2 * c + 1):
            following = jnp.minimum(b + 1, parts - 1)
            for r in range(block):
                i = b * block + r
                cap, sites = recv[b, r], recv[b, 2 * block + r]
                resist = jnp.where(inside, recv[b, block + r], 0.5)
                if r + 1 < block:
                    resist_ahead = recv[b, block + r + 1]
                else:
                    resist_ahead = recv[following, block]
                resist_ahead = jnp.where(inside, resist_ahead, 0.5)
                gx = 1.0 / (resist + resist_ahead)
                if r + 1 == block:
                    gx = gx * (b < parts - 1).astype(jnp.float32)
                gy = jnp.where(joined, 1.0 / (resist + left_by(resist, 1)), 0.0)
                gv = jnp.where(level_of < layers - 1, sites, 0.0)
                ground = jnp.where(level_of == 0, from_below(sites), 0.0)
                gy_low, gv_low = right_by(gy, 1), from_below(gv)
                total = (gx + behind_gx) + (gy + gy_low) + (gv + gv_low) + ground
                found = weights(cap, total, *scal)
                e0[i + 1] = gx
                for k, entry in enumerate((gy, gv, gy_low, gv_low) + found + (ground, cap, total)):
                    g0[k + 1, i] = entry
                behind_gx = gx
        return behind_gx

    def forcing(c, volt_behind):
        for b in (4 * c, 4 * c + 1, 4 * c + 2, 4 * c + 3):
            kind = recv[b, 4 * block]
            currents = [zero] * SECTIONS
            for t in range(LOADS):
                here = kind == float(t)
                for j in range(SECTIONS):
                    currents[j] = jnp.where(here, load_table[j, t], currents[j])
            for k in range(3):
                surf[k, b] = sum(mixing[j][k] * currents[j] for j in range(SECTIONS))
        for b in (4 * c, 4 * c + 1, 4 * c + 2, 4 * c + 3):
            following = jnp.minimum(b + 1, parts - 1)
            for r in range(block):
                i = b * block + r
                volt = recv[b, 3 * block + r]
                if r + 1 < block:
                    volt_ahead = recv[b, 3 * block + r + 1]
                else:
                    volt_ahead = recv[following, 3 * block]
                pulled = (
                    (e0[i + 1] * volt_ahead + e0[i] * volt_behind)
                    + (g0[GY, i] * left_by(volt, 1) + g0[GY_LOW, i] * right_by(volt, 1))
                    + (g0[GV, i] * from_above(volt) + g0[GV_LOW, i] * from_below(volt))
                )
                leak = g0[TOTAL, i] * volt - pulled
                source = [
                    jnp.where(
                        level_of == layers - 1,
                        jnp.broadcast_to(surf[k, b, r : r + 1, :], (layers, LANES)),
                        0.0,
                    )
                    - shares[k] * leak
                    for k in range(3)
                ]
                found = [g0[w, i] for w in (W_REAL, W_SAME, W_MATE)]
                first = solve_node(REAL, found, source[:1]) + solve_node(PAIR, found, source[1:])
                for k in range(3):
                    f0[k, i] = source[k]
                    x0[0, k, i + 1] = first[k]
                volt_behind = volt
        return volt_behind

    take(0)
    settle(0)
    behind = lax.fori_loop(0, parts // 4, coefficients, zero)
    take(1)
    lax.fori_loop(parts // 4, parts // 2, coefficients, behind)
    refs = ((e0, g0, x0, f0), (e1, g1, x1, f1), (e2, g2, x2, f2))
    coarsen(0, refs, scal)
    coarsen(1, refs, scal)
    settle(1)
    lax.fori_loop(0, parts // 4, forcing, zero)

    ringed = margin < BOTH_CYCLES
    first_sent, last_sent = exchanged(margin) if ringed else (0, margin)
    sent = last_sent - first_sent
    ring_share = LANES // sent
    ring_groups = -(-rows // ring_share)

    def ring_copies(fields):
        span = pl.ds(fields[0], len(fields))
        for side, exists, came, place in (
            (0, has_after, has_before, after),
            (1, has_before, has_after, before),
        ):
            slot = 2 * (len(fields) - 1) + side
            yield exists, came, remote(
                packed.at[side, span], landed.at[side, span],
                ring_send.at[slot], ring_recv.at[slot], place,
            )

    def exchange(fields):
        for q in range(ring_groups):
            for side, begin in ((0, width + first_sent), (1, LANES - width - last_sent)):
                for k in fields:
                    joint = None
                    for t in range(ring_share):
                        row = q + ring_groups * t
                        if row < rows:
                            moved = turn_by(x0[1, k, row + 1], sent * t - begin)
                            joint = moved if t == 0 else jnp.where(lanes >= sent * t, moved, joint)
                    packed[side, k, q] = joint
        for exists, came, copy in ring_copies(fields):

            @pl.when(exists)
            def _():
                copy.start()

    def finish(fields):
        for exists, came, copy in ring_copies(fields):

            @pl.when(exists)
            def _():
                copy.wait_send()

            @pl.when(came)
            def _():
                copy.wait_recv()

        low = (lanes >= first_sent) & (lanes < jnp.where(has_before, last_sent, 0))
        high = (lanes < LANES - first_sent) & (
            lanes >= jnp.where(has_after, LANES - last_sent, LANES)
        )
        for q in range(ring_groups):
            for k in fields:
                from_low, from_high = landed[0, k, q], landed[1, k, q]
                for t in range(ring_share):
                    row = q + ring_groups * t
                    if row < rows:
                        below = turn_by(from_low, first_sent - sent * t)
                        above = turn_by(from_high, LANES - last_sent - sent * t)
                        held = jnp.where(high, above, x0[1, k, row + 1])
                        x0[1, k, row + 1] = jnp.where(low, below, held)

    share = LANES // width
    groups = block // share
    half = max(groups // 2, 1)
    halves = groups // half
    slot_out = spot * 2 + system

    def gifts(fields, buf, into, sends, recvs, own):
        for d in range(parts):
            peer = (mine + d) % parts
            if d == 0:
                yield pltpu.make_async_copy(buf.at[peer], into.at[slot_out], own)
            else:
                yield remote(
                    buf.at[peer], into.at[slot_out], sends.at[d], recvs.at[d], group_device(peer)
                )

    def give(fields, buf, *rest):
        chosen = half if fields == REAL else groups

        def pack(b, carry):
            for n, k in enumerate(fields):
                for index in range(chosen):
                    joint = zero
                    for t in range(share):
                        row = b * block + index + groups * t + 1
                        held = x0[1, k, row]
                        if fields == REAL and halves > 1:
                            held = jnp.where(system == 0, held, x0[1, k, row + half])
                        moved = turn_by(held, width * t - margin)
                        joint = jnp.where(lanes // width == t, moved, joint)
                    buf[b, n * groups + index] = joint
            return carry

        if parts <= 8:
            for b in range(parts):
                pack(b, 0)
        else:
            lax.fori_loop(0, parts, pack, 0)
        for copy in gifts(fields, buf, *rest):
            copy.start()

    outputs = (
        (PAIR, pair_buf, pair_in, pair_send, pair_recv, own_sem.at[2]),
        (REAL, real_buf, real_in, real_send, real_recv, own_sem.at[3]),
    )

    def both(step, carry):
        for output in outputs:
            fields = output[0]

            @pl.when(step > 0)
            def _():
                if ringed:
                    finish(fields)
                sweep(0, refs, fields, 1)

            cycle(refs, fields)

            @pl.when(step == 0)
            def _():
                if ringed:
                    exchange(fields)

            @pl.when(step > 0)
            def _():
                give(*output)

        return carry

    lax.fori_loop(0, 2, both, 0)
    for output in outputs:
        for copy in gifts(*output):
            copy.wait()

    for tile in range(regions // share):
        mixed = [[None] * block for _ in range(SECTIONS)]
        for q in range(groups):
            fields = []
            for n in range(share):
                first = 2 * (tile * share + n)
                fields.append(
                    [real_in[first + q // half, q % half]]
                    + [pair_in[first, k * groups + q] for k in (0, 1)]
                    + [pair_in[first + 1, k * groups + q] for k in (0, 1)]
                )
            for s in range(SECTIONS):
                sums = [
                    sum(transform[s][k] * fields[n][k] for k in range(SECTIONS))
                    for n in range(share)
                ]
                for t in range(share):
                    joint = zero
                    for n in range(share):
                        turn = (width * (n - t)) % LANES
                        moved = right_by(sums[n], turn) if turn else sums[n]
                        joint = jnp.where(lanes // width == n, moved, joint)
                    mixed[s][q + groups * t] = joint
        place = pl.ds(tile * LANES, LANES)
        for s in range(SECTIONS):
            turned = jnp.swapaxes(jnp.stack(mixed[s]), 0, 1)
            sections[s, :, :, place] = turned
            if s == SECTIONS - 1:
                next_voltage[:, :, place] = voltage[:, :, place] + turned


def local(voltage, capacity, node_class, via_sites, ball_sites, load_type, load_table):
    layers, block, wide = voltage.shape
    gx_count = lax.axis_size("gx")
    gy_count = lax.axis_size("gy")
    parts = lax.axis_size("section") * gx_count
    regions = parts // 2
    width = wide // regions
    margin = (LANES - width) // 2
    sizes = (parts, gx_count, gy_count, width, margin, wide * gy_count)
    rows = parts * block
    count = 4 * block + 1
    per_tile = LANES // margin
    packs = -(-3 * block // per_tile) - (-(block + 1) // per_tile)

    def vmem(*shape):
        return pltpu.VMEM(shape, jnp.float32)

    def levels(extra, *lead):
        return [vmem(*lead, rows // 4**m + extra, layers, LANES) for m in range(LEVELS)]

    mid = 1
    if margin < BOTH_CYCLES:
        first_sent, last_sent = exchanged(margin)
        mid = -(-rows // (LANES // (last_sent - first_sent)))
    groups = block * width // LANES
    scratch = [
        pltpu.SMEM(load_table.shape[::-1], jnp.float32),
        vmem(*voltage.shape),
        vmem(*capacity.shape),
        pltpu.VMEM(node_class.shape, jnp.int32),
        pltpu.VMEM(via_sites.shape, jnp.int32),
        pltpu.VMEM(ball_sites.shape, jnp.int32),
        pltpu.VMEM(load_type.shape, jnp.int32),
        vmem(count, layers, wide),
        vmem(2, packs, layers, LANES),
        vmem(2, parts, packs, layers, LANES),
        vmem(regions, count, layers, LANES),
        vmem(parts, count, layers, LANES),
        vmem(3, parts, block, LANES),
        *levels(1),
        *levels(0, COEFFS),
        *levels(2, 2, 3),
        *levels(0, 3),
        vmem(2, 3, mid, layers, LANES),
        vmem(2, 3, mid, layers, LANES),
        *[vmem(parts, 2 * groups, layers, LANES)] * 2,
        *[vmem(parts, max(groups // 2, 1), layers, LANES)] * 2,
        pltpu.SemaphoreType.DMA((7,)),
        pltpu.SemaphoreType.DMA((2, 2, -(-margin // width))),
        *[pltpu.SemaphoreType.DMA((2, 2, regions))] * 3,
        *[pltpu.SemaphoreType.DMA((2, regions))] * 4,
        pltpu.SemaphoreType.DMA((4,)),
        pltpu.SemaphoreType.DMA((4,)),
        *[pltpu.SemaphoreType.DMA((parts,))] * 4,
        pltpu.SemaphoreType.DMA((4,)),
    ]
    grant = 4 * 1024 * 1024
    for part in scratch:
        if "vmem" in str(part.memory_space).lower():
            grant += 4 * math.prod(part.shape)
    arguments = (load_table.T, voltage, capacity, node_class, via_sites, ball_sites, load_type)
    found = pl.pallas_call(
        functools.partial(kernel, sizes, radau_tables()),
        out_shape=(
            jax.ShapeDtypeStruct((SECTIONS, layers, block, wide), jnp.float32),
            jax.ShapeDtypeStruct((layers, block, wide), jnp.float32),
        ),
        in_specs=[
            *[pl.BlockSpec(memory_space=pl.ANY)] * 7,
        ],
        out_specs=(
            pl.BlockSpec(memory_space=pltpu.VMEM),
            pl.BlockSpec(memory_space=pltpu.VMEM),
        ),
        scratch_shapes=scratch,
        compiler_params=pltpu.CompilerParams(
            collective_id=0, has_side_effects=True, vmem_limit_bytes=grant
        ),
    )(*[pltpu.with_memory_space_constraint(a, pltpu.MemorySpace.HBM) for a in arguments])

    def hand_out(first, second, first_out, second_out, sem):
        copies = [
            pltpu.make_async_copy(first, first_out, sem.at[0]),
            pltpu.make_async_copy(second, second_out, sem.at[1]),
        ]
        for copy in copies:
            copy.start()
        for copy in copies:
            copy.wait()

    return pl.pallas_call(
        hand_out,
        out_shape=tuple(jax.ShapeDtypeStruct(a.shape, a.dtype) for a in found),
        in_specs=[pl.BlockSpec(memory_space=pl.ANY)] * 2,
        out_specs=tuple(pl.BlockSpec(memory_space=pl.ANY) for _ in found),
        scratch_shapes=[pltpu.SemaphoreType.DMA((2,))],
        compiler_params=pltpu.CompilerParams(vmem_limit_bytes=1024 * 1024),
    )(*found)


def solution(mesh):
    return jax.shard_map(
        local,
        mesh=mesh,
        in_specs=(
            P(None, row_axes, "gy"),
            P(None, row_axes, "gy"),
            P(None, row_axes, "gy"),
            P(None, row_axes, "gy"),
            P(row_axes, "gy"),
            P(row_axes, "gy"),
            P(),
        ),
        out_specs=(P(None, None, row_axes, "gy"), P(None, row_axes, "gy")),
        check_vma=False,
    )
```
